256 devices in a mesh: tm: 32 (over z, x), elem: 8 (over y, core).
Axes of the slice: x: 4, y: 4, z: 8, core: 2. Of those that a mesh axis runs over, the one named last changes fastest.
Arguments:
- modal_coords: bfloat16 [16384, 512], P('tm'), may hold values from -6 to 6
- stress_modes: bfloat16 [3, 512, 16384], P(None, None, 'elem'), may hold values from -0.375 to 0.375
- step_decay: float32 [16384, 512], P('tm'), may hold values from 0 to 1, as said below
- ply_layup: int32 [128], P('elem'), may hold values from 0 to 15
- lin_table: float32 [16, 2], replicated, may hold values from -0.03 to 0.03
- quad_table: float32 [16, 3], replicated, may hold values from 0.0005 to 0.004
- base_index: float32 [16], replicated, may hold values from 0.9 to 1.1
Outputs:
- column_ks: float32 [16384], P('elem')
- adjoint_states: float32 [16384, 512], P('tm')
The draws below stay inside these ranges and needn't reach their ends.
Inputs may be any that keep to these rules, and one draw needn't show every extreme that they name: `step_decay`: per-step factors of the modal adjoint states.
All inputs are finite; a program needn't handle non-finite values.
Results may differ from the reference program's by a relative error of at most 0.0027.
Values sent between devices are 32-bit elements; how exact they have to be, the bound alone decides.
A program may use at most 128 MiB of HBM per device.

```python
import math
import jax
import jax.numpy as jnp
from jax import lax

MODES = 512
COL_DEV = 2048
STEP_DEV = 512
COL_BLOCK = 128
LAYUPS = 16
INSTANT_COUNT = 16384
COLS = 16384
BLOCKS = 128
N_TM = 32
N_ELEM = 8


def draw_step_decay(key, part):
    generator_key_array = jax.random.split(key, 7)
    slow_cut = 5
    slow_modes = jax.random.randint(generator_key_array[0], (MODES,), 0, 10) < slow_cut
    slow_rate = jax.random.uniform(generator_key_array[1], (MODES,), jnp.float32, 0.2, 0.7) / INSTANT_COUNT
    fast_rate = jax.random.uniform(generator_key_array[2], (MODES,), jnp.float32, 1.0 / 50.0, 1.0 / 30.0)
    damping_rate = jnp.where(slow_modes, slow_rate, fast_rate)
    group_order = jax.random.permutation(generator_key_array[3], N_TM).astype(jnp.float32)
    group_factor = 0.7 * 2.0 ** (group_order / max(N_TM - 1, 1))
    horizon_length = jnp.arange(INSTANT_COUNT, dtype=jnp.int32)
    attenuation_multiplier = group_factor[horizon_length // STEP_DEV]
    stochastic_jitter = jax.random.uniform(generator_key_array[4], (INSTANT_COUNT, MODES), jnp.float32, 0.75, 1.5)
    gust_onset_index = jax.random.randint(generator_key_array[5], (2,), 0, INSTANT_COUNT)
    gust_surviving_mask = jax.random.uniform(generator_key_array[6], (2,), jnp.float32, 0.6, 0.8)
    gust_amplitudes = horizon_length[:, None] == gust_onset_index[None, :]
    gust_onset_flags = jnp.prod(jnp.where(gust_amplitudes, gust_surviving_mask[None, :], 1.0), axis=1)
    return jnp.exp(-damping_rate[None, :] * attenuation_multiplier[:, None] * stochastic_jitter) * gust_onset_flags[:, None]


def plant(values, rng, smallest, largest):
    spot = [jax.random.randint(jax.random.fold_in(rng, axis), (), 0, length) for axis, length in enumerate(values.shape)]
    main_axis = values.shape.index(max(values.shape))
    next_to = spot[:main_axis] + [(spot[main_axis] + 1) % values.shape[main_axis]] + spot[main_axis + 1:]
    return values.at[tuple(spot)].set(smallest).at[tuple(next_to)].set(largest)


def spiked(result, rng, source, target, blocks, factor):
    owner, partner = [(jnp.arange(result.shape[axis_at]) // (result.shape[axis_at] // blocks)).reshape([-1 if axis == axis_at else 1 for axis in range(result.ndim)]) for axis_at in (source, target)]
    chosen = jax.random.permutation(rng, blocks)[partner]
    strong = (owner == chosen) | (owner == (partner + blocks // 2) % blocks)
    return jnp.where(strong, factor * result, result)


def steps_of(key, shape, pieces, low, largest):
    level, own = 1.0, jax.random.fold_in(key, 6)
    for dim, blocks in pieces:
        steps = jnp.exp(jax.random.uniform(jax.random.fold_in(own, dim), (blocks,), jnp.float32, low / len(pieces), largest / len(pieces)))
        level = level * jnp.repeat(steps, shape[dim] // blocks).reshape([-1 if axis == dim else 1 for axis in range(len(shape))])
    return level


def noise(own_key, extent, spread, bound, cuts=(), kind=jnp.bfloat16):
    array = jax.random.normal(own_key, extent, jnp.float32) * spread
    if len(cuts) > 0:
        array = steps_of(own_key, extent, cuts, -0.22, 0.18) * array
    return jnp.clip(array, min=-bound, max=bound).astype(kind)


def heavy_noise(rng, dims, scale, bound, shards, heavy, kind=jnp.bfloat16):
    result = scale * jax.random.normal(rng, dims, jnp.float32)
    if shards:
        result = result * steps_of(rng, dims, shards, -0.22, 0.18)
    return jnp.clip(spiked(result, jax.random.fold_in(rng, 3), *heavy), -bound, bound).astype(kind)


def setup_inputs(seed: int = 0) -> dict:
    streams_of = jax.random.split(jax.random.key(seed), 8)
    return {
        "modal_coords": noise(streams_of[0], (INSTANT_COUNT, MODES), 1.0, 6.0, ((0, 32),)),
        "stress_modes": heavy_noise(streams_of[1], (3, MODES, COLS), MODES ** -0.5, 0.375, ((2, 8),), (2, 1, 8, 2.0)),
        "step_decay": draw_step_decay(jax.random.fold_in(streams_of[7], 71), 0),
        "ply_layup": plant(jax.random.randint(streams_of[3], (BLOCKS,), 0, LAYUPS), jax.random.fold_in(streams_of[3], 1), 0, LAYUPS - 1).astype(jnp.int32),
        "lin_table": jnp.clip(jax.random.uniform(streams_of[4], (LAYUPS, 2), jnp.float32, -0.03, 0.03), -0.03, 0.03),
        "quad_table": jnp.clip(jnp.exp(jax.random.uniform(streams_of[5], (LAYUPS, 3), jnp.float32, math.log(0.0005), math.log(0.004))), 0.0005, 0.004),
        "base_index": jnp.clip(jax.random.uniform(streams_of[6], (LAYUPS,), jnp.float32, 0.9, 1.1), 0.9, 1.1),
    }


sharpness = 100.0

def column_coefs(ply_layup, lin_table, quad_table, base_index):
    levels = jnp.arange(LAYUPS, dtype=jnp.int32)
    onehot = (ply_layup[:, None] == levels[None, :]).astype(jnp.float32)
    coef_table = jnp.concatenate([lin_table, quad_table, base_index[:, None]], axis=1)
    per_block = jnp.dot(onehot, coef_table, precision=lax.Precision.HIGHEST)
    return jnp.repeat(per_block, COL_BLOCK, axis=0).T

def failure_terms(stress, col_coefs):
    stress_one = stress[0]
    stress_two = stress[1]
    stress_shear = stress[2]
    lin_one = col_coefs[0][None, :]
    lin_two = col_coefs[1][None, :]
    quad_one = col_coefs[2][None, :]
    quad_two = col_coefs[3][None, :]
    quad_shear = col_coefs[4][None, :]
    static = col_coefs[5][None, :]
    cross_term = -0.5 * jnp.sqrt(quad_one * quad_two)
    failure_index = static + lin_one * stress_one + lin_two * stress_two + quad_one * stress_one * stress_one + quad_two * stress_two * stress_two + quad_shear * stress_shear * stress_shear + 2.0 * cross_term * stress_one * stress_two
    slopes = (lin_one + 2.0 * quad_one * stress_one + 2.0 * cross_term * stress_two, lin_two + 2.0 * quad_two * stress_two + 2.0 * cross_term * stress_one, 2.0 * quad_shear * stress_shear)
    return (failure_index, slopes)

def reference(modal_coords, stress_modes, step_decay, ply_layup, lin_table, quad_table, base_index):
    col_coefs = column_coefs(ply_layup, lin_table, quad_table, base_index)

    def one_block(load_rows, block_id):
        row_start = (block_id * COL_DEV).astype(jnp.int32)
        mode_part = lax.dynamic_slice_in_dim(stress_modes, row_start, COL_DEV, 2)
        coef_part = lax.dynamic_slice_in_dim(col_coefs, row_start, COL_DEV, 1)
        stress = jnp.stack([jnp.dot(modal_coords, mode_part[0], preferred_element_type=jnp.float32), jnp.dot(modal_coords, mode_part[1], preferred_element_type=jnp.float32), jnp.dot(modal_coords, mode_part[2], preferred_element_type=jnp.float32)])
        failure_index, slopes = failure_terms(stress, coef_part)
        peak_value = lax.optimization_barrier(jnp.max(failure_index, axis=0))
        scaled_exp = jnp.exp(sharpness * (failure_index - peak_value[None, :]))
        mass_total = lax.optimization_barrier(jnp.sum(scaled_exp, axis=0))
        weight = sharpness * scaled_exp / mass_total[None, :]
        sens_one = (weight * slopes[0]).astype(jnp.bfloat16)
        sens_two = (weight * slopes[1]).astype(jnp.bfloat16)
        sens_three = (weight * slopes[2]).astype(jnp.bfloat16)
        load_rows = load_rows + jnp.dot(sens_one, mode_part[0].T, preferred_element_type=jnp.float32)
        load_rows = load_rows + jnp.dot(sens_two, mode_part[1].T, preferred_element_type=jnp.float32)
        load_rows = load_rows + jnp.dot(sens_three, mode_part[2].T, preferred_element_type=jnp.float32)
        return (load_rows, peak_value + jnp.log(mass_total) / sharpness)
    load_rows, ks_blocks = lax.scan(one_block, jnp.zeros((INSTANT_COUNT, MODES), jnp.float32), jnp.arange(N_ELEM, dtype=jnp.int32))

    def step_back(state_now, inputs):
        decay_row, load_row = inputs
        lam_next = load_row + decay_row * state_now
        return (lam_next, lam_next)
    unused_state, adjoint = lax.scan(step_back, jnp.zeros((MODES,), jnp.float32), (step_decay, load_rows), reverse=True)
    return (ks_blocks.reshape(COLS), adjoint)
```

```python
import jax
import jax.numpy as jnp
from jax import lax
from jax.experimental import pallas as pl
from jax.experimental.pallas import tpu as pltpu
from jax.sharding import PartitionSpec as P

MESH = pl.DeviceIdType.MESH
F32 = jnp.float32
BF16 = jnp.bfloat16

NX, NZ, NY = 4, 8, 4
STEPS, MODES, COLS = 512, 512, 2048
LANES = 128
BLOCKS = COLS // LANES
TILE = 256
TILES = COLS // TILE
CHUNKS = 2
CHUNK_TILES = TILES // CHUNKS
CHUNK_COLS = COLS // CHUNKS
CHUNK_BLOCKS = BLOCKS // CHUNKS
SLAB = 64
SLABS = STEPS // SLAB
ROWS = 64
HALF = 32
SHARPNESS = 100.0

NT = (((1,), (1,)), ((), ()))


def kernel(
    modal_hbm, modes_hbm, decay_hbm, layup, lin, quad, base,
    ks_hbm, adjoint_hbm,
    modal, modes, decay, stress_a, stress_b, graded, slab_max, slab_sum, sens, loads,
    pair_in, partial, far_in, near_in, tail_prod, head_prod, offsets, result, ks,
    lse_x, lse_z, carry_x, carry_z, incoming,
    in_sem, out_sem, send_sem, recv_sem,
):
    tm = lax.axis_index("tm")
    elem = lax.axis_index("elem")
    z, x = tm // NX, tm % NX
    y, core = elem // 2, elem % 2
    x_peers = [(z * NX + (x + d) % NX, elem) for d in range(1, NX)]
    z_peers = [(((z + d) % NZ) * NX + x, elem) for d in range(1, NZ)]
    elem_peers = [(tm, (elem + d) % (2 * NY)) for d in range(1, 2 * NY)]
    y_up, y_down, y_far = (y + 1) % NY, (y + 3) % NY, (y + 2) % NY
    up, down, pair = (tm, 2 * y_up + core), (tm, 2 * y_down + core), (tm, 2 * y + 1 - core)

    sent = []
    counter = [0]

    def reserve(count):
        first = counter[0]
        counter[0] += count
        return first

    def send(src, dst, slot, peer):
        copy = pltpu.make_async_remote_copy(
            src_ref=src, dst_ref=dst, send_sem=send_sem.at[slot], recv_sem=recv_sem.at[slot],
            device_id=peer, device_id_type=MESH,
        )
        copy.start()
        sent.append(copy)

    def arrived(dst, slot):
        pltpu.make_async_remote_copy(
            src_ref=dst, dst_ref=dst, send_sem=send_sem.at[slot], recv_sem=recv_sem.at[slot],
            device_id=pair, device_id_type=MESH,
        ).wait_recv()

    modal_copy = pltpu.make_async_copy(modal_hbm, modal, in_sem.at[TILES])
    modal_copy.start()
    tile_copies = []
    for j in range(TILES):
        cols = pl.ds(j * TILE, TILE)
        copy = pltpu.make_async_copy(modes_hbm.at[:, :, cols], modes.at[:, :, cols], in_sem.at[j])
        copy.start()
        tile_copies.append(copy)
    decay_copy = pltpu.make_async_copy(decay_hbm, decay, in_sem.at[TILES + 1])
    decay_copy.start()
    barrier = pltpu.get_barrier_semaphore()
    peers = x_peers + z_peers + elem_peers
    for peer in peers:
        pl.semaphore_signal(barrier, inc=1, device_id=peer, device_id_type=MESH)

    def stress_tile(target, j):
        cols = pl.ds(pl.multiple_of(j * TILE, TILE), TILE)
        for k in range(3):
            target[k] = jnp.dot(modal[...], modes[k, :, cols], preferred_element_type=F32)

    def grade_tile(source, j):
        for h in range(TILE // LANES):
            block = j * (TILE // LANES) + h
            layer = layup[block]
            lin_one = SHARPNESS * lin[0, layer]
            lin_two = SHARPNESS * lin[1, layer]
            quad_one = SHARPNESS * quad[0, layer]
            quad_two = SHARPNESS * quad[1, layer]
            quad_shear = SHARPNESS * quad[2, layer]
            cross = -0.5 * jnp.sqrt(jnp.full((8, LANES), quad_one * quad_two, F32))[None]
            here = pl.ds(h * LANES, LANES)
            there = pl.ds(pl.multiple_of(block * LANES, LANES), LANES)
            for r in range(SLABS):
                rows = pl.ds(r * SLAB, SLAB)
                one, two, shear = (
                    source[k, rows, here].reshape(SLAB // 8, 8, LANES) for k in range(3)
                )
                half_one = quad_one * one + cross * two
                half_two = quad_two * two + cross * one
                half_shear = quad_shear * shear
                slope_one = lin_one + half_one
                slope_two = lin_two + half_two
                index = one * slope_one + two * slope_two + shear * half_shear
                top = jnp.max(index, axis=0)
                mass = jnp.exp(index - top[None])
                slab_max[block, r] = top
                slab_sum[block, r] = jnp.sum(mass, axis=0)
                graded[0, rows, there] = (mass * (slope_one + half_one)).reshape(SLAB, LANES)
                graded[1, rows, there] = (mass * (slope_two + half_two)).reshape(SLAB, LANES)
                graded[2, rows, there] = (mass * half_shear).reshape(SLAB, LANES)

    def stress_pair(p, carry):
        first = 2 * p
        pltpu.make_async_copy(
            modes_hbm.at[:, :, pl.ds(0, TILE)], modes.at[:, :, pl.ds(0, TILE)], in_sem.at[first + 1]
        ).wait()

        @pl.when(first + 2 < TILES)
        def _():
            pltpu.make_async_copy(
                modes_hbm.at[:, :, pl.ds(0, TILE)], modes.at[:, :, pl.ds(0, TILE)], in_sem.at[first + 2]
            ).wait()

        stress_tile(stress_b, first + 1)
        grade_tile(stress_a, first)
        stress_tile(stress_a, jnp.minimum(first + 2, TILES - 1))
        grade_tile(stress_b, first + 1)
        return carry

    lse_x_slot = reserve(CHUNKS * (NX - 1))
    lse_z_slot = reserve(CHUNKS * (NZ - 1))

    def log_sum(values):
        top = jnp.max(values, axis=0)
        return top + jnp.log(jnp.sum(jnp.exp(values - top[None]), axis=0))

    def share_x(c):
        blocks = pl.ds(c * CHUNK_BLOCKS, CHUNK_BLOCKS)
        tops = slab_max[blocks]
        top = jnp.max(tops, axis=(1, 2))
        total = jnp.sum(slab_sum[blocks] * jnp.exp(tops - top[:, None, None, :]), axis=(1, 2))
        lse_x[c, x] = top + jnp.log(total)
        for d, peer in enumerate(x_peers):
            send(lse_x.at[c, x], lse_x.at[c, x], lse_x_slot + c * (NX - 1) + d, peer)

    def share_z(c):
        for d in range(NX - 1):
            arrived(lse_x.at[c, (x + NX - 1 - d) % NX], lse_x_slot + c * (NX - 1) + d)
        lse_z[c, z] = log_sum(lse_x[c])
        for d, peer in enumerate(z_peers):
            send(lse_z.at[c, z], lse_z.at[c, z], lse_z_slot + c * (NZ - 1) + d, peer)

    def finish_lse(c):
        for d in range(NZ - 1):
            arrived(lse_z.at[c, (z + NZ - 1 - d) % NZ], lse_z_slot + c * (NZ - 1) + d)
        lse = log_sum(lse_z[c])
        for b in range(CHUNK_BLOCKS):
            block = c * CHUNK_BLOCKS + b
            ks[pl.ds(block, 1), :] = lse[b : b + 1] * (1.0 / SHARPNESS) + base[layup[block]]
        return lse

    def weigh(c, lse, first_slab, count):
        def slab_step(i, carry):
            r = first_slab + i
            rows = pl.ds(pl.multiple_of(r * SLAB, SLAB), SLAB)
            for b in range(CHUNK_BLOCKS):
                block = c * CHUNK_BLOCKS + b
                scale = jnp.exp(slab_max[block, r] - lse[b : b + 1])[None]
                there = pl.ds(block * LANES, LANES)
                here = pl.ds(b * LANES, LANES)
                for k in range(3):
                    factor = scale if k < 2 else 2.0 * scale
                    value = graded[k, rows, there].reshape(SLAB // 8, 8, LANES) * factor
                    sens[k, rows, here] = value.reshape(SLAB, LANES).astype(BF16)
            return carry

        lax.fori_loop(0, count, slab_step, 0, unroll=True)

    def load_rows(c, half):
        rows = pl.ds(pl.multiple_of(half * (STEPS // 2), STEPS // 2), STEPS // 2)
        total = None
        for k in range(3):
            part = lax.dot_general(
                sens[k, rows, :], modes[k, :, pl.ds(c * CHUNK_COLS, CHUNK_COLS)], NT,
                preferred_element_type=F32,
            )
            total = part if total is None else total + part
        if c == 0:
            loads[rows, :] = total
        else:
            loads[rows, :] += total

    modal_copy.wait()
    tile_copies[0].wait()
    stress_tile(stress_a, 0)
    for c in range(CHUNKS):
        lax.fori_loop(c * CHUNK_TILES // 2, (c + 1) * CHUNK_TILES // 2, stress_pair, 0)
        if c == 0:
            pl.semaphore_wait(barrier, len(peers))
        share_x(c)
    decay_copy.wait()

    ones = tuple(jnp.ones((1, MODES), F32) for _ in range(STEPS // ROWS))

    def tail_step(j, products):
        out = []
        for r in range(STEPS // ROWS):
            row = pl.ds(r * ROWS + ROWS - 1 - j, 1)
            value = products[r] * decay[row, :]
            tail_prod[row, :] = value
            out.append(value)
        return tuple(out)

    def head_step(j, products):
        out = []
        for r in range(STEPS // ROWS):
            row = pl.ds(r * ROWS + j, 1)
            head_prod[row, :] = products[r]
            out.append(products[r] * decay[row, :])
        return tuple(out)

    share_z(0)
    block_prod = lax.fori_loop(0, ROWS, tail_step, ones, unroll=4)
    for c in range(1, CHUNKS):
        share_z(c)
    lax.fori_loop(0, ROWS, head_step, ones, unroll=4)

    for c in range(CHUNKS - 1):
        lse = finish_lse(c)
        weigh(c, lse, 0, SLABS)
        load_rows(c, 0)
        load_rows(c, 1)
    last = CHUNKS - 1
    lse = finish_lse(last)
    ks_copy = pltpu.make_async_copy(ks, ks_hbm, out_sem.at[SLABS])
    ks_copy.start()

    order = (y_far, y_up, y_down, y)
    pair_slot = reserve(4)
    weigh(last, lse, (1 - core) * (SLABS // 2), SLABS // 2)
    load_rows(last, 1 - core)
    for i, q in enumerate(order):
        rows = pl.ds(pl.multiple_of((1 - core) * (STEPS // 2) + q * ROWS, ROWS), ROWS)
        send(loads.at[rows, :], pair_in.at[i], pair_slot + i, pair)
    weigh(last, lse, core * (SLABS // 2), SLABS // 2)
    load_rows(last, core)

    first_half, second_half = pl.ds(0, HALF), pl.ds(HALF, HALF)
    ring_slot = reserve(6)
    for i, q in enumerate(order):
        arrived(pair_in.at[i], pair_slot + i)
        rows = pl.ds(pl.multiple_of(core * (STEPS // 2) + q * ROWS, ROWS), ROWS)
        partial[i] = loads[rows, :] + pair_in[i]
        if i == 0:
            send(partial.at[0, first_half], far_in.at[0], ring_slot, up)
            send(partial.at[0, second_half], far_in.at[1], ring_slot + 1, down)
        if i == 1:
            send(partial.at[1, second_half], near_in.at[0, second_half], ring_slot + 2, up)
        if i == 2:
            send(partial.at[2, first_half], near_in.at[1, first_half], ring_slot + 3, down)

    carry_x_slot = reserve(NX - 1)
    carry_z_slot = reserve(NZ - 1)
    incoming_slot = reserve(2 * NY - 1)
    ahead = jnp.ones((1, MODES), F32)
    state = jnp.zeros((1, MODES), F32)
    for r in range(STEPS // ROWS):
        rows = pl.ds(r * ROWS, ROWS)
        state = state + ahead * jnp.sum(head_prod[rows, :] * loads[rows, :], axis=0, keepdims=True)
        ahead = ahead * block_prod[r]
    carry_x[x, 0:1, :] = ahead
    carry_x[x, 1:2, :] = state
    for d, peer in enumerate(x_peers):
        send(carry_x.at[x], carry_x.at[x], carry_x_slot + d, peer)

    arrived(far_in.at[0], ring_slot)
    partial[1, first_half] = partial[1, first_half] + far_in[0]
    send(partial.at[1, first_half], near_in.at[0, first_half], ring_slot + 4, up)
    arrived(far_in.at[1], ring_slot + 1)
    partial[2, second_half] = partial[2, second_half] + far_in[1]
    send(partial.at[2, second_half], near_in.at[1, second_half], ring_slot + 5, down)

    for d in range(NX - 1):
        arrived(carry_x.at[(x + NX - 1 - d) % NX], carry_x_slot + d)
    slab_scale = jnp.ones((1, MODES), F32)
    slab_state = jnp.zeros((1, MODES), F32)
    later_scale, later_state = slab_scale, slab_state
    for q in range(NX - 1, -1, -1):
        scale, offset = carry_x[q, 0:1, :], carry_x[q, 1:2, :]
        slab_state = offset + scale * slab_state
        slab_scale = scale * slab_scale
        later_state = jnp.where(q > x, offset + scale * later_state, later_state)
        later_scale = jnp.where(q > x, scale * later_scale, later_scale)
    carry_z[z, 0:1, :] = slab_scale
    carry_z[z, 1:2, :] = slab_state
    for d, peer in enumerate(z_peers):
        send(carry_z.at[z], carry_z.at[z], carry_z_slot + d, peer)

    arrived(near_in.at[0, second_half], ring_slot + 2)
    arrived(near_in.at[1, first_half], ring_slot + 3)
    arrived(near_in.at[0, first_half], ring_slot + 4)
    arrived(near_in.at[1, second_half], ring_slot + 5)
    partial[3] = partial[3] + near_in[0] + near_in[1]
    mine = core * NY + y

    def scan_step(j, running):
        row = ROWS - 1 - j
        running = partial[3, pl.ds(row, 1), :] + decay[pl.ds(mine * ROWS + row, 1), :] * running
        offsets[mine, pl.ds(row, 1), :] = running
        return running

    lax.fori_loop(0, ROWS, scan_step, jnp.zeros((1, MODES), F32), unroll=8)

    spread_slot = reserve(6)
    across_slot = reserve(5)

    def spread(block, rows, slot, peer):
        send(offsets.at[block, rows], offsets.at[block, rows], slot, peer)

    whole = pl.ds(0, ROWS)
    spread(mine, first_half, spread_slot, up)
    spread(mine, second_half, spread_slot + 3, down)
    spread(mine, second_half, spread_slot + 1, up)
    spread(mine, first_half, spread_slot + 2, down)
    spread(mine, whole, across_slot, pair)

    for d in range(NZ - 1):
        arrived(carry_z.at[(z + NZ - 1 - d) % NZ], carry_z_slot + d)
    far_state = jnp.zeros((1, MODES), F32)
    for q in range(NZ - 1, -1, -1):
        far_state = jnp.where(q > z, carry_z[q, 1:2, :] + carry_z[q, 0:1, :] * far_state, far_state)
    incoming[elem] = later_state + later_scale * far_state
    for d, peer in enumerate(elem_peers):
        send(incoming.at[elem], incoming.at[elem], incoming_slot + d, peer)

    from_down, from_up, from_far = core * NY + y_down, core * NY + y_up, core * NY + y_far
    arrived(offsets.at[from_down, first_half], spread_slot)
    spread(from_down, first_half, spread_slot + 4, up)
    arrived(offsets.at[from_up, second_half], spread_slot + 3)
    spread(from_up, second_half, spread_slot + 5, down)
    arrived(offsets.at[from_down, second_half], spread_slot + 1)
    spread(from_down, whole, across_slot + 1, pair)
    arrived(offsets.at[from_up, first_half], spread_slot + 2)
    spread(from_up, whole, across_slot + 2, pair)
    arrived(offsets.at[from_far, first_half], spread_slot + 4)
    spread(from_far, first_half, across_slot + 3, pair)
    arrived(offsets.at[from_far, second_half], spread_slot + 5)
    spread(from_far, second_half, across_slot + 4, pair)

    other = (1 - core) * NY
    for d in range(2 * NY - 1):
        arrived(incoming.at[(elem + 2 * NY - 1 - d) % (2 * NY)], incoming_slot + d)
    arrived(offsets.at[other + y], across_slot)
    arrived(offsets.at[other + y_down], across_slot + 1)
    arrived(offsets.at[other + y_up], across_slot + 2)
    arrived(offsets.at[other + y_far, first_half], across_slot + 3)
    arrived(offsets.at[other + y_far, second_half], across_slot + 4)

    behind = incoming[0]
    for e in range(1, 2 * NY):
        behind = behind + incoming[e]
    out_copies = []
    for r in range(SLABS - 1, -1, -1):
        rows = pl.ds(r * ROWS, ROWS)
        result[rows, :] = offsets[r] + tail_prod[rows, :] * behind
        copy = pltpu.make_async_copy(result.at[rows, :], adjoint_hbm.at[rows, :], out_sem.at[r])
        copy.start()
        out_copies.append(copy)
        behind = offsets[r, 0:1, :] + tail_prod[r * ROWS : r * ROWS + 1, :] * behind

    for copy in out_copies:
        copy.wait()
    ks_copy.wait()
    for copy in sent:
        copy.wait_send()


SENDS = CHUNKS * (NX - 1 + NZ - 1) + 4 + 6 + (NX - 1) + (NZ - 1) + (2 * NY - 1) + 6 + 5


def body(modal_coords, stress_modes, step_decay, ply_layup, lin_table, quad_table, base_index):
    smem = pl.BlockSpec(memory_space=pltpu.SMEM)
    hbm = pl.BlockSpec(memory_space=pl.ANY)
    ks, adjoint = pl.pallas_call(
        kernel,
        out_shape=(
            jax.ShapeDtypeStruct((BLOCKS, LANES), F32),
            jax.ShapeDtypeStruct((STEPS, MODES), F32),
        ),
        in_specs=[hbm, hbm, hbm, smem, smem, smem, smem],
        out_specs=(hbm, hbm),
        scratch_shapes=[
            pltpu.VMEM((STEPS, MODES), BF16),
            pltpu.VMEM((3, MODES, COLS), BF16),
            pltpu.VMEM((STEPS, MODES), F32),
            pltpu.VMEM((3, STEPS, TILE), F32),
            pltpu.VMEM((3, STEPS, TILE), F32),
            pltpu.VMEM((3, STEPS, COLS), F32),
            pltpu.VMEM((BLOCKS, SLABS, 8, LANES), F32),
            pltpu.VMEM((BLOCKS, SLABS, 8, LANES), F32),
            pltpu.VMEM((3, STEPS, CHUNK_COLS), BF16),
            pltpu.VMEM((STEPS, MODES), F32),
            pltpu.VMEM((4, ROWS, MODES), F32),
            pltpu.VMEM((4, ROWS, MODES), F32),
            pltpu.VMEM((2, HALF, MODES), F32),
            pltpu.VMEM((2, ROWS, MODES), F32),
            pltpu.VMEM((STEPS, MODES), F32),
            pltpu.VMEM((STEPS, MODES), F32),
            pltpu.VMEM((2 * NY, ROWS, MODES), F32),
            pltpu.VMEM((STEPS, MODES), F32),
            pltpu.VMEM((BLOCKS, LANES), F32),
            pltpu.VMEM((CHUNKS, NX, CHUNK_BLOCKS, LANES), F32),
            pltpu.VMEM((CHUNKS, NZ, CHUNK_BLOCKS, LANES), F32),
            pltpu.VMEM((NX, 2, MODES), F32),
            pltpu.VMEM((NZ, 2, MODES), F32),
            pltpu.VMEM((2 * NY, 1, MODES), F32),
            pltpu.SemaphoreType.DMA((TILES + 2,)),
            pltpu.SemaphoreType.DMA((SLABS + 1,)),
            pltpu.SemaphoreType.DMA((SENDS,)),
            pltpu.SemaphoreType.DMA((SENDS,)),
        ],
        compiler_params=pltpu.CompilerParams(
            collective_id=0, has_side_effects=True, vmem_limit_bytes=60 * 1024 * 1024
        ),
        name="gust_adjoint",
    )(
        modal_coords, stress_modes, step_decay, ply_layup,
        lin_table.T, quad_table.T, base_index,
    )
    return ks.reshape(COLS), adjoint


def solution(mesh):
    return jax.shard_map(
        body,
        mesh=mesh,
        in_specs=(P("tm", None), P(None, None, "elem"), P("tm", None), P("elem"), P(), P(), P()),
        out_specs=(P("elem"), P("tm", None)),
        check_vma=False,
    )
```

```python
import math

import jax
import jax.numpy as jnp
from jax import lax
from jax.experimental import pallas as pl
from jax.experimental.pallas import tpu as pltpu
from jax.sharding import PartitionSpec as P

MESH = pl.DeviceIdType.MESH
F32 = jnp.float32
BF16 = jnp.bfloat16

NX, NZ, NY = 4, 8, 4
STEPS, MODES, COLS = 512, 512, 2048
LANES = 128
GROUPS = MODES // LANES
BLOCKS = COLS // LANES
LAYUPS = 16
TILE = 256
TILES = COLS // TILE
CHUNKS = TILES // 2
CHUNK_COLS = COLS // CHUNKS
CHUNK_BLOCKS = BLOCKS // CHUNKS
SLAB = 64
SLABS = STEPS // SLAB
ROWS = 64
ROW_BLOCKS = STEPS // ROWS
HALF = 32
PIECES = 2
WIDTH = MODES // PIECES
SHARPNESS = 100.0
SCALE = SHARPNESS * math.log2(math.e)
SHIFT = -math.log2(math.log(2.0))

NT = (((1,), (1,)), ((), ()))

LSE_X = 0
LSE_Z = LSE_X + CHUNKS * (NX - 1)
PAIR = LSE_Z + CHUNKS * (NZ - 1)
RING = PAIR + 4 * PIECES
CARRY_X = RING + 6 * PIECES
CARRY_Z = CARRY_X + NX - 1
INCOMING = CARRY_Z + NZ - 1
SPREAD = INCOMING + 2 * NY - 1
ACROSS = SPREAD + 6 * PIECES
SENDS = ACROSS + 5 * PIECES

MODAL_IN = TILES
DECAY_IN = TILES + 1
TABLE_IN = DECAY_IN + GROUPS
INPUTS = TABLE_IN + 4


def kernel(
    modal_hbm, modes_hbm, decay_hbm, layup_hbm, lin_hbm, quad_hbm, base_hbm,
    ks, result,
    layup, lin, quad, base,
    modal, modes, decay, stress_a, stress_b, graded, slab_max, slab_sum, sens, loads,
    pair_in, partial, far_in, near_in, tail_prod, head_prod, offsets,
    lse_x, lse_z, carry_x, carry_z, incoming,
    in_sem, send_sem, recv_sem,
):
    tm = lax.axis_index("tm")
    elem = lax.axis_index("elem")
    z, x = tm // NX, tm % NX
    y, core = elem // 2, elem % 2
    x_peers = [(z * NX + (x + d) % NX, elem) for d in range(1, NX)]
    z_peers = [(((z + d) % NZ) * NX + x, elem) for d in range(1, NZ)]
    elem_peers = [(tm, (elem + d) % (2 * NY)) for d in range(1, 2 * NY)]
    y_up, y_down, y_far = (y + 1) % NY, (y + 3) % NY, (y + 2) % NY
    up, down, pair = (tm, 2 * y_up + core), (tm, 2 * y_down + core), (tm, 2 * y + 1 - core)

    sent = []

    def describe(src, dst, slot, peer):
        return pltpu.make_async_remote_copy(
            src_ref=src, dst_ref=dst, send_sem=send_sem.at[slot], recv_sem=recv_sem.at[slot],
            device_id=peer, device_id_type=MESH,
        )

    def send(src, dst, slot, peer):
        copy = describe(src, dst, slot, peer)
        copy.start()
        sent.append(copy)

    def arrived(dst, slot):
        describe(dst, dst, slot, pair).wait_recv()

    table_copies = [
        pltpu.make_async_copy(src, dst, in_sem.at[TABLE_IN + i])
        for i, (src, dst) in enumerate(
            ((layup_hbm, layup), (lin_hbm, lin), (quad_hbm, quad), (base_hbm, base))
        )
    ]

    def tile_copy(j):
        cols = pl.ds(j * TILE, TILE)
        return pltpu.make_async_copy(modes_hbm.at[:, :, cols], modes.at[:, :, cols], in_sem.at[j])

    modal_copy = pltpu.make_async_copy(modal_hbm, modal, in_sem.at[MODAL_IN])
    modal_copy.start()
    tile_copy(0).start()
    for copy in table_copies:
        copy.start()
    for j in range(1, TILES):
        tile_copy(j).start()
    decay_copies = []
    for g in range(GROUPS):
        copy = pltpu.make_async_copy(
            decay_hbm.at[:, pl.ds(g * LANES, LANES)], decay.at[g], in_sem.at[DECAY_IN + g]
        )
        copy.start()
        decay_copies.append(copy)
    barrier = pltpu.get_barrier_semaphore()
    peers = x_peers + z_peers + elem_peers
    for peer in peers:
        pl.semaphore_signal(barrier, inc=1, device_id=peer, device_id_type=MESH)

    def stress_tile(target, j):
        cols = pl.ds(pl.multiple_of(j * TILE, TILE), TILE)
        for k in range(3):
            target[k] = jnp.dot(modal[...], modes[k, :, cols], preferred_element_type=F32)

    def grade_tile(source, j):
        for h in range(TILE // LANES):
            block = j * (TILE // LANES) + h
            layer = layup[block]
            lin_one = SCALE * lin[0, layer]
            lin_two = SCALE * lin[1, layer]
            quad_one = SCALE * quad[0, layer]
            quad_two = SCALE * quad[1, layer]
            quad_shear = SCALE * quad[2, layer]
            cross = -0.5 * jnp.sqrt(jnp.full((8, LANES), quad_one * quad_two, F32))[None]
            here = pl.ds(h * LANES, LANES)
            there = pl.ds(pl.multiple_of(block * LANES, LANES), LANES)
            for r in range(SLABS):
                rows = pl.ds(r * SLAB, SLAB)
                one, two, shear = (
                    source[k, rows, here].reshape(SLAB // 8, 8, LANES) for k in range(3)
                )
                half_one = quad_one * one + cross * two
                half_two = quad_two * two + cross * one
                half_shear = quad_shear * shear
                slope_one = lin_one + half_one
                slope_two = lin_two + half_two
                index = one * slope_one + two * slope_two + shear * half_shear
                top = jnp.max(index, axis=0)
                mass = jnp.exp2(index - top[None])
                slab_max[block, r] = top
                slab_sum[block, r] = jnp.sum(mass, axis=0)
                graded[0, rows, there] = (mass * (slope_one + half_one)).reshape(SLAB, LANES)
                graded[1, rows, there] = (mass * (slope_two + half_two)).reshape(SLAB, LANES)
                graded[2, rows, there] = (mass * half_shear).reshape(SLAB, LANES)

    def log_two(values):
        return jnp.log(values) * math.log2(math.e)

    def log_sum(values):
        top = jnp.max(values, axis=0)
        return top + log_two(jnp.sum(jnp.exp2(values - top[None]), axis=0))

    def share_x(c):
        blocks = pl.ds(c * CHUNK_BLOCKS, CHUNK_BLOCKS)
        tops = slab_max[blocks]
        top = jnp.max(tops, axis=(1, 2))
        total = jnp.sum(slab_sum[blocks] * jnp.exp2(tops - top[:, None, None, :]), axis=(1, 2))
        lse_x[c, x] = top + log_two(total)
        for d, peer in enumerate(x_peers):
            describe(lse_x.at[c, x], lse_x.at[c, x], LSE_X + c * (NX - 1) + d, peer).start()

    def share_z(c):
        for d in range(NX - 1):
            arrived(lse_x.at[c, (x + NX - 1 - d) % NX], LSE_X + c * (NX - 1) + d)
        lse_z[c, z] = log_sum(lse_x[c])
        for d, peer in enumerate(z_peers):
            describe(lse_z.at[c, z], lse_z.at[c, z], LSE_Z + c * (NZ - 1) + d, peer).start()

    def finish_lse(c):
        for d in range(NZ - 1):
            arrived(lse_z.at[c, (z + NZ - 1 - d) % NZ], LSE_Z + c * (NZ - 1) + d)
        lse = log_sum(lse_z[c])
        for b in range(CHUNK_BLOCKS):
            block = c * CHUNK_BLOCKS + b
            ks[pl.ds(block, 1), :] = lse[b : b + 1] * (1.0 / SCALE) + base[layup[block]]
        return lse + SHIFT

    def weigh(c, lse, half):
        for i in range(SLABS // 2):
            r = half * (SLABS // 2) + i
            rows = pl.ds(pl.multiple_of(r * SLAB, SLAB), SLAB)
            for b in range(CHUNK_BLOCKS):
                block = c * CHUNK_BLOCKS + b
                scale = jnp.exp2(slab_max[block, r] - lse[b : b + 1])[None]
                there = pl.ds(block * LANES, LANES)
                here = pl.ds(b * LANES, LANES)
                for k in range(3):
                    factor = scale if k < 2 else 2.0 * scale
                    value = graded[k, rows, there].reshape(SLAB // 8, 8, LANES) * factor
                    sens[k, rows, here] = value.reshape(SLAB, LANES).astype(BF16)

    def load_rows(c, half, piece):
        rows = pl.ds(pl.multiple_of(half * (STEPS // 2), STEPS // 2), STEPS // 2)
        total = None
        for k in range(3):
            part = lax.dot_general(
                sens[k, rows, :],
                modes[k, pl.ds(piece * WIDTH, WIDTH), pl.ds(c * CHUNK_COLS, CHUNK_COLS)],
                NT, preferred_element_type=F32,
            )
            total = part if total is None else total + part
        if c == 0:
            loads[piece, rows, :] = total
        else:
            loads[piece, rows, :] += total

    modal_copy.wait()
    tile_copy(0).wait()
    stress_tile(stress_a, 0)
    for copy in table_copies:
        copy.wait()

    def stress_chunk(c, carry):
        first = 2 * c
        tile_copy(first + 1).wait()

        @pl.when(first + 2 < TILES)
        def _():
            tile_copy(first + 2).wait()

        stress_tile(stress_b, first + 1)
        grade_tile(stress_a, first)
        stress_tile(stress_a, jnp.minimum(first + 2, TILES - 1))
        grade_tile(stress_b, first + 1)

        @pl.when(c == 0)
        def _():
            pl.semaphore_wait(barrier, len(peers))

        share_x(c)

        @pl.when(c >= 2)
        def _():
            share_z(c - 2)

        return carry

    lax.fori_loop(0, CHUNKS, stress_chunk, 0)

    for copy in decay_copies:
        copy.wait()
    ones = tuple(jnp.ones((ROW_BLOCKS, LANES), F32) for _ in range(2 * GROUPS))

    def product_step(j, products):
        tails, heads = [], []
        for g in range(GROUPS):
            rows = pl.ds(ROWS - 1 - j, ROW_BLOCKS, stride=ROWS)
            value = products[g] * decay[g, rows, :]
            tail_prod[g, rows, :] = value
            tails.append(value)
            rows = pl.ds(j, ROW_BLOCKS, stride=ROWS)
            value = products[GROUPS + g]
            head_prod[g, rows, :] = value
            heads.append(value * decay[g, rows, :])
        return tuple(tails + heads)

    block_prod = lax.fori_loop(0, ROWS, product_step, ones, unroll=8)[:GROUPS]

    share_z(CHUNKS - 2)
    for c in range(CHUNKS - 1):
        lse = finish_lse(c)
        for half in range(2):
            weigh(c, lse, half)
            for piece in range(PIECES):
                load_rows(c, half, piece)
        if c == 0:
            share_z(CHUNKS - 1)
    last = CHUNKS - 1
    lse = finish_lse(last)

    order = (y_far, y_up, y_down, y)
    weigh(last, lse, 1 - core)
    for piece in range(PIECES):
        load_rows(last, 1 - core, piece)
        for i, q in enumerate(order):
            rows = pl.ds(pl.multiple_of((1 - core) * (STEPS // 2) + q * ROWS, ROWS), ROWS)
            send(loads.at[piece, rows, :], pair_in.at[piece, i], PAIR + 4 * piece + i, pair)
    weigh(last, lse, core)
    for piece in range(PIECES):
        load_rows(last, core, piece)

    first_half, second_half = pl.ds(0, HALF), pl.ds(HALF, HALF)
    for piece in range(PIECES):
        slot = RING + 6 * piece
        for i, q in enumerate(order):
            arrived(pair_in.at[piece, i], PAIR + 4 * piece + i)
            rows = pl.ds(pl.multiple_of(core * (STEPS // 2) + q * ROWS, ROWS), ROWS)
            partial[piece, i] = loads[piece, rows, :] + pair_in[piece, i]
            if i == 0:
                send(partial.at[piece, 0, first_half], far_in.at[piece, 0], slot, up)
                send(partial.at[piece, 0, second_half], far_in.at[piece, 1], slot + 1, down)
            if i == 1:
                send(
                    partial.at[piece, 1, second_half], near_in.at[piece, 0, second_half],
                    slot + 2, up,
                )
            if i == 2:
                send(
                    partial.at[piece, 2, first_half], near_in.at[piece, 1, first_half],
                    slot + 3, down,
                )

    for g in range(GROUPS):
        piece, lanes = g // 2, pl.ds((g % 2) * LANES, LANES)
        ahead = jnp.ones((1, LANES), F32)
        state = jnp.zeros((1, LANES), F32)
        for r in range(ROW_BLOCKS):
            rows = pl.ds(r * ROWS, ROWS)
            block_sum = jnp.sum(head_prod[g, rows, :] * loads[piece, rows, lanes], axis=0, keepdims=True)
            state = state + ahead * block_sum
            ahead = ahead * block_prod[g][r : r + 1]
        carry_x[x, 0:1, pl.ds(g * LANES, LANES)] = ahead
        carry_x[x, 1:2, pl.ds(g * LANES, LANES)] = state
    for d, peer in enumerate(x_peers):
        send(carry_x.at[x], carry_x.at[x], CARRY_X + d, peer)

    for piece in range(PIECES):
        slot = RING + 6 * piece
        arrived(far_in.at[piece, 0], slot)
        partial[piece, 1, first_half] = partial[piece, 1, first_half] + far_in[piece, 0]
        send(partial.at[piece, 1, first_half], near_in.at[piece, 0, first_half], slot + 4, up)
        arrived(far_in.at[piece, 1], slot + 1)
        partial[piece, 2, second_half] = partial[piece, 2, second_half] + far_in[piece, 1]
        send(partial.at[piece, 2, second_half], near_in.at[piece, 1, second_half], slot + 5, down)

    for d in range(NX - 1):
        arrived(carry_x.at[(x + NX - 1 - d) % NX], CARRY_X + d)
    slab_scale = jnp.ones((1, MODES), F32)
    slab_state = jnp.zeros((1, MODES), F32)
    later_scale, later_state = slab_scale, slab_state
    for q in range(NX - 1, -1, -1):
        scale, offset = carry_x[q, 0:1, :], carry_x[q, 1:2, :]
        slab_state = offset + scale * slab_state
        slab_scale = scale * slab_scale
        later_state = jnp.where(q > x, offset + scale * later_state, later_state)
        later_scale = jnp.where(q > x, scale * later_scale, later_scale)
    carry_z[z, 0:1, :] = slab_scale
    carry_z[z, 1:2, :] = slab_state
    for d, peer in enumerate(z_peers):
        send(carry_z.at[z], carry_z.at[z], CARRY_Z + d, peer)

    mine = core * NY + y

    def spread(piece, block, rows, slot, peer):
        send(offsets.at[piece, block, rows], offsets.at[piece, block, rows], slot, peer)

    whole = pl.ds(0, ROWS)
    for piece in range(PIECES):
        slot = RING + 6 * piece
        arrived(near_in.at[piece, 0, second_half], slot + 2)
        arrived(near_in.at[piece, 1, first_half], slot + 3)
        arrived(near_in.at[piece, 0, first_half], slot + 4)
        arrived(near_in.at[piece, 1, second_half], slot + 5)
        partial[piece, 3] = partial[piece, 3] + near_in[piece, 0] + near_in[piece, 1]
        running = [jnp.zeros((1, LANES), F32) for _ in range(2)]
        for row in range(ROWS - 1, -1, -1):
            for h in range(2):
                lanes = pl.ds(h * LANES, LANES)
                factor = decay[2 * piece + h, pl.ds(mine * ROWS + row, 1), :]
                running[h] = partial[piece, 3, row : row + 1, lanes] + factor * running[h]
                offsets[piece, mine, row : row + 1, lanes] = running[h]
        slot = SPREAD + 6 * piece
        spread(piece, mine, first_half, slot, up)
        spread(piece, mine, second_half, slot + 3, down)
        spread(piece, mine, second_half, slot + 1, up)
        spread(piece, mine, first_half, slot + 2, down)
        spread(piece, mine, whole, ACROSS + 5 * piece, pair)

    for d in range(NZ - 1):
        arrived(carry_z.at[(z + NZ - 1 - d) % NZ], CARRY_Z + d)
    far_state = jnp.zeros((1, MODES), F32)
    for q in range(NZ - 1, -1, -1):
        far_state = jnp.where(q > z, carry_z[q, 1:2, :] + carry_z[q, 0:1, :] * far_state, far_state)
    incoming[elem] = later_state + later_scale * far_state
    for d, peer in enumerate(elem_peers):
        send(incoming.at[elem], incoming.at[elem], INCOMING + d, peer)

    from_down, from_up, from_far = core * NY + y_down, core * NY + y_up, core * NY + y_far
    for piece in range(PIECES):
        slot, across = SPREAD + 6 * piece, ACROSS + 5 * piece
        arrived(offsets.at[piece, from_down, first_half], slot)
        spread(piece, from_down, first_half, slot + 4, up)
        arrived(offsets.at[piece, from_up, second_half], slot + 3)
        spread(piece, from_up, second_half, slot + 5, down)
        arrived(offsets.at[piece, from_down, second_half], slot + 1)
        spread(piece, from_down, whole, across + 1, pair)
        arrived(offsets.at[piece, from_up, first_half], slot + 2)
        spread(piece, from_up, whole, across + 2, pair)
    for piece in range(PIECES):
        slot, across = SPREAD + 6 * piece, ACROSS + 5 * piece
        arrived(offsets.at[piece, from_far, first_half], slot + 4)
        spread(piece, from_far, first_half, across + 3, pair)
        arrived(offsets.at[piece, from_far, second_half], slot + 5)
        spread(piece, from_far, second_half, across + 4, pair)

    for d in range(2 * NY - 1):
        arrived(incoming.at[(elem + 2 * NY - 1 - d) % (2 * NY)], INCOMING + d)
    behind = incoming[0]
    for e in range(1, 2 * NY):
        behind = behind + incoming[e]

    other = (1 - core) * NY
    for piece in range(PIECES):
        across = ACROSS + 5 * piece
        arrived(offsets.at[piece, other + y], across)
        arrived(offsets.at[piece, other + y_down], across + 1)
        arrived(offsets.at[piece, other + y_up], across + 2)
        arrived(offsets.at[piece, other + y_far, first_half], across + 3)
        arrived(offsets.at[piece, other + y_far, second_half], across + 4)
        for h in range(2):
            g = 2 * piece + h
            here, there = pl.ds(h * LANES, LANES), pl.ds(g * LANES, LANES)
            state = behind[:, g * LANES : (g + 1) * LANES]
            for r in range(ROW_BLOCKS - 1, -1, -1):
                rows = pl.ds(r * ROWS, ROWS)
                result[rows, there] = offsets[piece, r, :, here] + tail_prod[g, rows, :] * state
                state = offsets[piece, r, 0:1, here] + tail_prod[g, r * ROWS : r * ROWS + 1, :] * state

    for copy in sent:
        copy.wait_send()
    for c in range(CHUNKS):
        for d, peer in enumerate(x_peers):
            describe(lse_x.at[c, x], lse_x.at[c, x], LSE_X + c * (NX - 1) + d, peer).wait_send()
        for d, peer in enumerate(z_peers):
            describe(lse_z.at[c, z], lse_z.at[c, z], LSE_Z + c * (NZ - 1) + d, peer).wait_send()


def write_out(ks, result, ks_hbm, adjoint_hbm, sem):
    copies = [
        pltpu.make_async_copy(result, adjoint_hbm, sem.at[0]),
        pltpu.make_async_copy(ks, ks_hbm, sem.at[1]),
    ]
    for copy in copies:
        copy.start()
    for copy in copies:
        copy.wait()


def body(modal_coords, stress_modes, step_decay, ply_layup, lin_table, quad_table, base_index):
    hbm = pl.BlockSpec(memory_space=pl.ANY)
    vmem = pl.BlockSpec(memory_space=pltpu.VMEM)
    ks, adjoint = pl.pallas_call(
        kernel,
        out_shape=(
            pltpu.VMEM((BLOCKS, LANES), F32),
            pltpu.VMEM((STEPS, MODES), F32),
        ),
        in_specs=[hbm] * 7,
        out_specs=(vmem, vmem),
        scratch_shapes=[
            pltpu.SMEM((BLOCKS,), jnp.int32),
            pltpu.SMEM((2, LAYUPS), F32),
            pltpu.SMEM((3, LAYUPS), F32),
            pltpu.SMEM((LAYUPS,), F32),
            pltpu.VMEM((STEPS, MODES), BF16),
            pltpu.VMEM((3, MODES, COLS), BF16),
            pltpu.VMEM((GROUPS, STEPS, LANES), F32),
            pltpu.VMEM((3, STEPS, TILE), F32),
            pltpu.VMEM((3, STEPS, TILE), F32),
            pltpu.VMEM((3, STEPS, COLS), F32),
            pltpu.VMEM((BLOCKS, SLABS, 8, LANES), F32),
            pltpu.VMEM((BLOCKS, SLABS, 8, LANES), F32),
            pltpu.VMEM((3, STEPS, CHUNK_COLS), BF16),
            pltpu.VMEM((PIECES, STEPS, WIDTH), F32),
            pltpu.VMEM((PIECES, 4, ROWS, WIDTH), F32),
            pltpu.VMEM((PIECES, 4, ROWS, WIDTH), F32),
            pltpu.VMEM((PIECES, 2, HALF, WIDTH), F32),
            pltpu.VMEM((PIECES, 2, ROWS, WIDTH), F32),
            pltpu.VMEM((GROUPS, STEPS, LANES), F32),
            pltpu.VMEM((GROUPS, STEPS, LANES), F32),
            pltpu.VMEM((PIECES, ROW_BLOCKS, ROWS, WIDTH), F32),
            pltpu.VMEM((CHUNKS, NX, CHUNK_BLOCKS, LANES), F32),
            pltpu.VMEM((CHUNKS, NZ, CHUNK_BLOCKS, LANES), F32),
            pltpu.VMEM((NX, 2, MODES), F32),
            pltpu.VMEM((NZ, 2, MODES), F32),
            pltpu.VMEM((2 * NY, 1, MODES), F32),
            pltpu.SemaphoreType.DMA((INPUTS,)),
            pltpu.SemaphoreType.DMA((SENDS,)),
            pltpu.SemaphoreType.DMA((SENDS,)),
        ],
        compiler_params=pltpu.CompilerParams(
            collective_id=0, has_side_effects=True, vmem_limit_bytes=48 * 1024 * 1024
        ),
        name="gust_adjoint",
    )(*(
        pltpu.with_memory_space_constraint(value, pltpu.HBM)
        for value in (
            modal_coords, stress_modes, step_decay, ply_layup,
            lin_table.T, quad_table.T, base_index,
        )
    ))
    ks, adjoint = pl.pallas_call(
        write_out,
        out_shape=(
            jax.ShapeDtypeStruct((BLOCKS, LANES), F32),
            jax.ShapeDtypeStruct((STEPS, MODES), F32),
        ),
        in_specs=[vmem] * 2,
        out_specs=(hbm, hbm),
        scratch_shapes=[pltpu.SemaphoreType.DMA((2,))],
        name="write_out",
    )(
        pltpu.with_memory_space_constraint(ks, pltpu.VMEM),
        pltpu.with_memory_space_constraint(adjoint, pltpu.VMEM),
    )
    return ks.reshape(COLS), adjoint


def solution(mesh):
    return jax.shard_map(
        body,
        mesh=mesh,
        in_specs=(P("tm", None), P(None, None, "elem"), P("tm", None), P("elem"), P(), P(), P()),
        out_specs=(P("elem"), P("tm", None)),
        check_vma=False,
    )
```

```python
import math

import jax
import jax.numpy as jnp
from jax import lax
from jax.experimental import pallas as pl
from jax.experimental.pallas import tpu as pltpu
from jax.sharding import PartitionSpec as P

MESH = pl.DeviceIdType.MESH
F32 = jnp.float32
BF16 = jnp.bfloat16

NX, NZ, NY = 4, 8, 4
STEPS, MODES, COLS = 512, 512, 2048
LANES = 128
GROUPS = MODES // LANES
BLOCKS = COLS // LANES
LAYUPS = 16
TILE = 256
TILES = COLS // TILE
CHUNKS = TILES // 2
CHUNK_COLS = COLS // CHUNKS
CHUNK_BLOCKS = BLOCKS // CHUNKS
SLAB = 64
SLABS = STEPS // SLAB
ROWS = 64
ROW_BLOCKS = STEPS // ROWS
WIDTH = 256
PER_DOT = WIDTH // LANES
SHARPNESS = 100.0
SCALE = SHARPNESS * math.log2(math.e)
HALF_SCALE = 0.5 * SCALE
SHIFT = -math.log2(2.0 * math.log(2.0))

NT = (((1,), (1,)), ((), ()))

LSE_X = 0
LSE_Z = LSE_X + CHUNKS * (NX - 1)
PAIR = LSE_Z + CHUNKS * (NZ - 1)
RING = PAIR + GROUPS
CARRY_X = RING + (NY - 1) * GROUPS
CARRY_Z = CARRY_X + NX - 1
INCOMING = CARRY_Z + NZ - 1
SPREAD = INCOMING + 2 * NY - 1
ACROSS = SPREAD + (NY - 1) * GROUPS
SENDS = ACROSS + NY * GROUPS

MODAL_IN = TILES
DECAY_IN = TILES + 1
TABLE_IN = DECAY_IN + GROUPS
INPUTS = TABLE_IN + 4


def kernel(
    modal_hbm, modes_hbm, decay_hbm, layup_hbm, lin_hbm, quad_hbm, base_hbm,
    ks, result,
    layup, lin, quad, base,
    modal, modes, decay, stress_a, stress_b, graded, index, slab_max, block_max, block_sum, sens, loads,
    pair_in, partial, near_in, tail_prod, head_prod, offsets,
    lse_x, lse_z, carry_x, carry_z, incoming,
    in_sem, send_sem, recv_sem,
):
    tm = lax.axis_index("tm")
    elem = lax.axis_index("elem")
    z, x = tm // NX, tm % NX
    y, core = elem // 2, elem % 2
    x_peers = [(z * NX + (x + d) % NX, elem) for d in range(1, NX)]
    z_peers = [(((z + d) % NZ) * NX + x, elem) for d in range(1, NZ)]
    elem_peers = [(tm, (elem + d) % (2 * NY)) for d in range(1, 2 * NY)]
    y_up, y_down, y_far = (y + 1) % NY, (y + 3) % NY, (y + 2) % NY
    pair = (tm, 2 * y + 1 - core)
    ring = [(tm, 2 * q + core) for q in (y_far, y_up, y_down)]
    ring_y = (y_far, y_down, y_up)

    sent = []

    def describe(src, dst, slot, peer):
        return pltpu.make_async_remote_copy(
            src_ref=src, dst_ref=dst, send_sem=send_sem.at[slot], recv_sem=recv_sem.at[slot],
            device_id=peer, device_id_type=MESH,
        )

    def send(src, dst, slot, peer):
        copy = describe(src, dst, slot, peer)
        copy.start()
        sent.append(copy)

    def arrived(dst, slot):
        describe(dst, dst, slot, pair).wait_recv()

    table_copies = [
        pltpu.make_async_copy(src, dst, in_sem.at[TABLE_IN + i])
        for i, (src, dst) in enumerate(
            ((layup_hbm, layup), (lin_hbm, lin), (quad_hbm, quad), (base_hbm, base))
        )
    ]

    def tile_copy(j):
        cols = pl.ds(j * TILE, TILE)
        return pltpu.make_async_copy(modes_hbm.at[:, :, cols], modes.at[:, :, cols], in_sem.at[j])

    modal_copy = pltpu.make_async_copy(modal_hbm, modal, in_sem.at[MODAL_IN])
    modal_copy.start()
    tile_copy(0).start()
    for copy in table_copies:
        copy.start()
    for j in range(1, TILES):
        tile_copy(j).start()
    decay_copies = []
    for g in range(GROUPS):
        copy = pltpu.make_async_copy(
            decay_hbm.at[:, pl.ds(g * LANES, LANES)], decay.at[g], in_sem.at[DECAY_IN + g]
        )
        copy.start()
        decay_copies.append(copy)
    barrier = pltpu.get_barrier_semaphore()
    peers = x_peers + z_peers + elem_peers
    for peer in peers:
        pl.semaphore_signal(barrier, inc=1, device_id=peer, device_id_type=MESH)

    def stress_tile(target, j):
        cols = pl.ds(pl.multiple_of(j * TILE, TILE), TILE)
        for k in range(3):
            target[k] = jnp.dot(modal[...], modes[k, :, cols], preferred_element_type=F32)

    def grade_tile(source, j):
        for h in range(TILE // LANES):
            block = j * (TILE // LANES) + h
            layer = layup[block]
            lin_one = HALF_SCALE * lin[0, layer]
            lin_two = HALF_SCALE * lin[1, layer]
            quad_one = SCALE * quad[0, layer]
            quad_two = SCALE * quad[1, layer]
            quad_shear = SCALE * quad[2, layer]
            cross = -0.5 * jnp.sqrt(jnp.full((8, LANES), quad_one * quad_two, F32))[None]
            here = pl.ds(h * LANES, LANES)
            there = pl.ds(pl.multiple_of(block * LANES, LANES), LANES)
            for r in range(SLABS):
                rows = pl.ds(r * SLAB, SLAB)
                one, two, shear = (
                    source[k, rows, here].reshape(SLAB // 8, 8, LANES) for k in range(3)
                )
                slope_one = lin_one + (quad_one * one + cross * two)
                slope_two = lin_two + (quad_two * two + cross * one)
                slope_shear = quad_shear * shear
                value = (
                    one * (lin_one + slope_one) + two * (lin_two + slope_two) + shear * slope_shear
                )
                graded[0, rows, there] = slope_one.reshape(SLAB, LANES)
                graded[1, rows, there] = slope_two.reshape(SLAB, LANES)
                graded[2, rows, there] = slope_shear.reshape(SLAB, LANES)
                index[rows, there] = value.reshape(SLAB, LANES)
                slab_max[block, r] = jnp.max(value, axis=0)

    def sum_tile(j):
        for h in range(TILE // LANES):
            block = j * (TILE // LANES) + h
            there = pl.ds(pl.multiple_of(block * LANES, LANES), LANES)
            top = jnp.max(slab_max[block], axis=0)
            parts = []
            for r in range(SLABS):
                value = index[pl.ds(r * SLAB, SLAB), there].reshape(SLAB // 8, 8, LANES)
                parts.append(jnp.sum(jnp.exp2(value - top[None]), axis=0))
            while len(parts) > 1:
                parts = [a + b for a, b in zip(parts[::2], parts[1::2])]
            block_max[block] = top
            block_sum[block] = parts[0]

    def log_two(values):
        return jnp.log(values) * math.log2(math.e)

    def log_sum(values):
        top = jnp.max(values, axis=0)
        return top + log_two(jnp.sum(jnp.exp2(values - top[None]), axis=0))

    def share_x(c):
        blocks = pl.ds(c * CHUNK_BLOCKS, CHUNK_BLOCKS)
        tops = block_max[blocks]
        top = jnp.max(tops, axis=1)
        total = jnp.sum(block_sum[blocks] * jnp.exp2(tops - top[:, None, :]), axis=1)
        lse_x[c, x] = top + log_two(total)
        for d, peer in enumerate(x_peers):
            describe(lse_x.at[c, x], lse_x.at[c, x], LSE_X + c * (NX - 1) + d, peer).start()

    def share_z(c):
        for d in range(NX - 1):
            arrived(lse_x.at[c, (x + NX - 1 - d) % NX], LSE_X + c * (NX - 1) + d)
        lse_z[c, z] = log_sum(lse_x[c])
        for d, peer in enumerate(z_peers):
            describe(lse_z.at[c, z], lse_z.at[c, z], LSE_Z + c * (NZ - 1) + d, peer).start()

    def finish_lse(c):
        for d in range(NZ - 1):
            arrived(lse_z.at[c, (z + NZ - 1 - d) % NZ], LSE_Z + c * (NZ - 1) + d)
        lse = log_sum(lse_z[c])
        for b in range(CHUNK_BLOCKS):
            block = c * CHUNK_BLOCKS + b
            ks[pl.ds(block, 1), :] = lse[b : b + 1] * (1.0 / SCALE) + base[layup[block]]
        return lse + SHIFT

    def weigh(c, lse, half):
        for i in range(SLABS // 2):
            r = half * (SLABS // 2) + i
            rows = pl.ds(pl.multiple_of(r * SLAB, SLAB), SLAB)
            for b in range(CHUNK_BLOCKS):
                there = pl.ds((c * CHUNK_BLOCKS + b) * LANES, LANES)
                here = pl.ds(b * LANES, LANES)
                weight = jnp.exp2(index[rows, there] - lse[b : b + 1])
                for k in range(3):
                    sens[k, rows, here] = (weight * graded[k, rows, there]).astype(BF16)

    def load_rows(c, half, piece):
        rows = pl.ds(pl.multiple_of(half * (STEPS // 2), STEPS // 2), STEPS // 2)
        total = None
        for k in range(3):
            part = lax.dot_general(
                sens[k, rows, :],
                modes[k, pl.ds(piece * WIDTH, WIDTH), pl.ds(c * CHUNK_COLS, CHUNK_COLS)],
                NT, preferred_element_type=F32,
            )
            total = part if total is None else total + part
        for h in range(PER_DOT):
            g = piece * PER_DOT + h
            part = total[:, h * LANES : (h + 1) * LANES]
            loads[g, rows, :] = part if c == 0 else loads[g, rows, :] + part

    modal_copy.wait()
    tile_copy(0).wait()
    stress_tile(stress_a, 0)
    for copy in table_copies:
        copy.wait()

    def stress_chunk(c, carry):
        first = 2 * c
        tile_copy(first + 1).wait()
        stress_tile(stress_b, first + 1)
        grade_tile(stress_a, first)

        @pl.when(first + 2 < TILES)
        def _():
            tile_copy(first + 2).wait()

        stress_tile(stress_a, jnp.minimum(first + 2, TILES - 1))
        grade_tile(stress_b, first + 1)
        sum_tile(first)

        @pl.when(c == 0)
        def _():
            pl.semaphore_wait(barrier, len(peers))

        sum_tile(first + 1)
        share_x(c)

        @pl.when(c >= 2)
        def _():
            share_z(c - 2)

        return carry

    lax.fori_loop(0, CHUNKS, stress_chunk, 0)

    for copy in decay_copies:
        copy.wait()
    tiles = ROWS // 8
    level = lax.broadcasted_iota(jnp.int32, (tiles, 8, LANES), 1)

    def product_step(i, carry):
        g, r = i // ROW_BLOCKS, i % ROW_BLOCKS
        rows = pl.ds(pl.multiple_of(r * ROWS, ROWS), ROWS)
        tail = decay[g, rows, :].reshape(tiles, 8, LANES)
        head = tail
        for step in (1, 2, 4):
            tail = tail * jnp.where(level < 8 - step, pltpu.roll(tail, 8 - step, 1), 1.0)
            head = head * jnp.where(level >= step, pltpu.roll(head, step, 1), 1.0)
        before = jnp.where(level >= 1, pltpu.roll(head, 1, 1), 1.0)
        after = jnp.ones((1, LANES), F32)
        ahead = jnp.ones((1, LANES), F32)
        for n in range(tiles):
            m = tiles - 1 - n
            tail_prod[g, pl.ds(pl.multiple_of(r * ROWS + m * 8, 8), 8), :] = tail[m] * after
            after = after * tail[m, 0:1]
            head_prod[g, pl.ds(pl.multiple_of(r * ROWS + n * 8, 8), 8), :] = before[n] * ahead
            ahead = ahead * head[n, 7:8]
        return carry

    lax.fori_loop(0, GROUPS * ROW_BLOCKS, product_step, 0, unroll=4)

    share_z(CHUNKS - 2)
    for c in range(CHUNKS - 1):
        lse = finish_lse(c)
        for half in range(2):
            weigh(c, lse, half)
            for piece in range(MODES // WIDTH):
                load_rows(c, half, piece)
        if c == 0:
            share_z(CHUNKS - 1)
    last = CHUNKS - 1
    lse = finish_lse(last)

    pair_rows = pl.ds(pl.multiple_of((1 - core) * (STEPS // 2), STEPS // 2), STEPS // 2)
    weigh(last, lse, 1 - core)
    for piece in range(MODES // WIDTH):
        load_rows(last, 1 - core, piece)
        for g in range(piece * PER_DOT, (piece + 1) * PER_DOT):
            send(loads.at[g, pair_rows, :], pair_in.at[g], PAIR + g, pair)
    weigh(last, lse, core)
    for piece in range(MODES // WIDTH):
        load_rows(last, core, piece)

    def pair_sum(g, q):
        here = pl.ds(pl.multiple_of(q * ROWS, ROWS), ROWS)
        there = pl.ds(pl.multiple_of(core * (STEPS // 2) + q * ROWS, ROWS), ROWS)
        return loads[g, there, :] + pair_in[g, here, :]

    for g in range(GROUPS):
        arrived(pair_in.at[g], PAIR + g)
        for i, q in enumerate((y_far, y_up, y_down)):
            partial[g, i] = pair_sum(g, q)
            send(partial.at[g, i], near_in.at[g, i], RING + (NY - 1) * g + i, ring[i])

    for g in range(GROUPS):
        ahead = jnp.ones((1, LANES), F32)
        state = jnp.zeros((1, LANES), F32)
        for r in range(ROW_BLOCKS):
            rows = pl.ds(r * ROWS, ROWS)
            block_sum = jnp.sum(head_prod[g, rows, :] * loads[g, rows, :], axis=0, keepdims=True)
            state = state + ahead * block_sum
            ahead = ahead * tail_prod[g, r * ROWS : r * ROWS + 1, :]
        carry_x[x, 0:1, pl.ds(g * LANES, LANES)] = ahead
        carry_x[x, 1:2, pl.ds(g * LANES, LANES)] = state
    for d, peer in enumerate(x_peers):
        send(carry_x.at[x], carry_x.at[x], CARRY_X + d, peer)

    for d in range(NX - 1):
        arrived(carry_x.at[(x + NX - 1 - d) % NX], CARRY_X + d)
    slab_scale = jnp.ones((1, MODES), F32)
    slab_state = jnp.zeros((1, MODES), F32)
    later_scale, later_state = slab_scale, slab_state
    for q in range(NX - 1, -1, -1):
        scale, offset = carry_x[q, 0:1, :], carry_x[q, 1:2, :]
        slab_state = offset + scale * slab_state
        slab_scale = scale * slab_scale
        later_state = jnp.where(q > x, offset + scale * later_state, later_state)
        later_scale = jnp.where(q > x, scale * later_scale, later_scale)
    carry_z[z, 0:1, :] = slab_scale
    carry_z[z, 1:2, :] = slab_state
    for d, peer in enumerate(z_peers):
        send(carry_z.at[z], carry_z.at[z], CARRY_Z + d, peer)

    mine = core * NY + y

    def spread(g, block, slot, peer):
        send(offsets.at[g, block], offsets.at[g, block], slot, peer)

    mine_rows = pl.ds(pl.multiple_of(mine * ROWS, ROWS), ROWS)
    for g in range(GROUPS):
        for i in range(NY - 1):
            arrived(near_in.at[g, i], RING + (NY - 1) * g + i)
        state = (pair_sum(g, y) + near_in[g, 1]) + (near_in[g, 2] + near_in[g, 0])
        state = state.reshape(tiles, 8, LANES)
        factor = decay[g, mine_rows, :].reshape(tiles, 8, LANES)
        for step in (1, 2, 4):
            inside = level < 8 - step
            state = state + factor * jnp.where(inside, pltpu.roll(state, 8 - step, 1), 0.0)
            factor = factor * jnp.where(inside, pltpu.roll(factor, 8 - step, 1), 1.0)
        running = jnp.zeros((1, LANES), F32)
        for m in range(tiles - 1, -1, -1):
            value = state[m] + factor[m] * running
            offsets[g, mine, pl.ds(m * 8, 8), :] = value
            running = value[0:1]
        for i in range(NY - 1):
            spread(g, mine, SPREAD + (NY - 1) * g + i, ring[i])
        spread(g, mine, ACROSS + NY * g, pair)

    for d in range(NZ - 1):
        arrived(carry_z.at[(z + NZ - 1 - d) % NZ], CARRY_Z + d)
    far_state = jnp.zeros((1, MODES), F32)
    for q in range(NZ - 1, -1, -1):
        far_state = jnp.where(q > z, carry_z[q, 1:2, :] + carry_z[q, 0:1, :] * far_state, far_state)
    incoming[elem] = later_state + later_scale * far_state
    for d, peer in enumerate(elem_peers):
        send(incoming.at[elem], incoming.at[elem], INCOMING + d, peer)

    for g in range(GROUPS):
        for i, q in enumerate(ring_y):
            arrived(offsets.at[g, core * NY + q], SPREAD + (NY - 1) * g + i)
            spread(g, core * NY + q, ACROSS + NY * g + 1 + i, pair)

    for d in range(2 * NY - 1):
        arrived(incoming.at[(elem + 2 * NY - 1 - d) % (2 * NY)], INCOMING + d)
    behind = incoming[0]
    for e in range(1, 2 * NY):
        behind = behind + incoming[e]

    other = (1 - core) * NY
    for g in range(GROUPS):
        for i, q in enumerate((y,) + ring_y):
            arrived(offsets.at[g, other + q], ACROSS + NY * g + i)
        there = pl.ds(g * LANES, LANES)
        state = behind[:, g * LANES : (g + 1) * LANES]
        for r in range(ROW_BLOCKS - 1, -1, -1):
            rows = pl.ds(r * ROWS, ROWS)
            result[rows, there] = offsets[g, r] + tail_prod[g, rows, :] * state
            state = offsets[g, r, 0:1, :] + tail_prod[g, r * ROWS : r * ROWS + 1, :] * state

    for copy in sent:
        copy.wait_send()
    for c in range(CHUNKS):
        for d, peer in enumerate(x_peers):
            describe(lse_x.at[c, x], lse_x.at[c, x], LSE_X + c * (NX - 1) + d, peer).wait_send()
        for d, peer in enumerate(z_peers):
            describe(lse_z.at[c, z], lse_z.at[c, z], LSE_Z + c * (NZ - 1) + d, peer).wait_send()


def write_out(ks, result, ks_hbm, adjoint_hbm, sem):
    copies = [
        pltpu.make_async_copy(result, adjoint_hbm, sem.at[0]),
        pltpu.make_async_copy(ks, ks_hbm, sem.at[1]),
    ]
    for copy in copies:
        copy.start()
    for copy in copies:
        copy.wait()


def body(modal_coords, stress_modes, step_decay, ply_layup, lin_table, quad_table, base_index):
    hbm = pl.BlockSpec(memory_space=pl.ANY)
    vmem = pl.BlockSpec(memory_space=pltpu.VMEM)
    ks, adjoint = pl.pallas_call(
        kernel,
        out_shape=(
            pltpu.VMEM((BLOCKS, LANES), F32),
            pltpu.VMEM((STEPS, MODES), F32),
        ),
        in_specs=[hbm] * 7,
        out_specs=(vmem, vmem),
        scratch_shapes=[
            pltpu.SMEM((BLOCKS,), jnp.int32),
            pltpu.SMEM((2, LAYUPS), F32),
            pltpu.SMEM((3, LAYUPS), F32),
            pltpu.SMEM((LAYUPS,), F32),
            pltpu.VMEM((STEPS, MODES), BF16),
            pltpu.VMEM((3, MODES, COLS), BF16),
            pltpu.VMEM((GROUPS, STEPS, LANES), F32),
            pltpu.VMEM((3, STEPS, TILE), F32),
            pltpu.VMEM((3, STEPS, TILE), F32),
            pltpu.VMEM((3, STEPS, COLS), F32),
            pltpu.VMEM((STEPS, COLS), F32),
            pltpu.VMEM((BLOCKS, SLABS, 8, LANES), F32),
            pltpu.VMEM((BLOCKS, 8, LANES), F32),
            pltpu.VMEM((BLOCKS, 8, LANES), F32),
            pltpu.VMEM((3, STEPS, CHUNK_COLS), BF16),
            pltpu.VMEM((GROUPS, STEPS, LANES), F32),
            pltpu.VMEM((GROUPS, STEPS // 2, LANES), F32),
            pltpu.VMEM((GROUPS, NY - 1, ROWS, LANES), F32),
            pltpu.VMEM((GROUPS, NY - 1, ROWS, LANES), F32),
            pltpu.VMEM((GROUPS, STEPS, LANES), F32),
            pltpu.VMEM((GROUPS, STEPS, LANES), F32),
            pltpu.VMEM((GROUPS, ROW_BLOCKS, ROWS, LANES), F32),
            pltpu.VMEM((CHUNKS, NX, CHUNK_BLOCKS, LANES), F32),
            pltpu.VMEM((CHUNKS, NZ, CHUNK_BLOCKS, LANES), F32),
            pltpu.VMEM((NX, 2, MODES), F32),
            pltpu.VMEM((NZ, 2, MODES), F32),
            pltpu.VMEM((2 * NY, 1, MODES), F32),
            pltpu.SemaphoreType.DMA((INPUTS,)),
            pltpu.SemaphoreType.DMA((SENDS,)),
            pltpu.SemaphoreType.DMA((SENDS,)),
        ],
        compiler_params=pltpu.CompilerParams(
            collective_id=0, has_side_effects=True, vmem_limit_bytes=48 * 1024 * 1024
        ),
        name="gust_adjoint",
    )(*(
        pltpu.with_memory_space_constraint(value, pltpu.HBM)
        for value in (
            modal_coords, stress_modes, step_decay, ply_layup,
            lin_table.T, quad_table.T, base_index,
        )
    ))
    ks, adjoint = pl.pallas_call(
        write_out,
        out_shape=(
            jax.ShapeDtypeStruct((BLOCKS, LANES), F32),
            jax.ShapeDtypeStruct((STEPS, MODES), F32),
        ),
        in_specs=[vmem] * 2,
        out_specs=(hbm, hbm),
        scratch_shapes=[pltpu.SemaphoreType.DMA((2,))],
        name="write_out",
    )(
        pltpu.with_memory_space_constraint(ks, pltpu.VMEM),
        pltpu.with_memory_space_constraint(adjoint, pltpu.VMEM),
    )
    return ks.reshape(COLS), adjoint


def solution(mesh):
    return jax.shard_map(
        body,
        mesh=mesh,
        in_specs=(P("tm", None), P(None, None, "elem"), P("tm", None), P("elem"), P(), P(), P()),
        out_specs=(P("elem"), P("tm", None)),
        check_vma=False,
    )
```

```python
import math

import jax
import jax.numpy as jnp
from jax import lax
from jax.experimental import pallas as pl
from jax.experimental.pallas import tpu as pltpu
from jax.sharding import PartitionSpec as P

MESH = pl.DeviceIdType.MESH
F32 = jnp.float32
BF16 = jnp.bfloat16

NX, NZ, NY = 4, 8, 4
STEPS, MODES, COLS = 512, 512, 2048
LANES = 128
GROUPS = MODES // LANES
BLOCKS = COLS // LANES
LAYUPS = 16
TILE = 256
PARTS = 1
PART = STEPS // PARTS
TILES = COLS // TILE
CHUNKS = 2
CHUNK_COLS = COLS // CHUNKS
CHUNK_BLOCKS = BLOCKS // CHUNKS
SLAB = 64
SLABS = STEPS // SLAB
ROWS = 64
ROW_BLOCKS = STEPS // ROWS
WIDTH = 256
PER_DOT = WIDTH // LANES
SHARPNESS = 100.0
SCALE = SHARPNESS * math.log2(math.e)
HALF_SCALE = 0.5 * SCALE
SHIFT = -math.log2(2.0 * math.log(2.0))

NT = (((1,), (1,)), ((), ()))

LSE = 0
PAIR = LSE + CHUNKS * (NX * NZ - 1)
RING = PAIR + GROUPS
CARRY_X = RING + (NY - 1) * GROUPS
CARRY_Z = CARRY_X + NX - 1
INCOMING = CARRY_Z + NZ - 1
SPREAD = INCOMING + 2 * NY - 1
ACROSS = SPREAD + (NY - 1) * GROUPS
SENDS = ACROSS + NY * GROUPS

MODAL_IN = TILES
DECAY_IN = TILES + 1
TABLE_IN = DECAY_IN + GROUPS
INPUTS = TABLE_IN + 4


def kernel(
    modal_hbm, modes_hbm, decay_hbm, layup_hbm, lin_hbm, quad_hbm, base_hbm,
    ks, result,
    layup, lin, quad, base,
    modal, modes, decay, stress, graded, index, slab_max, block_max, block_sum, sens, loads,
    pair_in, partial, near_in, tail_prod, head_prod, offsets,
    shares, carry_x, carry_z, incoming,
    in_sem, send_sem, recv_sem,
):
    tm = lax.axis_index("tm")
    elem = lax.axis_index("elem")
    z, x = tm // NX, tm % NX
    y, core = elem // 2, elem % 2
    x_peers = [(z * NX + (x + d) % NX, elem) for d in range(1, NX)]
    z_peers = [(((z + d) % NZ) * NX + x, elem) for d in range(1, NZ)]
    offsets_zx = sorted(
        ((dz, dx) for dz in range(NZ) for dx in range(NX) if dz or dx),
        key=lambda o: -min(o[0], NZ - o[0]) - min(o[1], NX - o[1]),
    )
    elem_peers = [(tm, (elem + d) % (2 * NY)) for d in range(1, 2 * NY)]
    y_up, y_down, y_far = (y + 1) % NY, (y + 3) % NY, (y + 2) % NY
    pair = (tm, 2 * y + 1 - core)
    ring = [(tm, 2 * q + core) for q in (y_far, y_up, y_down)]
    ring_y = (y_far, y_down, y_up)

    sent = []

    def describe(src, dst, slot, peer):
        return pltpu.make_async_remote_copy(
            src_ref=src, dst_ref=dst, send_sem=send_sem.at[slot], recv_sem=recv_sem.at[slot],
            device_id=peer, device_id_type=MESH,
        )

    def send(src, dst, slot, peer):
        copy = describe(src, dst, slot, peer)
        copy.start()
        sent.append(copy)

    def arrived(dst, slot):
        describe(dst, dst, slot, pair).wait_recv()

    table_copies = [
        pltpu.make_async_copy(src, dst, in_sem.at[TABLE_IN + i])
        for i, (src, dst) in enumerate(
            ((layup_hbm, layup), (lin_hbm, lin), (quad_hbm, quad), (base_hbm, base))
        )
    ]

    def tile_copy(j):
        cols = pl.ds(j * TILE, TILE)
        return pltpu.make_async_copy(modes_hbm.at[:, :, cols], modes.at[:, :, cols], in_sem.at[j])

    modal_copy = pltpu.make_async_copy(modal_hbm, modal, in_sem.at[MODAL_IN])
    modal_copy.start()
    tile_copy(0).start()
    for copy in table_copies:
        copy.start()
    for j in range(1, TILES):
        tile_copy(j).start()
    decay_copies = []
    for g in range(GROUPS):
        copy = pltpu.make_async_copy(
            decay_hbm.at[:, pl.ds(g * LANES, LANES)], decay.at[g], in_sem.at[DECAY_IN + g]
        )
        copy.start()
        decay_copies.append(copy)
    barrier = pltpu.get_barrier_semaphore()
    peers = elem_peers + [
        (((z + dz) % NZ) * NX + (x + dx) % NX, elem) for dz, dx in offsets_zx
    ]
    for peer in peers:
        pl.semaphore_signal(barrier, inc=1, device_id=peer, device_id_type=MESH)

    def stress_part(target, j, part):
        cols = pl.ds(pl.multiple_of(j * TILE, TILE), TILE)
        for k in range(3):
            target[k] = jnp.dot(
                modal[pl.ds(part * PART, PART), :], modes[k, :, cols], preferred_element_type=F32
            )

    def grade_part(source, j, part):
        for h in range(TILE // LANES):
            block = j * (TILE // LANES) + h
            layer = layup[block]
            lin_one = HALF_SCALE * lin[0, layer]
            lin_two = HALF_SCALE * lin[1, layer]
            quad_one = SCALE * quad[0, layer]
            quad_two = SCALE * quad[1, layer]
            quad_shear = SCALE * quad[2, layer]
            cross = -0.5 * jnp.sqrt(jnp.full((8, LANES), quad_one * quad_two, F32))[None]
            here = pl.ds(h * LANES, LANES)
            there = pl.ds(pl.multiple_of(block * LANES, LANES), LANES)
            for r in range(part * SLABS // PARTS, (part + 1) * SLABS // PARTS):
                rows = pl.ds(r * SLAB, SLAB)
                inner = pl.ds(r * SLAB - part * PART, SLAB)
                one, two, shear = (
                    source[k, inner, here].reshape(SLAB // 8, 8, LANES) for k in range(3)
                )
                slope_one = lin_one + (quad_one * one + cross * two)
                slope_two = lin_two + (quad_two * two + cross * one)
                slope_shear = quad_shear * shear
                value = (
                    one * (lin_one + slope_one) + two * (lin_two + slope_two) + shear * slope_shear
                )
                graded[0, rows, there] = slope_one.reshape(SLAB, LANES)
                graded[1, rows, there] = slope_two.reshape(SLAB, LANES)
                graded[2, rows, there] = slope_shear.reshape(SLAB, LANES)
                index[rows, there] = value.reshape(SLAB, LANES)
                slab_max[block, r] = jnp.max(value, axis=0)

    def sum_tile(j):
        for h in range(TILE // LANES):
            block = j * (TILE // LANES) + h
            there = pl.ds(pl.multiple_of(block * LANES, LANES), LANES)
            top = jnp.max(slab_max[block], axis=0)
            parts = []
            for r in range(SLABS):
                value = index[pl.ds(r * SLAB, SLAB), there].reshape(SLAB // 8, 8, LANES)
                parts.append(jnp.sum(jnp.exp2(value - top[None]), axis=0))
            while len(parts) > 1:
                parts = [a + b for a, b in zip(parts[::2], parts[1::2])]
            block_max[block] = top
            block_sum[block] = parts[0]

    def log_two(values):
        return jnp.log(values) * math.log2(math.e)

    def log_sum(values):
        top = jnp.max(values, axis=0)
        return top + log_two(jnp.sum(jnp.exp2(values - top[None]), axis=0))

    def share_copies(c):
        for d, (dz, dx) in enumerate(offsets_zx):
            peer = (((z + dz) % NZ) * NX + (x + dx) % NX, elem)
            yield describe(shares.at[c, tm], shares.at[c, tm], LSE + c * (NX * NZ - 1) + d, peer)

    def share(c):
        blocks = pl.ds(c * CHUNK_BLOCKS, CHUNK_BLOCKS)
        tops = block_max[blocks]
        top = jnp.max(tops, axis=1)
        total = jnp.sum(block_sum[blocks] * jnp.exp2(tops - top[:, None, :]), axis=1)
        shares[c, tm] = top + log_two(total)
        for copy in share_copies(c):
            copy.start()

    def finish_lse(c):
        for d, (dz, dx) in enumerate(offsets_zx):
            source = ((z + NZ - dz) % NZ) * NX + (x + NX - dx) % NX
            arrived(shares.at[c, source], LSE + c * (NX * NZ - 1) + d)
        lse = log_sum(shares[c])
        for b in range(CHUNK_BLOCKS):
            block = c * CHUNK_BLOCKS + b
            ks[pl.ds(block, 1), :] = lse[b : b + 1] * (1.0 / SCALE) + base[layup[block]]
        return lse + SHIFT

    def weigh(c, lse, half):
        for i in range(SLABS // 2):
            r = half * (SLABS // 2) + i
            rows = pl.ds(pl.multiple_of(r * SLAB, SLAB), SLAB)
            for b in range(CHUNK_BLOCKS):
                there = pl.ds((c * CHUNK_BLOCKS + b) * LANES, LANES)
                here = pl.ds(b * LANES, LANES)
                weight = jnp.exp2(index[rows, there] - lse[b : b + 1])
                for k in range(3):
                    sens[k, rows, here] = (weight * graded[k, rows, there]).astype(BF16)

    def load_rows(c, half, piece):
        rows = pl.ds(pl.multiple_of(half * (STEPS // 2), STEPS // 2), STEPS // 2)
        total = None
        for k in range(3):
            part = lax.dot_general(
                sens[k, rows, :],
                modes[k, pl.ds(piece * WIDTH, WIDTH), pl.ds(c * CHUNK_COLS, CHUNK_COLS)],
                NT, preferred_element_type=F32,
            )
            total = part if total is None else total + part
        for h in range(PER_DOT):
            g = piece * PER_DOT + h
            part = total[:, h * LANES : (h + 1) * LANES]
            loads[g, rows, :] = part if c == 0 else loads[g, rows, :] + part

    modal_copy.wait()
    for copy in table_copies:
        copy.wait()

    def stress_pair(p, carry):
        first = 2 * p
        tile_copy(first).wait()
        tile_copy(first + 1).wait()
        for n in range(2):
            for part in range(PARTS):
                target = stress.at[n * PARTS + part]
                stress_part(target, first + n, part)
                grade_part(target, first + n, part)
        sum_tile(first)

        @pl.when(p == 0)
        def _():
            pl.semaphore_wait(barrier, len(peers))

        sum_tile(first + 1)

        @pl.when(p % 2 == 1)
        def _():
            share(p // 2)

        return carry

    lax.fori_loop(0, TILES // 2, stress_pair, 0)

    for copy in decay_copies:
        copy.wait()
    tiles = ROWS // 8
    level = lax.broadcasted_iota(jnp.int32, (tiles, 8, LANES), 1)

    def product_step(i, carry):
        g, r = i // ROW_BLOCKS, i % ROW_BLOCKS
        rows = pl.ds(pl.multiple_of(r * ROWS, ROWS), ROWS)
        tail = decay[g, rows, :].reshape(tiles, 8, LANES)
        head = tail
        for step in (1, 2, 4):
            tail = tail * jnp.where(level < 8 - step, pltpu.roll(tail, 8 - step, 1), 1.0)
            head = head * jnp.where(level >= step, pltpu.roll(head, step, 1), 1.0)
        before = jnp.where(level >= 1, pltpu.roll(head, 1, 1), 1.0)
        after = jnp.ones((1, LANES), F32)
        ahead = jnp.ones((1, LANES), F32)
        for n in range(tiles):
            m = tiles - 1 - n
            tail_prod[g, pl.ds(pl.multiple_of(r * ROWS + m * 8, 8), 8), :] = tail[m] * after
            after = after * tail[m, 0:1]
            head_prod[g, pl.ds(pl.multiple_of(r * ROWS + n * 8, 8), 8), :] = before[n] * ahead
            ahead = ahead * head[n, 7:8]
        return carry

    lax.fori_loop(0, GROUPS * ROW_BLOCKS, product_step, 0, unroll=4)

    for c in range(CHUNKS - 1):
        lse = finish_lse(c)
        for half in range(2):
            weigh(c, lse, half)
            for piece in range(MODES // WIDTH):
                load_rows(c, half, piece)
    last = CHUNKS - 1
    lse = finish_lse(last)

    pair_rows = pl.ds(pl.multiple_of((1 - core) * (STEPS // 2), STEPS // 2), STEPS // 2)
    weigh(last, lse, 1 - core)
    for piece in range(MODES // WIDTH):
        load_rows(last, 1 - core, piece)
        for g in range(piece * PER_DOT, (piece + 1) * PER_DOT):
            send(loads.at[g, pair_rows, :], pair_in.at[g], PAIR + g, pair)
    weigh(last, lse, core)
    for piece in range(MODES // WIDTH):
        load_rows(last, core, piece)

    def pair_sum(g, q):
        here = pl.ds(pl.multiple_of(q * ROWS, ROWS), ROWS)
        there = pl.ds(pl.multiple_of(core * (STEPS // 2) + q * ROWS, ROWS), ROWS)
        return loads[g, there, :] + pair_in[g, here, :]

    for g in range(GROUPS):
        arrived(pair_in.at[g], PAIR + g)
        for i, q in enumerate((y_far, y_up, y_down)):
            partial[g, i] = pair_sum(g, q)
            send(partial.at[g, i], near_in.at[g, i], RING + (NY - 1) * g + i, ring[i])

    for g in range(GROUPS):
        ahead = jnp.ones((1, LANES), F32)
        state = jnp.zeros((1, LANES), F32)
        for r in range(ROW_BLOCKS):
            rows = pl.ds(r * ROWS, ROWS)
            block_sum = jnp.sum(head_prod[g, rows, :] * loads[g, rows, :], axis=0, keepdims=True)
            state = state + ahead * block_sum
            ahead = ahead * tail_prod[g, r * ROWS : r * ROWS + 1, :]
        carry_x[x, 0:1, pl.ds(g * LANES, LANES)] = ahead
        carry_x[x, 1:2, pl.ds(g * LANES, LANES)] = state
    for d, peer in enumerate(x_peers):
        send(carry_x.at[x], carry_x.at[x], CARRY_X + d, peer)

    for d in range(NX - 1):
        arrived(carry_x.at[(x + NX - 1 - d) % NX], CARRY_X + d)
    slab_scale = jnp.ones((1, MODES), F32)
    slab_state = jnp.zeros((1, MODES), F32)
    later_scale, later_state = slab_scale, slab_state
    for q in range(NX - 1, -1, -1):
        scale, offset = carry_x[q, 0:1, :], carry_x[q, 1:2, :]
        slab_state = offset + scale * slab_state
        slab_scale = scale * slab_scale
        later_state = jnp.where(q > x, offset + scale * later_state, later_state)
        later_scale = jnp.where(q > x, scale * later_scale, later_scale)
    carry_z[z, 0:1, :] = slab_scale
    carry_z[z, 1:2, :] = slab_state
    for d, peer in enumerate(z_peers):
        send(carry_z.at[z], carry_z.at[z], CARRY_Z + d, peer)

    mine = core * NY + y

    def spread(g, block, slot, peer):
        send(offsets.at[g, block], offsets.at[g, block], slot, peer)

    mine_rows = pl.ds(pl.multiple_of(mine * ROWS, ROWS), ROWS)
    for g in range(GROUPS):
        for i in range(NY - 1):
            arrived(near_in.at[g, i], RING + (NY - 1) * g + i)
        state = (pair_sum(g, y) + near_in[g, 1]) + (near_in[g, 2] + near_in[g, 0])
        state = state.reshape(tiles, 8, LANES)
        factor = decay[g, mine_rows, :].reshape(tiles, 8, LANES)
        for step in (1, 2, 4):
            inside = level < 8 - step
            state = state + factor * jnp.where(inside, pltpu.roll(state, 8 - step, 1), 0.0)
            factor = factor * jnp.where(inside, pltpu.roll(factor, 8 - step, 1), 1.0)
        running = jnp.zeros((1, LANES), F32)
        for m in range(tiles - 1, -1, -1):
            value = state[m] + factor[m] * running
            offsets[g, mine, pl.ds(m * 8, 8), :] = value
            running = value[0:1]
        for i in range(NY - 1):
            spread(g, mine, SPREAD + (NY - 1) * g + i, ring[i])
        spread(g, mine, ACROSS + NY * g, pair)

    for d in range(NZ - 1):
        arrived(carry_z.at[(z + NZ - 1 - d) % NZ], CARRY_Z + d)
    far_state = jnp.zeros((1, MODES), F32)
    for q in range(NZ - 1, -1, -1):
        far_state = jnp.where(q > z, carry_z[q, 1:2, :] + carry_z[q, 0:1, :] * far_state, far_state)
    incoming[elem] = later_state + later_scale * far_state
    for d, peer in enumerate(elem_peers):
        send(incoming.at[elem], incoming.at[elem], INCOMING + d, peer)

    for g in range(GROUPS):
        for i, q in enumerate(ring_y):
            arrived(offsets.at[g, core * NY + q], SPREAD + (NY - 1) * g + i)
            spread(g, core * NY + q, ACROSS + NY * g + 1 + i, pair)

    for d in range(2 * NY - 1):
        arrived(incoming.at[(elem + 2 * NY - 1 - d) % (2 * NY)], INCOMING + d)
    behind = incoming[0]
    for e in range(1, 2 * NY):
        behind = behind + incoming[e]

    other = (1 - core) * NY
    for g in range(GROUPS):
        for i, q in enumerate((y,) + ring_y):
            arrived(offsets.at[g, other + q], ACROSS + NY * g + i)
        there = pl.ds(g * LANES, LANES)
        state = behind[:, g * LANES : (g + 1) * LANES]
        for r in range(ROW_BLOCKS - 1, -1, -1):
            rows = pl.ds(r * ROWS, ROWS)
            result[rows, there] = offsets[g, r] + tail_prod[g, rows, :] * state
            state = offsets[g, r, 0:1, :] + tail_prod[g, r * ROWS : r * ROWS + 1, :] * state

    for copy in sent:
        copy.wait_send()
    for c in range(CHUNKS):
        for copy in share_copies(c):
            copy.wait_send()


def write_out(ks, result, ks_hbm, adjoint_hbm, sem):
    copies = [
        pltpu.make_async_copy(result, adjoint_hbm, sem.at[0]),
        pltpu.make_async_copy(ks, ks_hbm, sem.at[1]),
    ]
    for copy in copies:
        copy.start()
    for copy in copies:
        copy.wait()


def body(modal_coords, stress_modes, step_decay, ply_layup, lin_table, quad_table, base_index):
    hbm = pl.BlockSpec(memory_space=pl.ANY)
    vmem = pl.BlockSpec(memory_space=pltpu.VMEM)
    ks, adjoint = pl.pallas_call(
        kernel,
        out_shape=(
            pltpu.VMEM((BLOCKS, LANES), F32),
            pltpu.VMEM((STEPS, MODES), F32),
        ),
        in_specs=[hbm] * 7,
        out_specs=(vmem, vmem),
        scratch_shapes=[
            pltpu.SMEM((BLOCKS,), jnp.int32),
            pltpu.SMEM((2, LAYUPS), F32),
            pltpu.SMEM((3, LAYUPS), F32),
            pltpu.SMEM((LAYUPS,), F32),
            pltpu.VMEM((STEPS, MODES), BF16),
            pltpu.VMEM((3, MODES, COLS), BF16),
            pltpu.VMEM((GROUPS, STEPS, LANES), F32),
            pltpu.VMEM((2 * PARTS, 3, PART, TILE), F32),
            pltpu.VMEM((3, STEPS, COLS), F32),
            pltpu.VMEM((STEPS, COLS), F32),
            pltpu.VMEM((BLOCKS, SLABS, 8, LANES), F32),
            pltpu.VMEM((BLOCKS, 8, LANES), F32),
            pltpu.VMEM((BLOCKS, 8, LANES), F32),
            pltpu.VMEM((3, STEPS, CHUNK_COLS), BF16),
            pltpu.VMEM((GROUPS, STEPS, LANES), F32),
            pltpu.VMEM((GROUPS, STEPS // 2, LANES), F32),
            pltpu.VMEM((GROUPS, NY - 1, ROWS, LANES), F32),
            pltpu.VMEM((GROUPS, NY - 1, ROWS, LANES), F32),
            pltpu.VMEM((GROUPS, STEPS, LANES), F32),
            pltpu.VMEM((GROUPS, STEPS, LANES), F32),
            pltpu.VMEM((GROUPS, ROW_BLOCKS, ROWS, LANES), F32),
            pltpu.VMEM((CHUNKS, NX * NZ, CHUNK_BLOCKS, LANES), F32),
            pltpu.VMEM((NX, 2, MODES), F32),
            pltpu.VMEM((NZ, 2, MODES), F32),
            pltpu.VMEM((2 * NY, 1, MODES), F32),
            pltpu.SemaphoreType.DMA((INPUTS,)),
            pltpu.SemaphoreType.DMA((SENDS,)),
            pltpu.SemaphoreType.DMA((SENDS,)),
        ],
        compiler_params=pltpu.CompilerParams(
            collective_id=0, has_side_effects=True, vmem_limit_bytes=48 * 1024 * 1024
        ),
        name="gust_adjoint",
    )(*(
        pltpu.with_memory_space_constraint(value, pltpu.HBM)
        for value in (
            modal_coords, stress_modes, step_decay, ply_layup,
            lin_table.T, quad_table.T, base_index,
        )
    ))
    ks, adjoint = pl.pallas_call(
        write_out,
        out_shape=(
            jax.ShapeDtypeStruct((BLOCKS, LANES), F32),
            jax.ShapeDtypeStruct((STEPS, MODES), F32),
        ),
        in_specs=[vmem] * 2,
        out_specs=(hbm, hbm),
        scratch_shapes=[pltpu.SemaphoreType.DMA((2,))],
        name="write_out",
    )(
        pltpu.with_memory_space_constraint(ks, pltpu.VMEM),
        pltpu.with_memory_space_constraint(adjoint, pltpu.VMEM),
    )
    return ks.reshape(COLS), adjoint


def solution(mesh):
    return jax.shard_map(
        body,
        mesh=mesh,
        in_specs=(P("tm", None), P(None, None, "elem"), P("tm", None), P("elem"), P(), P(), P()),
        out_specs=(P("elem"), P("tm", None)),
        check_vma=False,
    )
```

```python
import math

import jax
import jax.numpy as jnp
from jax import lax
from jax.experimental import pallas as pl
from jax.experimental.pallas import tpu as pltpu
from jax.sharding import PartitionSpec as P

MESH = pl.DeviceIdType.MESH
F32 = jnp.float32
BF16 = jnp.bfloat16

NX, NZ, NY = 4, 8, 4
STEPS, MODES, COLS = 512, 512, 2048
LANES = 128
GROUPS = MODES // LANES
BLOCKS = COLS // LANES
LAYUPS = 16
TILE = 256
PARTS = 1
PART = STEPS // PARTS
TILES = COLS // TILE
CHUNKS = 4
CHUNK_COLS = COLS // CHUNKS
CHUNK_BLOCKS = BLOCKS // CHUNKS
SLAB = 64
SLABS = STEPS // SLAB
ROWS = 64
ROW_BLOCKS = STEPS // ROWS
WIDTH = 256
PER_DOT = WIDTH // LANES
SHARPNESS = 100.0
SCALE = SHARPNESS * math.log2(math.e)
HALF_SCALE = 0.5 * SCALE
SHIFT = -math.log2(2.0 * math.log(2.0))

NT = (((1,), (1,)), ((), ()))

LSE = 0
PAIR = LSE + CHUNKS * (NX * NZ - 1)
RING = PAIR + GROUPS
CARRY_X = RING + (NY - 1) * GROUPS
CARRY_Z = CARRY_X + NX - 1
INCOMING = CARRY_Z + NZ - 1
SPREAD = INCOMING + 2 * NY - 1
ACROSS = SPREAD + (NY - 1) * GROUPS
SENDS = ACROSS + NY * GROUPS

MODAL_IN = TILES
DECAY_IN = TILES + 1
TABLE_IN = DECAY_IN + GROUPS
INPUTS = TABLE_IN + 4


def kernel(
    modal_hbm, modes_hbm, decay_hbm, layup_hbm, lin_hbm, quad_hbm, base_hbm,
    ks, result,
    layup, lin, quad, base,
    modal, modes, decay, stress, graded, index, slab_max, block_max, block_sum, sens, loads,
    pair_in, partial, near_in, tail_prod, head_prod, offsets,
    shares, carry_x, carry_z, incoming,
    in_sem, send_sem, recv_sem,
):
    tm = lax.axis_index("tm")
    elem = lax.axis_index("elem")
    z, x = tm // NX, tm % NX
    y, core = elem // 2, elem % 2
    x_peers = [(z * NX + (x + d) % NX, elem) for d in range(1, NX)]
    z_peers = [(((z + d) % NZ) * NX + x, elem) for d in range(1, NZ)]
    offsets_zx = sorted(
        ((dz, dx) for dz in range(NZ) for dx in range(NX) if dz or dx),
        key=lambda o: -min(o[0], NZ - o[0]) - min(o[1], NX - o[1]),
    )
    elem_peers = [(tm, (elem + d) % (2 * NY)) for d in range(1, 2 * NY)]
    y_up, y_down, y_far = (y + 1) % NY, (y + 3) % NY, (y + 2) % NY
    pair = (tm, 2 * y + 1 - core)
    ring = [(tm, 2 * q + core) for q in (y_far, y_up, y_down)]
    ring_y = (y_far, y_down, y_up)

    sent = []

    def describe(src, dst, slot, peer):
        return pltpu.make_async_remote_copy(
            src_ref=src, dst_ref=dst, send_sem=send_sem.at[slot], recv_sem=recv_sem.at[slot],
            device_id=peer, device_id_type=MESH,
        )

    def send(src, dst, slot, peer):
        copy = describe(src, dst, slot, peer)
        copy.start()
        sent.append(copy)

    def arrived(dst, slot):
        describe(dst, dst, slot, pair).wait_recv()

    table_copies = [
        pltpu.make_async_copy(src, dst, in_sem.at[TABLE_IN + i])
        for i, (src, dst) in enumerate(
            ((layup_hbm, layup), (lin_hbm, lin), (quad_hbm, quad), (base_hbm, base))
        )
    ]

    def tile_copy(j):
        cols = pl.ds(j * TILE, TILE)
        return pltpu.make_async_copy(modes_hbm.at[:, :, cols], modes.at[:, :, cols], in_sem.at[j])

    modal_copy = pltpu.make_async_copy(modal_hbm, modal, in_sem.at[MODAL_IN])
    modal_copy.start()
    tile_copy(0).start()
    for copy in table_copies:
        copy.start()
    for j in range(1, TILES):
        tile_copy(j).start()
    decay_copies = []
    for g in range(GROUPS):
        copy = pltpu.make_async_copy(
            decay_hbm.at[:, pl.ds(g * LANES, LANES)], decay.at[g], in_sem.at[DECAY_IN + g]
        )
        copy.start()
        decay_copies.append(copy)
    barrier = pltpu.get_barrier_semaphore()
    peers = elem_peers + [
        (((z + dz) % NZ) * NX + (x + dx) % NX, elem) for dz, dx in offsets_zx
    ]
    for peer in peers:
        pl.semaphore_signal(barrier, inc=1, device_id=peer, device_id_type=MESH)

    def stress_part(target, j, part):
        cols = pl.ds(pl.multiple_of(j * TILE, TILE), TILE)
        for k in range(3):
            target[k] = jnp.dot(
                modal[pl.ds(part * PART, PART), :], modes[k, :, cols], preferred_element_type=F32
            )

    def grade_part(source, j, part):
        for h in range(TILE // LANES):
            block = j * (TILE // LANES) + h
            layer = layup[block]
            lin_one = HALF_SCALE * lin[0, layer]
            lin_two = HALF_SCALE * lin[1, layer]
            quad_one = SCALE * quad[0, layer]
            quad_two = SCALE * quad[1, layer]
            quad_shear = SCALE * quad[2, layer]
            cross = -0.5 * jnp.sqrt(jnp.full((8, LANES), quad_one * quad_two, F32))[None]
            here = pl.ds(h * LANES, LANES)
            there = pl.ds(pl.multiple_of(block * LANES, LANES), LANES)
            for r in range(part * SLABS // PARTS, (part + 1) * SLABS // PARTS):
                rows = pl.ds(r * SLAB, SLAB)
                inner = pl.ds(r * SLAB - part * PART, SLAB)
                one, two, shear = (
                    source[k, inner, here].reshape(SLAB // 8, 8, LANES) for k in range(3)
                )
                slope_one = lin_one + (quad_one * one + cross * two)
                slope_two = lin_two + (quad_two * two + cross * one)
                slope_shear = quad_shear * shear
                value = (
                    one * (lin_one + slope_one) + two * (lin_two + slope_two) + shear * slope_shear
                )
                graded[0, rows, there] = slope_one.reshape(SLAB, LANES)
                graded[1, rows, there] = slope_two.reshape(SLAB, LANES)
                graded[2, rows, there] = slope_shear.reshape(SLAB, LANES)
                index[rows, there] = value.reshape(SLAB, LANES)
                slab_max[block, r] = jnp.max(value, axis=0)

    def sum_tile(j):
        for h in range(TILE // LANES):
            block = j * (TILE // LANES) + h
            there = pl.ds(pl.multiple_of(block * LANES, LANES), LANES)
            top = jnp.max(slab_max[block], axis=0)
            parts = []
            for r in range(SLABS):
                value = index[pl.ds(r * SLAB, SLAB), there].reshape(SLAB // 8, 8, LANES)
                parts.append(jnp.sum(jnp.exp2(value - top[None]), axis=0))
            while len(parts) > 1:
                parts = [a + b for a, b in zip(parts[::2], parts[1::2])]
            block_max[block] = top
            block_sum[block] = parts[0]

    def log_two(values):
        return jnp.log(values) * math.log2(math.e)

    def log_sum(values):
        top = jnp.max(values, axis=0)
        return top + log_two(jnp.sum(jnp.exp2(values - top[None]), axis=0))

    def share_copies(c):
        for d, (dz, dx) in enumerate(offsets_zx):
            peer = (((z + dz) % NZ) * NX + (x + dx) % NX, elem)
            yield describe(shares.at[c, tm], shares.at[c, tm], LSE + c * (NX * NZ - 1) + d, peer)

    def share(c):
        blocks = pl.ds(c * CHUNK_BLOCKS, CHUNK_BLOCKS)
        tops = block_max[blocks]
        top = jnp.max(tops, axis=1)
        total = jnp.sum(block_sum[blocks] * jnp.exp2(tops - top[:, None, :]), axis=1)
        shares[c, tm] = top + log_two(total)
        for copy in share_copies(c):
            copy.start()

    def finish_lse(c):
        for d, (dz, dx) in enumerate(offsets_zx):
            source = ((z + NZ - dz) % NZ) * NX + (x + NX - dx) % NX
            arrived(shares.at[c, source], LSE + c * (NX * NZ - 1) + d)
        lse = log_sum(shares[c])
        for b in range(CHUNK_BLOCKS):
            block = c * CHUNK_BLOCKS + b
            ks[pl.ds(block, 1), :] = lse[b : b + 1] * (1.0 / SCALE) + base[layup[block]]
        return lse + SHIFT

    def weigh(c, lse, half):
        for i in range(SLABS // 2):
            r = half * (SLABS // 2) + i
            rows = pl.ds(pl.multiple_of(r * SLAB, SLAB), SLAB)
            for b in range(CHUNK_BLOCKS):
                there = pl.ds((c * CHUNK_BLOCKS + b) * LANES, LANES)
                here = pl.ds(b * LANES, LANES)
                weight = jnp.exp2(index[rows, there] - lse[b : b + 1])
                for k in range(3):
                    sens[k, rows, here] = (weight * graded[k, rows, there]).astype(BF16)

    def load_rows(c, half, piece):
        rows = pl.ds(pl.multiple_of(half * (STEPS // 2), STEPS // 2), STEPS // 2)
        total = None
        for k in range(3):
            part = lax.dot_general(
                sens[k, rows, :],
                modes[k, pl.ds(piece * WIDTH, WIDTH), pl.ds(c * CHUNK_COLS, CHUNK_COLS)],
                NT, preferred_element_type=F32,
            )
            total = part if total is None else total + part
        for h in range(PER_DOT):
            g = piece * PER_DOT + h
            part = total[:, h * LANES : (h + 1) * LANES]
            loads[g, rows, :] = part if c == 0 else loads[g, rows, :] + part

    modal_copy.wait()
    for copy in table_copies:
        copy.wait()

    def stress_pair(p, carry):
        first = 2 * p
        tile_copy(first).wait()
        tile_copy(first + 1).wait()
        for n in range(2):
            for part in range(PARTS):
                target = stress.at[n * PARTS + part]
                stress_part(target, first + n, part)
                grade_part(target, first + n, part)
        sum_tile(first)

        @pl.when(p == 0)
        def _():
            pl.semaphore_wait(barrier, len(peers))

        sum_tile(first + 1)

        share(p)
        return carry

    lax.fori_loop(0, TILES // 2, stress_pair, 0)

    for copy in decay_copies:
        copy.wait()
    tiles = ROWS // 8
    level = lax.broadcasted_iota(jnp.int32, (tiles, 8, LANES), 1)

    def product_step(i, carry):
        g, r = i // ROW_BLOCKS, i % ROW_BLOCKS
        rows = pl.ds(pl.multiple_of(r * ROWS, ROWS), ROWS)
        tail = decay[g, rows, :].reshape(tiles, 8, LANES)
        head = tail
        for step in (1, 2, 4):
            tail = tail * jnp.where(level < 8 - step, pltpu.roll(tail, 8 - step, 1), 1.0)
            head = head * jnp.where(level >= step, pltpu.roll(head, step, 1), 1.0)
        before = jnp.where(level >= 1, pltpu.roll(head, 1, 1), 1.0)
        after = jnp.ones((1, LANES), F32)
        ahead = jnp.ones((1, LANES), F32)
        for n in range(tiles):
            m = tiles - 1 - n
            tail_prod[g, pl.ds(pl.multiple_of(r * ROWS + m * 8, 8), 8), :] = tail[m] * after
            after = after * tail[m, 0:1]
            head_prod[g, pl.ds(pl.multiple_of(r * ROWS + n * 8, 8), 8), :] = before[n] * ahead
            ahead = ahead * head[n, 7:8]
        return carry

    lax.fori_loop(0, GROUPS * ROW_BLOCKS, product_step, 0, unroll=4)

    for c in range(CHUNKS - 1):
        lse = finish_lse(c)
        for half in range(2):
            weigh(c, lse, half)
            for piece in range(MODES // WIDTH):
                load_rows(c, half, piece)
    last = CHUNKS - 1
    lse = finish_lse(last)

    pair_rows = pl.ds(pl.multiple_of((1 - core) * (STEPS // 2), STEPS // 2), STEPS // 2)
    weigh(last, lse, 1 - core)
    for piece in range(MODES // WIDTH):
        load_rows(last, 1 - core, piece)
        for g in range(piece * PER_DOT, (piece + 1) * PER_DOT):
            send(loads.at[g, pair_rows, :], pair_in.at[g], PAIR + g, pair)
    weigh(last, lse, core)
    for piece in range(MODES // WIDTH):
        load_rows(last, core, piece)

    def pair_sum(g, q):
        here = pl.ds(pl.multiple_of(q * ROWS, ROWS), ROWS)
        there = pl.ds(pl.multiple_of(core * (STEPS // 2) + q * ROWS, ROWS), ROWS)
        return loads[g, there, :] + pair_in[g, here, :]

    for g in range(GROUPS):
        arrived(pair_in.at[g], PAIR + g)
        for i, q in enumerate((y_far, y_up, y_down)):
            partial[g, i] = pair_sum(g, q)
            send(partial.at[g, i], near_in.at[g, i], RING + (NY - 1) * g + i, ring[i])

    for g in range(GROUPS):
        ahead = jnp.ones((1, LANES), F32)
        state = jnp.zeros((1, LANES), F32)
        for r in range(ROW_BLOCKS):
            rows = pl.ds(r * ROWS, ROWS)
            block_sum = jnp.sum(head_prod[g, rows, :] * loads[g, rows, :], axis=0, keepdims=True)
            state = state + ahead * block_sum
            ahead = ahead * tail_prod[g, r * ROWS : r * ROWS + 1, :]
        carry_x[x, 0:1, pl.ds(g * LANES, LANES)] = ahead
        carry_x[x, 1:2, pl.ds(g * LANES, LANES)] = state
    for d, peer in enumerate(x_peers):
        send(carry_x.at[x], carry_x.at[x], CARRY_X + d, peer)

    for d in range(NX - 1):
        arrived(carry_x.at[(x + NX - 1 - d) % NX], CARRY_X + d)
    slab_scale = jnp.ones((1, MODES), F32)
    slab_state = jnp.zeros((1, MODES), F32)
    later_scale, later_state = slab_scale, slab_state
    for q in range(NX - 1, -1, -1):
        scale, offset = carry_x[q, 0:1, :], carry_x[q, 1:2, :]
        slab_state = offset + scale * slab_state
        slab_scale = scale * slab_scale
        later_state = jnp.where(q > x, offset + scale * later_state, later_state)
        later_scale = jnp.where(q > x, scale * later_scale, later_scale)
    carry_z[z, 0:1, :] = slab_scale
    carry_z[z, 1:2, :] = slab_state
    for d, peer in enumerate(z_peers):
        send(carry_z.at[z], carry_z.at[z], CARRY_Z + d, peer)

    mine = core * NY + y

    def spread(g, block, slot, peer):
        send(offsets.at[g, block], offsets.at[g, block], slot, peer)

    mine_rows = pl.ds(pl.multiple_of(mine * ROWS, ROWS), ROWS)
    for g in range(GROUPS):
        for i in range(NY - 1):
            arrived(near_in.at[g, i], RING + (NY - 1) * g + i)
        state = (pair_sum(g, y) + near_in[g, 1]) + (near_in[g, 2] + near_in[g, 0])
        state = state.reshape(tiles, 8, LANES)
        factor = decay[g, mine_rows, :].reshape(tiles, 8, LANES)
        for step in (1, 2, 4):
            inside = level < 8 - step
            state = state + factor * jnp.where(inside, pltpu.roll(state, 8 - step, 1), 0.0)
            factor = factor * jnp.where(inside, pltpu.roll(factor, 8 - step, 1), 1.0)
        running = jnp.zeros((1, LANES), F32)
        for m in range(tiles - 1, -1, -1):
            value = state[m] + factor[m] * running
            offsets[g, mine, pl.ds(m * 8, 8), :] = value
            running = value[0:1]
        for i in range(NY - 1):
            spread(g, mine, SPREAD + (NY - 1) * g + i, ring[i])
        spread(g, mine, ACROSS + NY * g, pair)

    for d in range(NZ - 1):
        arrived(carry_z.at[(z + NZ - 1 - d) % NZ], CARRY_Z + d)
    far_state = jnp.zeros((1, MODES), F32)
    for q in range(NZ - 1, -1, -1):
        far_state = jnp.where(q > z, carry_z[q, 1:2, :] + carry_z[q, 0:1, :] * far_state, far_state)
    incoming[elem] = later_state + later_scale * far_state
    for d, peer in enumerate(elem_peers):
        send(incoming.at[elem], incoming.at[elem], INCOMING + d, peer)

    for g in range(GROUPS):
        for i, q in enumerate(ring_y):
            arrived(offsets.at[g, core * NY + q], SPREAD + (NY - 1) * g + i)
            spread(g, core * NY + q, ACROSS + NY * g + 1 + i, pair)

    for d in range(2 * NY - 1):
        arrived(incoming.at[(elem + 2 * NY - 1 - d) % (2 * NY)], INCOMING + d)
    behind = incoming[0]
    for e in range(1, 2 * NY):
        behind = behind + incoming[e]

    other = (1 - core) * NY
    for g in range(GROUPS):
        for i, q in enumerate((y,) + ring_y):
            arrived(offsets.at[g, other + q], ACROSS + NY * g + i)
        there = pl.ds(g * LANES, LANES)
        state = behind[:, g * LANES : (g + 1) * LANES]
        for r in range(ROW_BLOCKS - 1, -1, -1):
            rows = pl.ds(r * ROWS, ROWS)
            result[rows, there] = offsets[g, r] + tail_prod[g, rows, :] * state
            state = offsets[g, r, 0:1, :] + tail_prod[g, r * ROWS : r * ROWS + 1, :] * state

    for copy in sent:
        copy.wait_send()
    for c in range(CHUNKS):
        for copy in share_copies(c):
            copy.wait_send()


def write_out(ks, result, ks_hbm, adjoint_hbm, sem):
    copies = [
        pltpu.make_async_copy(result, adjoint_hbm, sem.at[0]),
        pltpu.make_async_copy(ks, ks_hbm, sem.at[1]),
    ]
    for copy in copies:
        copy.start()
    for copy in copies:
        copy.wait()


def body(modal_coords, stress_modes, step_decay, ply_layup, lin_table, quad_table, base_index):
    hbm = pl.BlockSpec(memory_space=pl.ANY)
    vmem = pl.BlockSpec(memory_space=pltpu.VMEM)
    ks, adjoint = pl.pallas_call(
        kernel,
        out_shape=(
            pltpu.VMEM((BLOCKS, LANES), F32),
            pltpu.VMEM((STEPS, MODES), F32),
        ),
        in_specs=[hbm] * 7,
        out_specs=(vmem, vmem),
        scratch_shapes=[
            pltpu.SMEM((BLOCKS,), jnp.int32),
            pltpu.SMEM((2, LAYUPS), F32),
            pltpu.SMEM((3, LAYUPS), F32),
            pltpu.SMEM((LAYUPS,), F32),
            pltpu.VMEM((STEPS, MODES), BF16),
            pltpu.VMEM((3, MODES, COLS), BF16),
            pltpu.VMEM((GROUPS, STEPS, LANES), F32),
            pltpu.VMEM((2 * PARTS, 3, PART, TILE), F32),
            pltpu.VMEM((3, STEPS, COLS), F32),
            pltpu.VMEM((STEPS, COLS), F32),
            pltpu.VMEM((BLOCKS, SLABS, 8, LANES), F32),
            pltpu.VMEM((BLOCKS, 8, LANES), F32),
            pltpu.VMEM((BLOCKS, 8, LANES), F32),
            pltpu.VMEM((3, STEPS, CHUNK_COLS), BF16),
            pltpu.VMEM((GROUPS, STEPS, LANES), F32),
            pltpu.VMEM((GROUPS, STEPS // 2, LANES), F32),
            pltpu.VMEM((GROUPS, NY - 1, ROWS, LANES), F32),
            pltpu.VMEM((GROUPS, NY - 1, ROWS, LANES), F32),
            pltpu.VMEM((GROUPS, STEPS, LANES), F32),
            pltpu.VMEM((GROUPS, STEPS, LANES), F32),
            pltpu.VMEM((GROUPS, ROW_BLOCKS, ROWS, LANES), F32),
            pltpu.VMEM((CHUNKS, NX * NZ, CHUNK_BLOCKS, LANES), F32),
            pltpu.VMEM((NX, 2, MODES), F32),
            pltpu.VMEM((NZ, 2, MODES), F32),
            pltpu.VMEM((2 * NY, 1, MODES), F32),
            pltpu.SemaphoreType.DMA((INPUTS,)),
            pltpu.SemaphoreType.DMA((SENDS,)),
            pltpu.SemaphoreType.DMA((SENDS,)),
        ],
        compiler_params=pltpu.CompilerParams(
            collective_id=0, has_side_effects=True, vmem_limit_bytes=48 * 1024 * 1024
        ),
        name="gust_adjoint",
    )(*(
        pltpu.with_memory_space_constraint(value, pltpu.HBM)
        for value in (
            modal_coords, stress_modes, step_decay, ply_layup,
            lin_table.T, quad_table.T, base_index,
        )
    ))
    ks, adjoint = pl.pallas_call(
        write_out,
        out_shape=(
            jax.ShapeDtypeStruct((BLOCKS, LANES), F32),
            jax.ShapeDtypeStruct((STEPS, MODES), F32),
        ),
        in_specs=[vmem] * 2,
        out_specs=(hbm, hbm),
        scratch_shapes=[pltpu.SemaphoreType.DMA((2,))],
        name="write_out",
    )(
        pltpu.with_memory_space_constraint(ks, pltpu.VMEM),
        pltpu.with_memory_space_constraint(adjoint, pltpu.VMEM),
    )
    return ks.reshape(COLS), adjoint


def solution(mesh):
    return jax.shard_map(
        body,
        mesh=mesh,
        in_specs=(P("tm", None), P(None, None, "elem"), P("tm", None), P("elem"), P(), P(), P()),
        out_specs=(P("elem"), P("tm", None)),
        check_vma=False,
    )
```

```python
import math

import jax
import jax.numpy as jnp
from jax import lax
from jax.experimental import pallas as pl
from jax.experimental.pallas import tpu as pltpu
from jax.sharding import PartitionSpec as P

MESH = pl.DeviceIdType.MESH
F32 = jnp.float32
BF16 = jnp.bfloat16

NX, NZ, NY = 4, 8, 4
STEPS, MODES, COLS = 512, 512, 2048
LANES = 128
GROUPS = MODES // LANES
BLOCKS = COLS // LANES
LAYUPS = 16
TILE = 256
PARTS = 1
PART = STEPS // PARTS
TILES = COLS // TILE
CHUNKS = 2
CHUNK_COLS = COLS // CHUNKS
CHUNK_BLOCKS = BLOCKS // CHUNKS
SLAB = 64
SLABS = STEPS // SLAB
ROWS = 64
ROW_BLOCKS = STEPS // ROWS
WIDTH = 256
PER_DOT = WIDTH // LANES
SHARPNESS = 100.0
SCALE = SHARPNESS * math.log2(math.e)
HALF_SCALE = 0.5 * SCALE
SHIFT = -math.log2(2.0 * math.log(2.0))

NT = (((1,), (1,)), ((), ()))

LSE = 0
PAIR = LSE + CHUNKS
RING = PAIR + GROUPS
CARRY_X = RING + GROUPS
CARRY_Z = CARRY_X + 1
INCOMING = CARRY_Z + 1
SPREAD = INCOMING + 1
ACROSS = SPREAD + GROUPS
RECEIVES = ACROSS + GROUPS

MODAL_IN = TILES
DECAY_IN = TILES + 1
TABLE_IN = DECAY_IN + GROUPS
INPUTS = TABLE_IN + 4


def kernel(
    modal_hbm, modes_hbm, decay_hbm, layup_hbm, lin_hbm, quad_hbm, base_hbm,
    ks, result,
    layup, lin, quad, base,
    modal, modes, decay, stress, graded, index, slab_max, block_max, block_sum, sens, loads,
    pair_in, partial, near_in, tail_prod, head_prod, offsets,
    shares, carry_x, carry_z, incoming,
    in_sem, send_sem, recv_sem,
):
    tm = lax.axis_index("tm")
    elem = lax.axis_index("elem")
    z, x = tm // NX, tm % NX
    y, core = elem // 2, elem % 2
    x_peers = [(z * NX + (x + d) % NX, elem) for d in range(1, NX)]
    z_peers = [(((z + d) % NZ) * NX + x, elem) for d in range(1, NZ)]
    offsets_zx = sorted(
        ((dz, dx) for dz in range(NZ) for dx in range(NX) if dz or dx),
        key=lambda o: -min(o[0], NZ - o[0]) - min(o[1], NX - o[1]),
    )
    elem_peers = [(tm, (elem + d) % (2 * NY)) for d in range(1, 2 * NY)]
    y_up, y_down, y_far = (y + 1) % NY, (y + 3) % NY, (y + 2) % NY
    pair = (tm, 2 * y + 1 - core)
    ring = [(tm, 2 * q + core) for q in (y_far, y_up, y_down)]
    ring_y = (y_far, y_down, y_up)

    def describe(src, dst, send_slot, slot, peer):
        return pltpu.make_async_remote_copy(
            src_ref=src, dst_ref=dst, send_sem=send_sem.at[send_slot], recv_sem=recv_sem.at[slot],
            device_id=peer, device_id_type=MESH,
        )

    def send(src, dst, send_slot, slot, peer):
        describe(src, dst, send_slot, slot, peer).start()

    def arrived(extent, slot):
        describe(extent, extent, 0, slot, pair).wait_recv()

    def gone(extent, send_slot):
        describe(extent, extent, send_slot, 0, pair).wait_send()

    table_copies = [
        pltpu.make_async_copy(src, dst, in_sem.at[TABLE_IN + i])
        for i, (src, dst) in enumerate(
            ((layup_hbm, layup), (lin_hbm, lin), (quad_hbm, quad), (base_hbm, base))
        )
    ]

    def tile_copy(j):
        cols = pl.ds(j * TILE, TILE)
        return pltpu.make_async_copy(modes_hbm.at[:, :, cols], modes.at[:, :, cols], in_sem.at[j])

    modal_copy = pltpu.make_async_copy(modal_hbm, modal, in_sem.at[MODAL_IN])
    modal_copy.start()
    tile_copy(0).start()
    for copy in table_copies:
        copy.start()
    for j in range(1, TILES):
        tile_copy(j).start()
    decay_copies = []
    for g in range(GROUPS):
        copy = pltpu.make_async_copy(
            decay_hbm.at[:, pl.ds(g * LANES, LANES)], decay.at[g], in_sem.at[DECAY_IN + g]
        )
        copy.start()
        decay_copies.append(copy)
    barrier = pltpu.get_barrier_semaphore()
    peers = elem_peers + [
        (((z + dz) % NZ) * NX + (x + dx) % NX, elem) for dz, dx in offsets_zx
    ]
    for peer in peers:
        pl.semaphore_signal(barrier, inc=1, device_id=peer, device_id_type=MESH)

    def stress_part(target, j, part):
        cols = pl.ds(pl.multiple_of(j * TILE, TILE), TILE)
        for k in range(3):
            target[k] = jnp.dot(
                modal[pl.ds(part * PART, PART), :], modes[k, :, cols], preferred_element_type=F32
            )

    def grade_part(source, j, part):
        for h in range(TILE // LANES):
            block = j * (TILE // LANES) + h
            layer = layup[block]
            lin_one = HALF_SCALE * lin[0, layer]
            lin_two = HALF_SCALE * lin[1, layer]
            quad_one = SCALE * quad[0, layer]
            quad_two = SCALE * quad[1, layer]
            quad_shear = SCALE * quad[2, layer]
            cross = -0.5 * jnp.sqrt(jnp.full((8, LANES), quad_one * quad_two, F32))[None]
            here = pl.ds(h * LANES, LANES)
            there = pl.ds(pl.multiple_of(block * LANES, LANES), LANES)
            for r in range(part * SLABS // PARTS, (part + 1) * SLABS // PARTS):
                rows = pl.ds(r * SLAB, SLAB)
                inner = pl.ds(r * SLAB - part * PART, SLAB)
                one, two, shear = (
                    source[k, inner, here].reshape(SLAB // 8, 8, LANES) for k in range(3)
                )
                slope_one = lin_one + (quad_one * one + cross * two)
                slope_two = lin_two + (quad_two * two + cross * one)
                slope_shear = quad_shear * shear
                value = (
                    one * (lin_one + slope_one) + two * (lin_two + slope_two) + shear * slope_shear
                )
                graded[0, rows, there] = slope_one.reshape(SLAB, LANES)
                graded[1, rows, there] = slope_two.reshape(SLAB, LANES)
                graded[2, rows, there] = slope_shear.reshape(SLAB, LANES)
                index[rows, there] = value.reshape(SLAB, LANES)
                slab_max[block, r] = jnp.max(value, axis=0)

    def sum_tile(j):
        for h in range(TILE // LANES):
            block = j * (TILE // LANES) + h
            there = pl.ds(pl.multiple_of(block * LANES, LANES), LANES)
            top = jnp.max(slab_max[block], axis=0)
            parts = []
            for r in range(SLABS):
                value = index[pl.ds(r * SLAB, SLAB), there].reshape(SLAB // 8, 8, LANES)
                parts.append(jnp.sum(jnp.exp2(value - top[None]), axis=0))
            while len(parts) > 1:
                parts = [a + b for a, b in zip(parts[::2], parts[1::2])]
            block_max[block] = top
            block_sum[block] = parts[0]

    def log_two(values):
        return jnp.log(values) * math.log2(math.e)

    def log_sum(values):
        top = jnp.max(values, axis=0)
        return top + log_two(jnp.sum(jnp.exp2(values - top[None]), axis=0))

    def share(c):
        blocks = pl.ds(c * CHUNK_BLOCKS, CHUNK_BLOCKS)
        tops = block_max[blocks]
        top = jnp.max(tops, axis=1)
        total = jnp.sum(block_sum[blocks] * jnp.exp2(tops - top[:, None, :]), axis=1)
        shares[c, tm] = top + log_two(total)
        for dz, dx in offsets_zx:
            peer = (((z + dz) % NZ) * NX + (x + dx) % NX, elem)
            send(shares.at[c, tm], shares.at[c, tm], LSE + c, LSE + c, peer)

    def finish_lse(c):
        arrived(shares.at[c, pl.ds(0, NX * NZ - 1)], LSE + c)
        lse = log_sum(shares[c])
        for b in range(CHUNK_BLOCKS):
            block = c * CHUNK_BLOCKS + b
            ks[pl.ds(block, 1), :] = lse[b : b + 1] * (1.0 / SCALE) + base[layup[block]]
        return lse + SHIFT

    def weigh(c, lse, half):
        for i in range(SLABS // 2):
            r = half * (SLABS // 2) + i
            rows = pl.ds(pl.multiple_of(r * SLAB, SLAB), SLAB)
            for b in range(CHUNK_BLOCKS):
                there = pl.ds((c * CHUNK_BLOCKS + b) * LANES, LANES)
                here = pl.ds(b * LANES, LANES)
                weight = jnp.exp2(index[rows, there] - lse[b : b + 1])
                for k in range(3):
                    sens[k, rows, here] = (weight * graded[k, rows, there]).astype(BF16)

    def load_rows(c, half, piece):
        rows = pl.ds(pl.multiple_of(half * (STEPS // 2), STEPS // 2), STEPS // 2)
        total = None
        for k in range(3):
            part = lax.dot_general(
                sens[k, rows, :],
                modes[k, pl.ds(piece * WIDTH, WIDTH), pl.ds(c * CHUNK_COLS, CHUNK_COLS)],
                NT, preferred_element_type=F32,
            )
            total = part if total is None else total + part
        for h in range(PER_DOT):
            g = piece * PER_DOT + h
            part = total[:, h * LANES : (h + 1) * LANES]
            loads[g, rows, :] = part if c == 0 else loads[g, rows, :] + part

    modal_copy.wait()
    for copy in table_copies:
        copy.wait()

    def stress_pair(p, carry):
        first = 2 * p
        tile_copy(first).wait()
        tile_copy(first + 1).wait()
        for n in range(2):
            for part in range(PARTS):
                target = stress.at[n * PARTS + part]
                stress_part(target, first + n, part)
                grade_part(target, first + n, part)
        sum_tile(first)

        @pl.when(p == 0)
        def _():
            pl.semaphore_wait(barrier, len(peers))

        sum_tile(first + 1)

        @pl.when(p % 2 == 1)
        def _():
            share(p // 2)

        return carry

    lax.fori_loop(0, TILES // 2, stress_pair, 0)

    for copy in decay_copies:
        copy.wait()
    tiles = ROWS // 8
    level = lax.broadcasted_iota(jnp.int32, (tiles, 8, LANES), 1)

    def product_step(i, carry):
        g, r = i // ROW_BLOCKS, i % ROW_BLOCKS
        rows = pl.ds(pl.multiple_of(r * ROWS, ROWS), ROWS)
        tail = decay[g, rows, :].reshape(tiles, 8, LANES)
        head = tail
        for step in (1, 2, 4):
            tail = tail * jnp.where(level < 8 - step, pltpu.roll(tail, 8 - step, 1), 1.0)
            head = head * jnp.where(level >= step, pltpu.roll(head, step, 1), 1.0)
        before = jnp.where(level >= 1, pltpu.roll(head, 1, 1), 1.0)
        after = jnp.ones((1, LANES), F32)
        ahead = jnp.ones((1, LANES), F32)
        for n in range(tiles):
            m = tiles - 1 - n
            tail_prod[g, pl.ds(pl.multiple_of(r * ROWS + m * 8, 8), 8), :] = tail[m] * after
            after = after * tail[m, 0:1]
            head_prod[g, pl.ds(pl.multiple_of(r * ROWS + n * 8, 8), 8), :] = before[n] * ahead
            ahead = ahead * head[n, 7:8]
        return carry

    lax.fori_loop(0, GROUPS * ROW_BLOCKS, product_step, 0, unroll=4)

    for c in range(CHUNKS - 1):
        lse = finish_lse(c)
        for half in range(2):
            weigh(c, lse, half)
            for piece in range(MODES // WIDTH):
                load_rows(c, half, piece)
    last = CHUNKS - 1
    lse = finish_lse(last)

    pair_rows = pl.ds(pl.multiple_of((1 - core) * (STEPS // 2), STEPS // 2), STEPS // 2)
    weigh(last, lse, 1 - core)
    for piece in range(MODES // WIDTH):
        load_rows(last, 1 - core, piece)
        for g in range(piece * PER_DOT, (piece + 1) * PER_DOT):
            send(loads.at[g, pair_rows, :], pair_in.at[g], PAIR, PAIR + g, pair)
    weigh(last, lse, core)
    for piece in range(MODES // WIDTH):
        load_rows(last, core, piece)

    def pair_sum(g, q):
        here = pl.ds(pl.multiple_of(q * ROWS, ROWS), ROWS)
        there = pl.ds(pl.multiple_of(core * (STEPS // 2) + q * ROWS, ROWS), ROWS)
        return loads[g, there, :] + pair_in[g, here, :]

    for g in range(GROUPS):
        arrived(pair_in.at[g], PAIR + g)
        for i, q in enumerate((y_far, y_up, y_down)):
            partial[g, i] = pair_sum(g, q)
            send(partial.at[g, i], near_in.at[g, i], RING, RING + g, ring[i])

    for g in range(GROUPS):
        ahead = jnp.ones((1, LANES), F32)
        state = jnp.zeros((1, LANES), F32)
        for r in range(ROW_BLOCKS):
            rows = pl.ds(r * ROWS, ROWS)
            block_sum = jnp.sum(head_prod[g, rows, :] * loads[g, rows, :], axis=0, keepdims=True)
            state = state + ahead * block_sum
            ahead = ahead * tail_prod[g, r * ROWS : r * ROWS + 1, :]
        carry_x[x, 0:1, pl.ds(g * LANES, LANES)] = ahead
        carry_x[x, 1:2, pl.ds(g * LANES, LANES)] = state
    for peer in x_peers:
        send(carry_x.at[x], carry_x.at[x], CARRY_X, CARRY_X, peer)

    arrived(carry_x.at[pl.ds(0, NX - 1)], CARRY_X)
    slab_scale = jnp.ones((1, MODES), F32)
    slab_state = jnp.zeros((1, MODES), F32)
    later_scale, later_state = slab_scale, slab_state
    for q in range(NX - 1, -1, -1):
        scale, offset = carry_x[q, 0:1, :], carry_x[q, 1:2, :]
        slab_state = offset + scale * slab_state
        slab_scale = scale * slab_scale
        later_state = jnp.where(q > x, offset + scale * later_state, later_state)
        later_scale = jnp.where(q > x, scale * later_scale, later_scale)
    carry_z[z, 0:1, :] = slab_scale
    carry_z[z, 1:2, :] = slab_state
    for peer in z_peers:
        send(carry_z.at[z], carry_z.at[z], CARRY_Z, CARRY_Z, peer)

    mine = core * NY + y

    def spread(g, block, send_slot, slot, peer):
        send(offsets.at[g, block], offsets.at[g, block], send_slot, slot, peer)

    mine_rows = pl.ds(pl.multiple_of(mine * ROWS, ROWS), ROWS)
    for g in range(GROUPS):
        arrived(near_in.at[g], RING + g)
        state = (pair_sum(g, y) + near_in[g, 1]) + (near_in[g, 2] + near_in[g, 0])
        state = state.reshape(tiles, 8, LANES)
        factor = decay[g, mine_rows, :].reshape(tiles, 8, LANES)
        for step in (1, 2, 4):
            inside = level < 8 - step
            state = state + factor * jnp.where(inside, pltpu.roll(state, 8 - step, 1), 0.0)
            factor = factor * jnp.where(inside, pltpu.roll(factor, 8 - step, 1), 1.0)
        running = jnp.zeros((1, LANES), F32)
        for m in range(tiles - 1, -1, -1):
            value = state[m] + factor[m] * running
            offsets[g, mine, pl.ds(m * 8, 8), :] = value
            running = value[0:1]
        for i in range(NY - 1):
            spread(g, mine, SPREAD, SPREAD + g, ring[i])
        spread(g, mine, ACROSS, ACROSS + g, pair)

    arrived(carry_z.at[pl.ds(0, NZ - 1)], CARRY_Z)
    far_state = jnp.zeros((1, MODES), F32)
    for q in range(NZ - 1, -1, -1):
        far_state = jnp.where(q > z, carry_z[q, 1:2, :] + carry_z[q, 0:1, :] * far_state, far_state)
    incoming[elem] = later_state + later_scale * far_state
    for peer in elem_peers:
        send(incoming.at[elem], incoming.at[elem], INCOMING, INCOMING, peer)

    for g in range(GROUPS):
        arrived(offsets.at[g, pl.ds(0, NY - 1)], SPREAD + g)
        for q in ring_y:
            spread(g, core * NY + q, ACROSS, ACROSS + g, pair)

    arrived(incoming.at[pl.ds(0, 2 * NY - 1)], INCOMING)
    behind = incoming[0]
    for e in range(1, 2 * NY):
        behind = behind + incoming[e]

    for g in range(GROUPS):
        arrived(offsets.at[g, pl.ds(0, NY)], ACROSS + g)
        there = pl.ds(g * LANES, LANES)
        state = behind[:, g * LANES : (g + 1) * LANES]
        for r in range(ROW_BLOCKS - 1, -1, -1):
            rows = pl.ds(r * ROWS, ROWS)
            result[rows, there] = offsets[g, r] + tail_prod[g, rows, :] * state
            state = offsets[g, r, 0:1, :] + tail_prod[g, r * ROWS : r * ROWS + 1, :] * state

    for c in range(CHUNKS):
        gone(shares.at[c, pl.ds(0, NX * NZ - 1)], LSE + c)
    gone(pair_in, PAIR)
    gone(partial, RING)
    gone(carry_x.at[pl.ds(0, NX - 1)], CARRY_X)
    gone(carry_z.at[pl.ds(0, NZ - 1)], CARRY_Z)
    gone(incoming.at[pl.ds(0, 2 * NY - 1)], INCOMING)
    gone(offsets.at[:, pl.ds(0, NY - 1)], SPREAD)
    gone(offsets.at[:, pl.ds(0, NY)], ACROSS)


def write_out(ks, result, ks_hbm, adjoint_hbm, sem):
    copies = [
        pltpu.make_async_copy(result, adjoint_hbm, sem.at[0]),
        pltpu.make_async_copy(ks, ks_hbm, sem.at[1]),
    ]
    for copy in copies:
        copy.start()
    for copy in copies:
        copy.wait()


def body(modal_coords, stress_modes, step_decay, ply_layup, lin_table, quad_table, base_index):
    hbm = pl.BlockSpec(memory_space=pl.ANY)
    vmem = pl.BlockSpec(memory_space=pltpu.VMEM)
    ks, adjoint = pl.pallas_call(
        kernel,
        out_shape=(
            pltpu.VMEM((BLOCKS, LANES), F32),
            pltpu.VMEM((STEPS, MODES), F32),
        ),
        in_specs=[hbm] * 7,
        out_specs=(vmem, vmem),
        scratch_shapes=[
            pltpu.SMEM((BLOCKS,), jnp.int32),
            pltpu.SMEM((2, LAYUPS), F32),
            pltpu.SMEM((3, LAYUPS), F32),
            pltpu.SMEM((LAYUPS,), F32),
            pltpu.VMEM((STEPS, MODES), BF16),
            pltpu.VMEM((3, MODES, COLS), BF16),
            pltpu.VMEM((GROUPS, STEPS, LANES), F32),
            pltpu.VMEM((2 * PARTS, 3, PART, TILE), F32),
            pltpu.VMEM((3, STEPS, COLS), F32),
            pltpu.VMEM((STEPS, COLS), F32),
            pltpu.VMEM((BLOCKS, SLABS, 8, LANES), F32),
            pltpu.VMEM((BLOCKS, 8, LANES), F32),
            pltpu.VMEM((BLOCKS, 8, LANES), F32),
            pltpu.VMEM((3, STEPS, CHUNK_COLS), BF16),
            pltpu.VMEM((GROUPS, STEPS, LANES), F32),
            pltpu.VMEM((GROUPS, STEPS // 2, LANES), F32),
            pltpu.VMEM((GROUPS, NY - 1, ROWS, LANES), F32),
            pltpu.VMEM((GROUPS, NY - 1, ROWS, LANES), F32),
            pltpu.VMEM((GROUPS, STEPS, LANES), F32),
            pltpu.VMEM((GROUPS, STEPS, LANES), F32),
            pltpu.VMEM((GROUPS, ROW_BLOCKS, ROWS, LANES), F32),
            pltpu.VMEM((CHUNKS, NX * NZ, CHUNK_BLOCKS, LANES), F32),
            pltpu.VMEM((NX, 2, MODES), F32),
            pltpu.VMEM((NZ, 2, MODES), F32),
            pltpu.VMEM((2 * NY, 1, MODES), F32),
            pltpu.SemaphoreType.DMA((INPUTS,)),
            pltpu.SemaphoreType.DMA((RECEIVES,)),
            pltpu.SemaphoreType.DMA((RECEIVES,)),
        ],
        compiler_params=pltpu.CompilerParams(
            collective_id=0, has_side_effects=True, vmem_limit_bytes=48 * 1024 * 1024
        ),
        name="gust_adjoint",
    )(*(
        pltpu.with_memory_space_constraint(value, pltpu.HBM)
        for value in (
            modal_coords, stress_modes, step_decay, ply_layup,
            lin_table.T, quad_table.T, base_index,
        )
    ))
    ks, adjoint = pl.pallas_call(
        write_out,
        out_shape=(
            jax.ShapeDtypeStruct((BLOCKS, LANES), F32),
            jax.ShapeDtypeStruct((STEPS, MODES), F32),
        ),
        in_specs=[vmem] * 2,
        out_specs=(hbm, hbm),
        scratch_shapes=[pltpu.SemaphoreType.DMA((2,))],
        name="write_out",
    )(
        pltpu.with_memory_space_constraint(ks, pltpu.VMEM),
        pltpu.with_memory_space_constraint(adjoint, pltpu.VMEM),
    )
    return ks.reshape(COLS), adjoint


def solution(mesh):
    return jax.shard_map(
        body,
        mesh=mesh,
        in_specs=(P("tm", None), P(None, None, "elem"), P("tm", None), P("elem"), P(), P(), P()),
        out_specs=(P("elem"), P("tm", None)),
        check_vma=False,
    )
```

```python
import math

import jax
import jax.numpy as jnp
from jax import lax
from jax.experimental import pallas as pl
from jax.experimental.pallas import tpu as pltpu
from jax.sharding import PartitionSpec as P

MESH = pl.DeviceIdType.MESH
F32 = jnp.float32
BF16 = jnp.bfloat16

NX, NZ, NY = 4, 8, 4
STEPS, MODES, COLS = 512, 512, 2048
LANES = 128
GROUPS = MODES // LANES
BLOCKS = COLS // LANES
LAYUPS = 16
TILE = 256
PARTS = 1
PART = STEPS // PARTS
TILES = COLS // TILE
CHUNKS = 4
CHUNK_COLS = COLS // CHUNKS
CHUNK_BLOCKS = BLOCKS // CHUNKS
SLAB = 64
SLABS = STEPS // SLAB
ROWS = 64
ROW_BLOCKS = STEPS // ROWS
WIDTH = 256
PER_DOT = WIDTH // LANES
SHARPNESS = 100.0
SCALE = SHARPNESS * math.log2(math.e)
HALF_SCALE = 0.5 * SCALE
SHIFT = -math.log2(2.0 * math.log(2.0))

NT = (((1,), (1,)), ((), ()))

LSE = 0
PAIR = LSE + CHUNKS
RING = PAIR + GROUPS
CARRY_X = RING + GROUPS
CARRY_Z = CARRY_X + 1
INCOMING = CARRY_Z + 1
SPREAD = INCOMING + 1
ACROSS = SPREAD + GROUPS
RECEIVES = ACROSS + GROUPS

MODAL_IN = TILES
DECAY_IN = TILES + 1
TABLE_IN = DECAY_IN + GROUPS
INPUTS = TABLE_IN + 4


def kernel(
    modal_hbm, modes_hbm, decay_hbm, layup_hbm, lin_hbm, quad_hbm, base_hbm,
    ks, result,
    layup, lin, quad, base,
    modal, modes, decay, stress, graded, index, slab_max, block_max, block_sum, sens, loads,
    pair_in, partial, near_in, tail_prod, head_prod, offsets,
    shares, carry_x, carry_z, incoming,
    in_sem, send_sem, recv_sem,
):
    tm = lax.axis_index("tm")
    elem = lax.axis_index("elem")
    z, x = tm // NX, tm % NX
    y, core = elem // 2, elem % 2
    x_peers = [(z * NX + (x + d) % NX, elem) for d in range(1, NX)]
    z_peers = [(((z + d) % NZ) * NX + x, elem) for d in range(1, NZ)]
    offsets_zx = sorted(
        ((dz, dx) for dz in range(NZ) for dx in range(NX) if dz or dx),
        key=lambda o: -min(o[0], NZ - o[0]) - min(o[1], NX - o[1]),
    )
    elem_peers = [(tm, (elem + d) % (2 * NY)) for d in range(1, 2 * NY)]
    y_up, y_down, y_far = (y + 1) % NY, (y + 3) % NY, (y + 2) % NY
    pair = (tm, 2 * y + 1 - core)
    ring = [(tm, 2 * q + core) for q in (y_far, y_up, y_down)]
    ring_y = (y_far, y_down, y_up)

    def describe(src, dst, send_slot, slot, peer):
        return pltpu.make_async_remote_copy(
            src_ref=src, dst_ref=dst, send_sem=send_sem.at[send_slot], recv_sem=recv_sem.at[slot],
            device_id=peer, device_id_type=MESH,
        )

    def send(src, dst, send_slot, slot, peer):
        describe(src, dst, send_slot, slot, peer).start()

    def arrived(extent, slot):
        describe(extent, extent, 0, slot, pair).wait_recv()

    def gone(extent, send_slot):
        describe(extent, extent, send_slot, 0, pair).wait_send()

    table_copies = [
        pltpu.make_async_copy(src, dst, in_sem.at[TABLE_IN + i])
        for i, (src, dst) in enumerate(
            ((layup_hbm, layup), (lin_hbm, lin), (quad_hbm, quad), (base_hbm, base))
        )
    ]

    def tile_copy(j):
        cols = pl.ds(j * TILE, TILE)
        return pltpu.make_async_copy(modes_hbm.at[:, :, cols], modes.at[:, :, cols], in_sem.at[j])

    modal_copy = pltpu.make_async_copy(modal_hbm, modal, in_sem.at[MODAL_IN])
    modal_copy.start()
    tile_copy(0).start()
    for copy in table_copies:
        copy.start()
    for j in range(1, TILES):
        tile_copy(j).start()
    decay_copies = []
    for g in range(GROUPS):
        copy = pltpu.make_async_copy(
            decay_hbm.at[:, pl.ds(g * LANES, LANES)], decay.at[g], in_sem.at[DECAY_IN + g]
        )
        copy.start()
        decay_copies.append(copy)
    barrier = pltpu.get_barrier_semaphore()
    peers = elem_peers + [
        (((z + dz) % NZ) * NX + (x + dx) % NX, elem) for dz, dx in offsets_zx
    ]
    for peer in peers:
        pl.semaphore_signal(barrier, inc=1, device_id=peer, device_id_type=MESH)

    def stress_part(target, j, part):
        cols = pl.ds(pl.multiple_of(j * TILE, TILE), TILE)
        for k in range(3):
            target[k] = jnp.dot(
                modal[pl.ds(part * PART, PART), :], modes[k, :, cols], preferred_element_type=F32
            )

    def grade_part(source, j, part):
        for h in range(TILE // LANES):
            block = j * (TILE // LANES) + h
            layer = layup[block]
            lin_one = HALF_SCALE * lin[0, layer]
            lin_two = HALF_SCALE * lin[1, layer]
            quad_one = SCALE * quad[0, layer]
            quad_two = SCALE * quad[1, layer]
            quad_shear = SCALE * quad[2, layer]
            cross = -0.5 * jnp.sqrt(jnp.full((8, LANES), quad_one * quad_two, F32))[None]
            here = pl.ds(h * LANES, LANES)
            there = pl.ds(pl.multiple_of(block * LANES, LANES), LANES)
            for r in range(part * SLABS // PARTS, (part + 1) * SLABS // PARTS):
                rows = pl.ds(r * SLAB, SLAB)
                inner = pl.ds(r * SLAB - part * PART, SLAB)
                one, two, shear = (
                    source[k, inner, here].reshape(SLAB // 8, 8, LANES) for k in range(3)
                )
                slope_one = lin_one + (quad_one * one + cross * two)
                slope_two = lin_two + (quad_two * two + cross * one)
                slope_shear = quad_shear * shear
                value = (
                    one * (lin_one + slope_one) + two * (lin_two + slope_two) + shear * slope_shear
                )
                graded[0, rows, there] = slope_one.reshape(SLAB, LANES)
                graded[1, rows, there] = slope_two.reshape(SLAB, LANES)
                graded[2, rows, there] = slope_shear.reshape(SLAB, LANES)
                index[rows, there] = value.reshape(SLAB, LANES)
                slab_max[block, r] = jnp.max(value, axis=0)

    def sum_tile(j):
        for h in range(TILE // LANES):
            block = j * (TILE // LANES) + h
            there = pl.ds(pl.multiple_of(block * LANES, LANES), LANES)
            top = jnp.max(slab_max[block], axis=0)
            parts = []
            for r in range(SLABS):
                value = index[pl.ds(r * SLAB, SLAB), there].reshape(SLAB // 8, 8, LANES)
                parts.append(jnp.sum(jnp.exp2(value - top[None]), axis=0))
            while len(parts) > 1:
                parts = [a + b for a, b in zip(parts[::2], parts[1::2])]
            block_max[block] = top
            block_sum[block] = parts[0]

    def log_two(values):
        return jnp.log(values) * math.log2(math.e)

    def log_sum(values):
        top = jnp.max(values, axis=0)
        return top + log_two(jnp.sum(jnp.exp2(values - top[None]), axis=0))

    def share(c):
        blocks = pl.ds(c * CHUNK_BLOCKS, CHUNK_BLOCKS)
        tops = block_max[blocks]
        top = jnp.max(tops, axis=1)
        total = jnp.sum(block_sum[blocks] * jnp.exp2(tops - top[:, None, :]), axis=1)
        shares[c, tm] = top + log_two(total)
        for dz, dx in offsets_zx:
            peer = (((z + dz) % NZ) * NX + (x + dx) % NX, elem)
            send(shares.at[c, tm], shares.at[c, tm], LSE + c, LSE + c, peer)

    def finish_lse(c):
        arrived(shares.at[c, pl.ds(0, NX * NZ - 1)], LSE + c)
        lse = log_sum(shares[c])
        for b in range(CHUNK_BLOCKS):
            block = c * CHUNK_BLOCKS + b
            ks[pl.ds(block, 1), :] = lse[b : b + 1] * (1.0 / SCALE) + base[layup[block]]
        return lse + SHIFT

    def weigh(c, lse, half):
        for i in range(SLABS // 2):
            r = half * (SLABS // 2) + i
            rows = pl.ds(pl.multiple_of(r * SLAB, SLAB), SLAB)
            for b in range(CHUNK_BLOCKS):
                there = pl.ds((c * CHUNK_BLOCKS + b) * LANES, LANES)
                here = pl.ds(b * LANES, LANES)
                weight = jnp.exp2(index[rows, there] - lse[b : b + 1])
                for k in range(3):
                    sens[k, rows, here] = (weight * graded[k, rows, there]).astype(BF16)

    def load_rows(c, half, piece):
        rows = pl.ds(pl.multiple_of(half * (STEPS // 2), STEPS // 2), STEPS // 2)
        total = None
        for k in range(3):
            part = lax.dot_general(
                sens[k, rows, :],
                modes[k, pl.ds(piece * WIDTH, WIDTH), pl.ds(c * CHUNK_COLS, CHUNK_COLS)],
                NT, preferred_element_type=F32,
            )
            total = part if total is None else total + part
        for h in range(PER_DOT):
            g = piece * PER_DOT + h
            part = total[:, h * LANES : (h + 1) * LANES]
            loads[g, rows, :] = part if c == 0 else loads[g, rows, :] + part

    modal_copy.wait()
    for copy in table_copies:
        copy.wait()

    def stress_pair(p, carry):
        first = 2 * p
        tile_copy(first).wait()
        tile_copy(first + 1).wait()
        for n in range(2):
            for part in range(PARTS):
                target = stress.at[n * PARTS + part]
                stress_part(target, first + n, part)
                grade_part(target, first + n, part)
        sum_tile(first)

        @pl.when(p == 0)
        def _():
            pl.semaphore_wait(barrier, len(peers))

        sum_tile(first + 1)

        share(p)
        return carry

    lax.fori_loop(0, TILES // 2, stress_pair, 0)

    for copy in decay_copies:
        copy.wait()
    tiles = ROWS // 8
    level = lax.broadcasted_iota(jnp.int32, (tiles, 8, LANES), 1)

    def product_step(i, carry):
        g, r = i // ROW_BLOCKS, i % ROW_BLOCKS
        rows = pl.ds(pl.multiple_of(r * ROWS, ROWS), ROWS)
        tail = decay[g, rows, :].reshape(tiles, 8, LANES)
        head = tail
        for step in (1, 2, 4):
            tail = tail * jnp.where(level < 8 - step, pltpu.roll(tail, 8 - step, 1), 1.0)
            head = head * jnp.where(level >= step, pltpu.roll(head, step, 1), 1.0)
        before = jnp.where(level >= 1, pltpu.roll(head, 1, 1), 1.0)
        after = jnp.ones((1, LANES), F32)
        ahead = jnp.ones((1, LANES), F32)
        for n in range(tiles):
            m = tiles - 1 - n
            tail_prod[g, pl.ds(pl.multiple_of(r * ROWS + m * 8, 8), 8), :] = tail[m] * after
            after = after * tail[m, 0:1]
            head_prod[g, pl.ds(pl.multiple_of(r * ROWS + n * 8, 8), 8), :] = before[n] * ahead
            ahead = ahead * head[n, 7:8]
        return carry

    lax.fori_loop(0, GROUPS * ROW_BLOCKS, product_step, 0, unroll=4)

    for c in range(CHUNKS - 1):
        lse = finish_lse(c)
        for half in range(2):
            weigh(c, lse, half)
            for piece in range(MODES // WIDTH):
                load_rows(c, half, piece)
    last = CHUNKS - 1
    lse = finish_lse(last)

    pair_rows = pl.ds(pl.multiple_of((1 - core) * (STEPS // 2), STEPS // 2), STEPS // 2)
    weigh(last, lse, 1 - core)
    for piece in range(MODES // WIDTH):
        load_rows(last, 1 - core, piece)
        for g in range(piece * PER_DOT, (piece + 1) * PER_DOT):
            send(loads.at[g, pair_rows, :], pair_in.at[g], PAIR, PAIR + g, pair)
    weigh(last, lse, core)
    for piece in range(MODES // WIDTH):
        load_rows(last, core, piece)

    def pair_sum(g, q):
        here = pl.ds(pl.multiple_of(q * ROWS, ROWS), ROWS)
        there = pl.ds(pl.multiple_of(core * (STEPS // 2) + q * ROWS, ROWS), ROWS)
        return loads[g, there, :] + pair_in[g, here, :]

    for g in range(GROUPS):
        arrived(pair_in.at[g], PAIR + g)
        for i, q in enumerate((y_far, y_up, y_down)):
            partial[g, i] = pair_sum(g, q)
            send(partial.at[g, i], near_in.at[g, i], RING, RING + g, ring[i])

    for g in range(GROUPS):
        ahead = jnp.ones((1, LANES), F32)
        state = jnp.zeros((1, LANES), F32)
        for r in range(ROW_BLOCKS):
            rows = pl.ds(r * ROWS, ROWS)
            block_sum = jnp.sum(head_prod[g, rows, :] * loads[g, rows, :], axis=0, keepdims=True)
            state = state + ahead * block_sum
            ahead = ahead * tail_prod[g, r * ROWS : r * ROWS + 1, :]
        carry_x[x, 0:1, pl.ds(g * LANES, LANES)] = ahead
        carry_x[x, 1:2, pl.ds(g * LANES, LANES)] = state
    for peer in x_peers:
        send(carry_x.at[x], carry_x.at[x], CARRY_X, CARRY_X, peer)

    arrived(carry_x.at[pl.ds(0, NX - 1)], CARRY_X)
    slab_scale = jnp.ones((1, MODES), F32)
    slab_state = jnp.zeros((1, MODES), F32)
    later_scale, later_state = slab_scale, slab_state
    for q in range(NX - 1, -1, -1):
        scale, offset = carry_x[q, 0:1, :], carry_x[q, 1:2, :]
        slab_state = offset + scale * slab_state
        slab_scale = scale * slab_scale
        later_state = jnp.where(q > x, offset + scale * later_state, later_state)
        later_scale = jnp.where(q > x, scale * later_scale, later_scale)
    carry_z[z, 0:1, :] = slab_scale
    carry_z[z, 1:2, :] = slab_state
    for peer in z_peers:
        send(carry_z.at[z], carry_z.at[z], CARRY_Z, CARRY_Z, peer)

    mine = core * NY + y

    def spread(g, block, send_slot, slot, peer):
        send(offsets.at[g, block], offsets.at[g, block], send_slot, slot, peer)

    mine_rows = pl.ds(pl.multiple_of(mine * ROWS, ROWS), ROWS)
    for g in range(GROUPS):
        arrived(near_in.at[g], RING + g)
        state = (pair_sum(g, y) + near_in[g, 1]) + (near_in[g, 2] + near_in[g, 0])
        state = state.reshape(tiles, 8, LANES)
        factor = decay[g, mine_rows, :].reshape(tiles, 8, LANES)
        for step in (1, 2, 4):
            inside = level < 8 - step
            state = state + factor * jnp.where(inside, pltpu.roll(state, 8 - step, 1), 0.0)
            factor = factor * jnp.where(inside, pltpu.roll(factor, 8 - step, 1), 1.0)
        running = jnp.zeros((1, LANES), F32)
        for m in range(tiles - 1, -1, -1):
            value = state[m] + factor[m] * running
            offsets[g, mine, pl.ds(m * 8, 8), :] = value
            running = value[0:1]
        for i in range(NY - 1):
            spread(g, mine, SPREAD, SPREAD + g, ring[i])
        spread(g, mine, ACROSS, ACROSS + g, pair)

    arrived(carry_z.at[pl.ds(0, NZ - 1)], CARRY_Z)
    far_state = jnp.zeros((1, MODES), F32)
    for q in range(NZ - 1, -1, -1):
        far_state = jnp.where(q > z, carry_z[q, 1:2, :] + carry_z[q, 0:1, :] * far_state, far_state)
    incoming[elem] = later_state + later_scale * far_state
    for peer in elem_peers:
        send(incoming.at[elem], incoming.at[elem], INCOMING, INCOMING, peer)

    for g in range(GROUPS):
        arrived(offsets.at[g, pl.ds(0, NY - 1)], SPREAD + g)
        for q in ring_y:
            spread(g, core * NY + q, ACROSS, ACROSS + g, pair)

    arrived(incoming.at[pl.ds(0, 2 * NY - 1)], INCOMING)
    behind = incoming[0]
    for e in range(1, 2 * NY):
        behind = behind + incoming[e]

    for g in range(GROUPS):
        arrived(offsets.at[g, pl.ds(0, NY)], ACROSS + g)
        there = pl.ds(g * LANES, LANES)
        state = behind[:, g * LANES : (g + 1) * LANES]
        for r in range(ROW_BLOCKS - 1, -1, -1):
            rows = pl.ds(r * ROWS, ROWS)
            result[rows, there] = offsets[g, r] + tail_prod[g, rows, :] * state
            state = offsets[g, r, 0:1, :] + tail_prod[g, r * ROWS : r * ROWS + 1, :] * state

    for c in range(CHUNKS):
        gone(shares.at[c, pl.ds(0, NX * NZ - 1)], LSE + c)
    gone(pair_in, PAIR)
    gone(partial, RING)
    gone(carry_x.at[pl.ds(0, NX - 1)], CARRY_X)
    gone(carry_z.at[pl.ds(0, NZ - 1)], CARRY_Z)
    gone(incoming.at[pl.ds(0, 2 * NY - 1)], INCOMING)
    gone(offsets.at[:, pl.ds(0, NY - 1)], SPREAD)
    gone(offsets.at[:, pl.ds(0, NY)], ACROSS)


def write_out(ks, result, ks_hbm, adjoint_hbm, sem):
    copies = [
        pltpu.make_async_copy(result, adjoint_hbm, sem.at[0]),
        pltpu.make_async_copy(ks, ks_hbm, sem.at[1]),
    ]
    for copy in copies:
        copy.start()
    for copy in copies:
        copy.wait()


def body(modal_coords, stress_modes, step_decay, ply_layup, lin_table, quad_table, base_index):
    hbm = pl.BlockSpec(memory_space=pl.ANY)
    vmem = pl.BlockSpec(memory_space=pltpu.VMEM)
    ks, adjoint = pl.pallas_call(
        kernel,
        out_shape=(
            pltpu.VMEM((BLOCKS, LANES), F32),
            pltpu.VMEM((STEPS, MODES), F32),
        ),
        in_specs=[hbm] * 7,
        out_specs=(vmem, vmem),
        scratch_shapes=[
            pltpu.SMEM((BLOCKS,), jnp.int32),
            pltpu.SMEM((2, LAYUPS), F32),
            pltpu.SMEM((3, LAYUPS), F32),
            pltpu.SMEM((LAYUPS,), F32),
            pltpu.VMEM((STEPS, MODES), BF16),
            pltpu.VMEM((3, MODES, COLS), BF16),
            pltpu.VMEM((GROUPS, STEPS, LANES), F32),
            pltpu.VMEM((2 * PARTS, 3, PART, TILE), F32),
            pltpu.VMEM((3, STEPS, COLS), F32),
            pltpu.VMEM((STEPS, COLS), F32),
            pltpu.VMEM((BLOCKS, SLABS, 8, LANES), F32),
            pltpu.VMEM((BLOCKS, 8, LANES), F32),
            pltpu.VMEM((BLOCKS, 8, LANES), F32),
            pltpu.VMEM((3, STEPS, CHUNK_COLS), BF16),
            pltpu.VMEM((GROUPS, STEPS, LANES), F32),
            pltpu.VMEM((GROUPS, STEPS // 2, LANES), F32),
            pltpu.VMEM((GROUPS, NY - 1, ROWS, LANES), F32),
            pltpu.VMEM((GROUPS, NY - 1, ROWS, LANES), F32),
            pltpu.VMEM((GROUPS, STEPS, LANES), F32),
            pltpu.VMEM((GROUPS, STEPS, LANES), F32),
            pltpu.VMEM((GROUPS, ROW_BLOCKS, ROWS, LANES), F32),
            pltpu.VMEM((CHUNKS, NX * NZ, CHUNK_BLOCKS, LANES), F32),
            pltpu.VMEM((NX, 2, MODES), F32),
            pltpu.VMEM((NZ, 2, MODES), F32),
            pltpu.VMEM((2 * NY, 1, MODES), F32),
            pltpu.SemaphoreType.DMA((INPUTS,)),
            pltpu.SemaphoreType.DMA((RECEIVES,)),
            pltpu.SemaphoreType.DMA((RECEIVES,)),
        ],
        compiler_params=pltpu.CompilerParams(
            collective_id=0, has_side_effects=True, vmem_limit_bytes=48 * 1024 * 1024
        ),
        name="gust_adjoint",
    )(*(
        pltpu.with_memory_space_constraint(value, pltpu.HBM)
        for value in (
            modal_coords, stress_modes, step_decay, ply_layup,
            lin_table.T, quad_table.T, base_index,
        )
    ))
    ks, adjoint = pl.pallas_call(
        write_out,
        out_shape=(
            jax.ShapeDtypeStruct((BLOCKS, LANES), F32),
            jax.ShapeDtypeStruct((STEPS, MODES), F32),
        ),
        in_specs=[vmem] * 2,
        out_specs=(hbm, hbm),
        scratch_shapes=[pltpu.SemaphoreType.DMA((2,))],
        name="write_out",
    )(
        pltpu.with_memory_space_constraint(ks, pltpu.VMEM),
        pltpu.with_memory_space_constraint(adjoint, pltpu.VMEM),
    )
    return ks.reshape(COLS), adjoint


def solution(mesh):
    return jax.shard_map(
        body,
        mesh=mesh,
        in_specs=(P("tm", None), P(None, None, "elem"), P("tm", None), P("elem"), P(), P(), P()),
        out_specs=(P("elem"), P("tm", None)),
        check_vma=False,
    )
```

```python
import math

import jax
import jax.numpy as jnp
from jax import lax
from jax.experimental import pallas as pl
from jax.experimental.pallas import tpu as pltpu
from jax.sharding import PartitionSpec as P

MESH = pl.DeviceIdType.MESH
F32 = jnp.float32
BF16 = jnp.bfloat16

NX, NZ, NY = 4, 8, 4
STEPS, MODES, COLS = 512, 512, 2048
LANES = 128
GROUPS = MODES // LANES
BLOCKS = COLS // LANES
LAYUPS = 16
TILE = 256
PARTS = 1
PART = STEPS // PARTS
TILES = COLS // TILE
CHUNKS = 4
CHUNK_COLS = COLS // CHUNKS
CHUNK_BLOCKS = BLOCKS // CHUNKS
SLAB = 64
SLABS = STEPS // SLAB
ROWS = 64
ROW_BLOCKS = STEPS // ROWS
WIDTH = 256
PER_DOT = WIDTH // LANES
SHARPNESS = 100.0
SCALE = SHARPNESS * math.log2(math.e)
HALF_SCALE = 0.5 * SCALE
SHIFT = -math.log2(2.0 * math.log(2.0))

NT = (((1,), (1,)), ((), ()))

LSE = 0
PAIR = LSE + CHUNKS
RING = PAIR + GROUPS
CARRY_X = RING + GROUPS
CARRY_Z = CARRY_X + 1
INCOMING = CARRY_Z + 1
SPREAD = INCOMING + 1
ACROSS = SPREAD + GROUPS
RECEIVES = ACROSS + GROUPS

MODAL_IN = TILES
DECAY_IN = TILES + 1
TABLE_IN = DECAY_IN + GROUPS
INPUTS = TABLE_IN + 4


def kernel(
    modal_hbm, modes_hbm, decay_hbm, layup_hbm, lin_hbm, quad_hbm, base_hbm,
    ks, result,
    layup, lin, quad, base,
    modal, modes, decay, stress, graded, index, slab_max, block_max, block_sum, sens, loads,
    pair_in, partial, near_in, tail_prod, head_prod, offsets,
    shares, carry_x, carry_z, incoming,
    in_sem, send_sem, recv_sem,
):
    tm = lax.axis_index("tm")
    elem = lax.axis_index("elem")
    z, x = tm // NX, tm % NX
    y, core = elem // 2, elem % 2
    x_peers = [(z * NX + (x + d) % NX, elem) for d in range(1, NX)]
    z_peers = [(((z + d) % NZ) * NX + x, elem) for d in range(1, NZ)]
    offsets_zx = sorted(
        ((dz, dx) for dz in range(NZ) for dx in range(NX) if dz or dx),
        key=lambda o: -min(o[0], NZ - o[0]) - min(o[1], NX - o[1]),
    )
    elem_peers = [(tm, (elem + d) % (2 * NY)) for d in range(1, 2 * NY)]
    y_up, y_down, y_far = (y + 1) % NY, (y + 3) % NY, (y + 2) % NY
    pair = (tm, 2 * y + 1 - core)
    ring = [(tm, 2 * q + core) for q in (y_far, y_up, y_down)]
    ring_y = (y_far, y_down, y_up)

    def describe(src, dst, send_slot, slot, peer):
        return pltpu.make_async_remote_copy(
            src_ref=src, dst_ref=dst, send_sem=send_sem.at[send_slot], recv_sem=recv_sem.at[slot],
            device_id=peer, device_id_type=MESH,
        )

    def send(src, dst, send_slot, slot, peer):
        describe(src, dst, send_slot, slot, peer).start()

    def arrived(extent, slot):
        describe(extent, extent, 0, slot, pair).wait_recv()

    def gone(extent, send_slot):
        describe(extent, extent, send_slot, 0, pair).wait_send()

    table_copies = [
        pltpu.make_async_copy(src, dst, in_sem.at[TABLE_IN + i])
        for i, (src, dst) in enumerate(
            ((layup_hbm, layup), (lin_hbm, lin), (quad_hbm, quad), (base_hbm, base))
        )
    ]

    def tile_copy(j):
        cols = pl.ds(j * TILE, TILE)
        return pltpu.make_async_copy(modes_hbm.at[:, :, cols], modes.at[:, :, cols], in_sem.at[j])

    modal_copy = pltpu.make_async_copy(modal_hbm, modal, in_sem.at[MODAL_IN])
    modal_copy.start()
    tile_copy(0).start()
    for copy in table_copies:
        copy.start()
    for j in range(1, TILES):
        tile_copy(j).start()
    decay_copies = []
    for g in range(GROUPS):
        copy = pltpu.make_async_copy(
            decay_hbm.at[:, pl.ds(g * LANES, LANES)], decay.at[g], in_sem.at[DECAY_IN + g]
        )
        copy.start()
        decay_copies.append(copy)
    barrier = pltpu.get_barrier_semaphore()
    peers = elem_peers + [
        (((z + dz) % NZ) * NX + (x + dx) % NX, elem) for dz, dx in offsets_zx
    ]
    for peer in peers:
        pl.semaphore_signal(barrier, inc=1, device_id=peer, device_id_type=MESH)

    def stress_part(target, j, part):
        cols = pl.ds(pl.multiple_of(j * TILE, TILE), TILE)
        for k in range(3):
            target[k] = jnp.dot(
                modal[pl.ds(part * PART, PART), :], modes[k, :, cols], preferred_element_type=F32
            )

    def grade_part(source, j, part):
        for h in range(TILE // LANES):
            block = j * (TILE // LANES) + h
            layer = layup[block]
            lin_one = HALF_SCALE * lin[0, layer]
            lin_two = HALF_SCALE * lin[1, layer]
            quad_one = SCALE * quad[0, layer]
            quad_two = SCALE * quad[1, layer]
            quad_shear = SCALE * quad[2, layer]
            cross = -0.5 * jnp.sqrt(jnp.full((8, LANES), quad_one * quad_two, F32))[None]
            here = pl.ds(h * LANES, LANES)
            there = pl.ds(pl.multiple_of(block * LANES, LANES), LANES)
            for r in range(part * SLABS // PARTS, (part + 1) * SLABS // PARTS):
                rows = pl.ds(r * SLAB, SLAB)
                inner = pl.ds(r * SLAB - part * PART, SLAB)
                one, two, shear = (
                    source[k, inner, here].reshape(SLAB // 8, 8, LANES) for k in range(3)
                )
                slope_one = lin_one + (quad_one * one + cross * two)
                slope_two = lin_two + (quad_two * two + cross * one)
                slope_shear = quad_shear * shear
                value = (
                    one * (lin_one + slope_one) + two * (lin_two + slope_two) + shear * slope_shear
                )
                graded[0, rows, there] = slope_one.reshape(SLAB, LANES)
                graded[1, rows, there] = slope_two.reshape(SLAB, LANES)
                graded[2, rows, there] = slope_shear.reshape(SLAB, LANES)
                index[rows, there] = value.reshape(SLAB, LANES)
                slab_max[block, r] = jnp.max(value, axis=0)

    def sum_tile(j):
        for h in range(TILE // LANES):
            block = j * (TILE // LANES) + h
            there = pl.ds(pl.multiple_of(block * LANES, LANES), LANES)
            top = jnp.max(slab_max[block], axis=0)
            parts = []
            for r in range(SLABS):
                value = index[pl.ds(r * SLAB, SLAB), there].reshape(SLAB // 8, 8, LANES)
                parts.append(jnp.sum(jnp.exp2(value - top[None]), axis=0))
            while len(parts) > 1:
                parts = [a + b for a, b in zip(parts[::2], parts[1::2])]
            block_max[block] = top
            block_sum[block] = parts[0]

    def log_two(values):
        return jnp.log(values) * math.log2(math.e)

    def log_sum(values):
        top = jnp.max(values, axis=0)
        return top + log_two(jnp.sum(jnp.exp2(values - top[None]), axis=0))

    def share(c):
        blocks = pl.ds(c * CHUNK_BLOCKS, CHUNK_BLOCKS)
        tops = block_max[blocks]
        top = jnp.max(tops, axis=1)
        total = jnp.sum(block_sum[blocks] * jnp.exp2(tops - top[:, None, :]), axis=1)
        shares[c, tm] = top + log_two(total)
        for dz, dx in offsets_zx:
            peer = (((z + dz) % NZ) * NX + (x + dx) % NX, elem)
            send(shares.at[c, tm], shares.at[c, tm], LSE + c, LSE + c, peer)

    def finish_lse(c):
        arrived(shares.at[c, pl.ds(0, NX * NZ - 1)], LSE + c)
        lse = log_sum(shares[c])
        for b in range(CHUNK_BLOCKS):
            block = c * CHUNK_BLOCKS + b
            ks[pl.ds(block, 1), :] = lse[b : b + 1] * (1.0 / SCALE) + base[layup[block]]
        return lse + SHIFT

    def weigh(c, lse, half):
        for i in range(SLABS // 2):
            r = half * (SLABS // 2) + i
            rows = pl.ds(pl.multiple_of(r * SLAB, SLAB), SLAB)
            for b in range(CHUNK_BLOCKS):
                there = pl.ds((c * CHUNK_BLOCKS + b) * LANES, LANES)
                here = pl.ds(b * LANES, LANES)
                weight = jnp.exp2(index[rows, there] - lse[b : b + 1])
                for k in range(3):
                    sens[k, rows, here] = (weight * graded[k, rows, there]).astype(BF16)

    def load_rows(c, half, piece):
        rows = pl.ds(pl.multiple_of(half * (STEPS // 2), STEPS // 2), STEPS // 2)
        total = None
        for k in range(3):
            part = lax.dot_general(
                sens[k, rows, :],
                modes[k, pl.ds(piece * WIDTH, WIDTH), pl.ds(c * CHUNK_COLS, CHUNK_COLS)],
                NT, preferred_element_type=F32,
            )
            total = part if total is None else total + part
        for h in range(PER_DOT):
            g = piece * PER_DOT + h
            part = total[:, h * LANES : (h + 1) * LANES]
            loads[g, rows, :] = part if c == 0 else loads[g, rows, :] + part

    modal_copy.wait()
    for copy in table_copies:
        copy.wait()

    def stress_pair(p, carry):
        first = 2 * p
        tile_copy(first).wait()
        tile_copy(first + 1).wait()
        for n in range(2):
            for part in range(PARTS):
                target = stress.at[n * PARTS + part]
                stress_part(target, first + n, part)
                grade_part(target, first + n, part)
        sum_tile(first)

        @pl.when(p == 0)
        def _():
            pl.semaphore_wait(barrier, len(peers))

        sum_tile(first + 1)

        share(p)
        return carry

    lax.fori_loop(0, TILES // 2, stress_pair, 0)

    for copy in decay_copies:
        copy.wait()
    tiles = ROWS // 8
    level = lax.broadcasted_iota(jnp.int32, (tiles, 8, LANES), 1)

    def product_step(i, carry):
        g, r = i // ROW_BLOCKS, i % ROW_BLOCKS
        rows = pl.ds(pl.multiple_of(r * ROWS, ROWS), ROWS)
        tail = decay[g, rows, :].reshape(tiles, 8, LANES)
        head = tail
        for step in (1, 2, 4):
            tail = tail * jnp.where(level < 8 - step, pltpu.roll(tail, 8 - step, 1), 1.0)
            head = head * jnp.where(level >= step, pltpu.roll(head, step, 1), 1.0)
        before = jnp.where(level >= 1, pltpu.roll(head, 1, 1), 1.0)
        after = jnp.ones((1, LANES), F32)
        ahead = jnp.ones((1, LANES), F32)
        for n in range(tiles):
            m = tiles - 1 - n
            tail_prod[g, pl.ds(pl.multiple_of(r * ROWS + m * 8, 8), 8), :] = tail[m] * after
            after = after * tail[m, 0:1]
            head_prod[g, pl.ds(pl.multiple_of(r * ROWS + n * 8, 8), 8), :] = before[n] * ahead
            ahead = ahead * head[n, 7:8]
        return carry

    lax.fori_loop(0, GROUPS * ROW_BLOCKS, product_step, 0, unroll=4)

    for c in range(CHUNKS - 1):
        lse = finish_lse(c)
        for half in range(2):
            weigh(c, lse, half)
            for piece in range(MODES // WIDTH):
                load_rows(c, half, piece)
    last = CHUNKS - 1
    lse = finish_lse(last)

    pair_rows = pl.ds(pl.multiple_of((1 - core) * (STEPS // 2), STEPS // 2), STEPS // 2)
    weigh(last, lse, 1 - core)
    for piece in range(MODES // WIDTH):
        load_rows(last, 1 - core, piece)
        for g in range(piece * PER_DOT, (piece + 1) * PER_DOT):
            send(loads.at[g, pair_rows, :], pair_in.at[g], PAIR, PAIR + g, pair)
    weigh(last, lse, core)
    for piece in range(MODES // WIDTH):
        load_rows(last, core, piece)

    def pair_sum(g, q):
        here = pl.ds(pl.multiple_of(q * ROWS, ROWS), ROWS)
        there = pl.ds(pl.multiple_of(core * (STEPS // 2) + q * ROWS, ROWS), ROWS)
        return loads[g, there, :] + pair_in[g, here, :]

    for g in range(GROUPS):
        arrived(pair_in.at[g], PAIR + g)
        for i, q in enumerate((y_far, y_up, y_down)):
            partial[g, i] = pair_sum(g, q)
            send(partial.at[g, i], near_in.at[g, i], RING, RING + g, ring[i])

    for g in range(GROUPS):
        ahead = jnp.ones((1, LANES), F32)
        state = jnp.zeros((1, LANES), F32)
        for r in range(ROW_BLOCKS):
            rows = pl.ds(r * ROWS, ROWS)
            block_sum = jnp.sum(head_prod[g, rows, :] * loads[g, rows, :], axis=0, keepdims=True)
            state = state + ahead * block_sum
            ahead = ahead * tail_prod[g, r * ROWS : r * ROWS + 1, :]
        carry_x[x, 0:1, pl.ds(g * LANES, LANES)] = ahead
        carry_x[x, 1:2, pl.ds(g * LANES, LANES)] = state
    for peer in x_peers:
        send(carry_x.at[x], carry_x.at[x], CARRY_X, CARRY_X, peer)

    arrived(carry_x.at[pl.ds(0, NX - 1)], CARRY_X)
    slab_scale = jnp.ones((1, MODES), F32)
    slab_state = jnp.zeros((1, MODES), F32)
    later_scale, later_state = slab_scale, slab_state
    for q in range(NX - 1, -1, -1):
        scale, offset = carry_x[q, 0:1, :], carry_x[q, 1:2, :]
        slab_state = offset + scale * slab_state
        slab_scale = scale * slab_scale
        later_state = jnp.where(q > x, offset + scale * later_state, later_state)
        later_scale = jnp.where(q > x, scale * later_scale, later_scale)
    carry_z[z, 0:1, :] = slab_scale
    carry_z[z, 1:2, :] = slab_state
    for peer in z_peers:
        send(carry_z.at[z], carry_z.at[z], CARRY_Z, CARRY_Z, peer)

    mine = core * NY + y

    def spread(g, block, send_slot, slot, peer):
        send(offsets.at[g, block], offsets.at[g, block], send_slot, slot, peer)

    mine_rows = pl.ds(pl.multiple_of(mine * ROWS, ROWS), ROWS)
    for g in range(GROUPS):
        arrived(near_in.at[g], RING + g)
        state = (pair_sum(g, y) + near_in[g, 1]) + (near_in[g, 2] + near_in[g, 0])
        state = state.reshape(tiles, 8, LANES)
        factor = decay[g, mine_rows, :].reshape(tiles, 8, LANES)
        for step in (1, 2, 4):
            inside = level < 8 - step
            state = state + factor * jnp.where(inside, pltpu.roll(state, 8 - step, 1), 0.0)
            factor = factor * jnp.where(inside, pltpu.roll(factor, 8 - step, 1), 1.0)
        running = jnp.zeros((1, LANES), F32)
        for m in range(tiles - 1, -1, -1):
            value = state[m] + factor[m] * running
            offsets[g, mine, pl.ds(m * 8, 8), :] = value
            running = value[0:1]
        for i in range(NY - 1):
            spread(g, mine, SPREAD, SPREAD + g, ring[i])
        spread(g, mine, ACROSS, ACROSS + g, pair)

    arrived(carry_z.at[pl.ds(0, NZ - 1)], CARRY_Z)
    far_state = jnp.zeros((1, MODES), F32)
    for q in range(NZ - 1, -1, -1):
        far_state = jnp.where(q > z, carry_z[q, 1:2, :] + carry_z[q, 0:1, :] * far_state, far_state)
    incoming[elem] = later_state + later_scale * far_state
    for peer in elem_peers:
        send(incoming.at[elem], incoming.at[elem], INCOMING, INCOMING, peer)

    for g in range(GROUPS):
        arrived(offsets.at[g, pl.ds(0, NY - 1)], SPREAD + g)
        for q in ring_y:
            spread(g, core * NY + q, ACROSS, ACROSS + g, pair)

    arrived(incoming.at[pl.ds(0, 2 * NY - 1)], INCOMING)
    behind = incoming[0]
    for e in range(1, 2 * NY):
        behind = behind + incoming[e]

    for g in range(GROUPS):
        arrived(offsets.at[g, pl.ds(0, NY)], ACROSS + g)
        there = pl.ds(g * LANES, LANES)
        state = behind[:, g * LANES : (g + 1) * LANES]
        for r in range(ROW_BLOCKS - 1, -1, -1):
            rows = pl.ds(r * ROWS, ROWS)
            result[rows, there] = offsets[g, r] + tail_prod[g, rows, :] * state
            state = offsets[g, r, 0:1, :] + tail_prod[g, r * ROWS : r * ROWS + 1, :] * state

    for c in range(CHUNKS):
        gone(shares.at[c, pl.ds(0, NX * NZ - 1)], LSE + c)
    gone(pair_in, PAIR)
    gone(partial, RING)
    gone(carry_x.at[pl.ds(0, NX - 1)], CARRY_X)
    gone(carry_z.at[pl.ds(0, NZ - 1)], CARRY_Z)
    gone(incoming.at[pl.ds(0, 2 * NY - 1)], INCOMING)
    gone(offsets.at[:, pl.ds(0, NY - 1)], SPREAD)
    gone(offsets.at[:, pl.ds(0, NY)], ACROSS)


def write_out(ks, result, ks_hbm, adjoint_hbm, sem):
    copies = [
        pltpu.make_async_copy(
            result.at[pl.ds(r * ROWS, ROWS), :], adjoint_hbm.at[pl.ds(r * ROWS, ROWS), :], sem.at[r]
        )
        for r in range(ROW_BLOCKS)
    ] + [pltpu.make_async_copy(ks, ks_hbm, sem.at[ROW_BLOCKS])]
    for copy in copies:
        copy.start()
    for copy in copies:
        copy.wait()


def body(modal_coords, stress_modes, step_decay, ply_layup, lin_table, quad_table, base_index):
    hbm = pl.BlockSpec(memory_space=pl.ANY)
    vmem = pl.BlockSpec(memory_space=pltpu.VMEM)
    ks, adjoint = pl.pallas_call(
        kernel,
        out_shape=(
            pltpu.VMEM((BLOCKS, LANES), F32),
            pltpu.VMEM((STEPS, MODES), F32),
        ),
        in_specs=[hbm] * 7,
        out_specs=(vmem, vmem),
        scratch_shapes=[
            pltpu.SMEM((BLOCKS,), jnp.int32),
            pltpu.SMEM((2, LAYUPS), F32),
            pltpu.SMEM((3, LAYUPS), F32),
            pltpu.SMEM((LAYUPS,), F32),
            pltpu.VMEM((STEPS, MODES), BF16),
            pltpu.VMEM((3, MODES, COLS), BF16),
            pltpu.VMEM((GROUPS, STEPS, LANES), F32),
            pltpu.VMEM((2 * PARTS, 3, PART, TILE), F32),
            pltpu.VMEM((3, STEPS, COLS), F32),
            pltpu.VMEM((STEPS, COLS), F32),
            pltpu.VMEM((BLOCKS, SLABS, 8, LANES), F32),
            pltpu.VMEM((BLOCKS, 8, LANES), F32),
            pltpu.VMEM((BLOCKS, 8, LANES), F32),
            pltpu.VMEM((3, STEPS, CHUNK_COLS), BF16),
            pltpu.VMEM((GROUPS, STEPS, LANES), F32),
            pltpu.VMEM((GROUPS, STEPS // 2, LANES), F32),
            pltpu.VMEM((GROUPS, NY - 1, ROWS, LANES), F32),
            pltpu.VMEM((GROUPS, NY - 1, ROWS, LANES), F32),
            pltpu.VMEM((GROUPS, STEPS, LANES), F32),
            pltpu.VMEM((GROUPS, STEPS, LANES), F32),
            pltpu.VMEM((GROUPS, ROW_BLOCKS, ROWS, LANES), F32),
            pltpu.VMEM((CHUNKS, NX * NZ, CHUNK_BLOCKS, LANES), F32),
            pltpu.VMEM((NX, 2, MODES), F32),
            pltpu.VMEM((NZ, 2, MODES), F32),
            pltpu.VMEM((2 * NY, 1, MODES), F32),
            pltpu.SemaphoreType.DMA((INPUTS,)),
            pltpu.SemaphoreType.DMA((RECEIVES,)),
            pltpu.SemaphoreType.DMA((RECEIVES,)),
        ],
        compiler_params=pltpu.CompilerParams(
            collective_id=0, has_side_effects=True, vmem_limit_bytes=48 * 1024 * 1024
        ),
        name="gust_adjoint",
    )(*(
        pltpu.with_memory_space_constraint(value, pltpu.HBM)
        for value in (
            modal_coords, stress_modes, step_decay, ply_layup,
            lin_table.T, quad_table.T, base_index,
        )
    ))
    ks, adjoint = pl.pallas_call(
        write_out,
        out_shape=(
            jax.ShapeDtypeStruct((BLOCKS, LANES), F32),
            jax.ShapeDtypeStruct((STEPS, MODES), F32),
        ),
        in_specs=[vmem] * 2,
        out_specs=(hbm, hbm),
        scratch_shapes=[pltpu.SemaphoreType.DMA((ROW_BLOCKS + 1,))],
        name="write_out",
    )(
        pltpu.with_memory_space_constraint(ks, pltpu.VMEM),
        pltpu.with_memory_space_constraint(adjoint, pltpu.VMEM),
    )
    return ks.reshape(COLS), adjoint


def solution(mesh):
    return jax.shard_map(
        body,
        mesh=mesh,
        in_specs=(P("tm", None), P(None, None, "elem"), P("tm", None), P("elem"), P(), P(), P()),
        out_specs=(P("elem"), P("tm", None)),
        check_vma=False,
    )
```

```python
import math

import jax
import jax.numpy as jnp
from jax import lax
from jax.experimental import pallas as pl
from jax.experimental.pallas import tpu as pltpu
from jax.sharding import PartitionSpec as P

MESH = pl.DeviceIdType.MESH
F32 = jnp.float32
BF16 = jnp.bfloat16

NX, NZ, NY = 4, 8, 4
STEPS, MODES, COLS = 512, 512, 2048
LANES = 128
GROUPS = MODES // LANES
BLOCKS = COLS // LANES
LAYUPS = 16
TILE = 256
PARTS = 1
PART = STEPS // PARTS
TILES = COLS // TILE
CHUNKS = 4
CHUNK_COLS = COLS // CHUNKS
CHUNK_BLOCKS = BLOCKS // CHUNKS
SLAB = 64
SLABS = STEPS // SLAB
ROWS = 64
ROW_BLOCKS = STEPS // ROWS
WIDTH = 256
PER_DOT = WIDTH // LANES
SHARPNESS = 100.0
SCALE = SHARPNESS * math.log2(math.e)
HALF_SCALE = 0.5 * SCALE
SHIFT = -math.log2(2.0 * math.log(2.0))

NT = (((1,), (1,)), ((), ()))

LSE = 0
PAIR = LSE + CHUNKS
RING = PAIR + GROUPS
CARRY_X = RING + GROUPS
CARRY_Z = CARRY_X + 1
INCOMING = CARRY_Z + 1
SPREAD = INCOMING + 1
ACROSS = SPREAD + GROUPS
RECEIVES = ACROSS + GROUPS

MODAL_IN = TILES
DECAY_IN = TILES + 1
TABLE_IN = DECAY_IN + GROUPS
INPUTS = TABLE_IN + 4


def kernel(
    modal_hbm, modes_hbm, decay_hbm, layup_hbm, lin_hbm, quad_hbm, base_hbm,
    ks, result,
    layup, lin, quad, base,
    modal, modes, decay, stress, graded, index, slab_max, block_max, block_sum, sens, loads,
    pair_in, partial, near_in, tail_prod, head_prod, offsets,
    shares, carry_x, carry_z, incoming,
    in_sem, send_sem, recv_sem,
):
    tm = lax.axis_index("tm")
    elem = lax.axis_index("elem")
    z, x = tm // NX, tm % NX
    y, core = elem // 2, elem % 2
    x_peers = [(z * NX + (x + d) % NX, elem) for d in range(1, NX)]
    z_peers = [(((z + d) % NZ) * NX + x, elem) for d in range(1, NZ)]
    offsets_zx = sorted(
        ((dz, dx) for dz in range(NZ) for dx in range(NX) if dz or dx),
        key=lambda o: -min(o[0], NZ - o[0]) - min(o[1], NX - o[1]),
    )
    elem_peers = [(tm, (elem + d) % (2 * NY)) for d in range(1, 2 * NY)]
    y_up, y_down, y_far = (y + 1) % NY, (y + 3) % NY, (y + 2) % NY
    pair = (tm, 2 * y + 1 - core)
    ring = [(tm, 2 * q + core) for q in (y_far, y_up, y_down)]
    ring_y = (y_far, y_down, y_up)

    def describe(src, dst, send_slot, slot, peer):
        return pltpu.make_async_remote_copy(
            src_ref=src, dst_ref=dst, send_sem=send_sem.at[send_slot], recv_sem=recv_sem.at[slot],
            device_id=peer, device_id_type=MESH,
        )

    def send(src, dst, send_slot, slot, peer):
        describe(src, dst, send_slot, slot, peer).start()

    def arrived(extent, slot):
        describe(extent, extent, 0, slot, pair).wait_recv()

    def gone(extent, send_slot):
        describe(extent, extent, send_slot, 0, pair).wait_send()

    table_copies = [
        pltpu.make_async_copy(src, dst, in_sem.at[TABLE_IN + i])
        for i, (src, dst) in enumerate(
            ((layup_hbm, layup), (lin_hbm, lin), (quad_hbm, quad), (base_hbm, base))
        )
    ]

    def tile_copy(j):
        cols = pl.ds(j * TILE, TILE)
        return pltpu.make_async_copy(modes_hbm.at[:, :, cols], modes.at[:, :, cols], in_sem.at[j])

    modal_copy = pltpu.make_async_copy(modal_hbm, modal, in_sem.at[MODAL_IN])
    modal_copy.start()
    tile_copy(0).start()
    for copy in table_copies:
        copy.start()
    for j in range(1, TILES):
        tile_copy(j).start()
    decay_copies = []
    for g in range(GROUPS):
        copy = pltpu.make_async_copy(
            decay_hbm.at[:, pl.ds(g * LANES, LANES)], decay.at[g], in_sem.at[DECAY_IN + g]
        )
        copy.start()
        decay_copies.append(copy)
    barrier = pltpu.get_barrier_semaphore()
    peers = elem_peers + [
        (((z + dz) % NZ) * NX + (x + dx) % NX, elem) for dz, dx in offsets_zx
    ]
    for peer in peers:
        pl.semaphore_signal(barrier, inc=1, device_id=peer, device_id_type=MESH)

    def stress_part(target, j, part):
        cols = pl.ds(pl.multiple_of(j * TILE, TILE), TILE)
        for k in range(3):
            target[k] = jnp.dot(
                modal[pl.ds(part * PART, PART), :], modes[k, :, cols], preferred_element_type=F32
            )

    def grade_part(source, j, part):
        for h in range(TILE // LANES):
            block = j * (TILE // LANES) + h
            layer = layup[block]
            lin_one = HALF_SCALE * lin[0, layer]
            lin_two = HALF_SCALE * lin[1, layer]
            quad_one = SCALE * quad[0, layer]
            quad_two = SCALE * quad[1, layer]
            quad_shear = SCALE * quad[2, layer]
            cross = -0.5 * jnp.sqrt(jnp.full((8, LANES), quad_one * quad_two, F32))[None]
            here = pl.ds(h * LANES, LANES)
            there = pl.ds(pl.multiple_of(block * LANES, LANES), LANES)
            for r in range(part * SLABS // PARTS, (part + 1) * SLABS // PARTS):
                rows = pl.ds(r * SLAB, SLAB)
                inner = pl.ds(r * SLAB - part * PART, SLAB)
                one, two, shear = (
                    source[k, inner, here].reshape(SLAB // 8, 8, LANES) for k in range(3)
                )
                slope_one = lin_one + (quad_one * one + cross * two)
                slope_two = lin_two + (quad_two * two + cross * one)
                slope_shear = quad_shear * shear
                value = (
                    one * (lin_one + slope_one) + two * (lin_two + slope_two) + shear * slope_shear
                )
                graded[0, rows, there] = slope_one.reshape(SLAB, LANES)
                graded[1, rows, there] = slope_two.reshape(SLAB, LANES)
                graded[2, rows, there] = slope_shear.reshape(SLAB, LANES)
                index[rows, there] = value.reshape(SLAB, LANES)
                slab_max[block, r] = jnp.max(value, axis=0)

    def sum_tile(j):
        for h in range(TILE // LANES):
            block = j * (TILE // LANES) + h
            there = pl.ds(pl.multiple_of(block * LANES, LANES), LANES)
            top = jnp.max(slab_max[block], axis=0)
            parts = []
            for r in range(SLABS):
                value = index[pl.ds(r * SLAB, SLAB), there].reshape(SLAB // 8, 8, LANES)
                parts.append(jnp.sum(jnp.exp2(value - top[None]), axis=0))
            while len(parts) > 1:
                parts = [a + b for a, b in zip(parts[::2], parts[1::2])]
            block_max[block] = top
            block_sum[block] = parts[0]

    def log_two(values):
        return jnp.log(values) * math.log2(math.e)

    def log_sum(values):
        top = jnp.max(values, axis=0)
        return top + log_two(jnp.sum(jnp.exp2(values - top[None]), axis=0))

    def share(c):
        blocks = pl.ds(c * CHUNK_BLOCKS, CHUNK_BLOCKS)
        tops = block_max[blocks]
        top = jnp.max(tops, axis=1)
        total = jnp.sum(block_sum[blocks] * jnp.exp2(tops - top[:, None, :]), axis=1)
        shares[c, tm] = top + log_two(total)
        for dz, dx in offsets_zx:
            peer = (((z + dz) % NZ) * NX + (x + dx) % NX, elem)
            send(shares.at[c, tm], shares.at[c, tm], LSE + c, LSE + c, peer)

    def finish_lse(c):
        arrived(shares.at[c, pl.ds(0, NX * NZ - 1)], LSE + c)
        lse = log_sum(shares[c])
        for b in range(CHUNK_BLOCKS):
            block = c * CHUNK_BLOCKS + b
            ks[pl.ds(block, 1), :] = lse[b : b + 1] * (1.0 / SCALE) + base[layup[block]]
        return lse + SHIFT

    def weigh(c, lse, half):
        for i in range(SLABS // 2):
            r = half * (SLABS // 2) + i
            rows = pl.ds(pl.multiple_of(r * SLAB, SLAB), SLAB)
            for b in range(CHUNK_BLOCKS):
                there = pl.ds((c * CHUNK_BLOCKS + b) * LANES, LANES)
                weight = jnp.exp2(index[rows, there] - lse[b : b + 1])
                for k in range(3):
                    sens[k, b, rows, :] = (weight * graded[k, rows, there]).astype(BF16)

    def load_rows(c, half, piece):
        rows = pl.ds(pl.multiple_of(half * (STEPS // 2), STEPS // 2), STEPS // 2)
        total = None
        for k in range(3):
            part = lax.dot_general(
                jnp.concatenate([sens[k, b, rows, :] for b in range(CHUNK_BLOCKS)], axis=1),
                modes[k, pl.ds(piece * WIDTH, WIDTH), pl.ds(c * CHUNK_COLS, CHUNK_COLS)],
                NT, preferred_element_type=F32,
            )
            total = part if total is None else total + part
        for h in range(PER_DOT):
            g = piece * PER_DOT + h
            part = total[:, h * LANES : (h + 1) * LANES]
            loads[g, rows, :] = part if c == 0 else loads[g, rows, :] + part

    modal_copy.wait()
    for copy in table_copies:
        copy.wait()

    def stress_pair(p, carry):
        first = 2 * p
        tile_copy(first).wait()
        tile_copy(first + 1).wait()
        for n in range(2):
            for part in range(PARTS):
                target = stress.at[n * PARTS + part]
                stress_part(target, first + n, part)
                grade_part(target, first + n, part)
        sum_tile(first)

        @pl.when(p == 0)
        def _():
            pl.semaphore_wait(barrier, len(peers))

        sum_tile(first + 1)

        share(p)
        return carry

    lax.fori_loop(0, TILES // 2, stress_pair, 0)

    for copy in decay_copies:
        copy.wait()
    tiles = ROWS // 8
    level = lax.broadcasted_iota(jnp.int32, (tiles, 8, LANES), 1)

    def product_step(i, carry):
        g, r = i // ROW_BLOCKS, i % ROW_BLOCKS
        rows = pl.ds(pl.multiple_of(r * ROWS, ROWS), ROWS)
        tail = decay[g, rows, :].reshape(tiles, 8, LANES)
        head = tail
        for step in (1, 2, 4):
            tail = tail * jnp.where(level < 8 - step, pltpu.roll(tail, 8 - step, 1), 1.0)
            head = head * jnp.where(level >= step, pltpu.roll(head, step, 1), 1.0)
        before = jnp.where(level >= 1, pltpu.roll(head, 1, 1), 1.0)
        after = jnp.ones((1, LANES), F32)
        ahead = jnp.ones((1, LANES), F32)
        for n in range(tiles):
            m = tiles - 1 - n
            tail_prod[g, pl.ds(pl.multiple_of(r * ROWS + m * 8, 8), 8), :] = tail[m] * after
            after = after * tail[m, 0:1]
            head_prod[g, pl.ds(pl.multiple_of(r * ROWS + n * 8, 8), 8), :] = before[n] * ahead
            ahead = ahead * head[n, 7:8]
        return carry

    lax.fori_loop(0, GROUPS * ROW_BLOCKS, product_step, 0, unroll=4)

    for c in range(CHUNKS - 1):
        lse = finish_lse(c)
        for half in range(2):
            weigh(c, lse, half)
            for piece in range(MODES // WIDTH):
                load_rows(c, half, piece)
    last = CHUNKS - 1
    lse = finish_lse(last)

    pair_rows = pl.ds(pl.multiple_of((1 - core) * (STEPS // 2), STEPS // 2), STEPS // 2)
    weigh(last, lse, 1 - core)
    for piece in range(MODES // WIDTH):
        load_rows(last, 1 - core, piece)
        for g in range(piece * PER_DOT, (piece + 1) * PER_DOT):
            send(loads.at[g, pair_rows, :], pair_in.at[g], PAIR, PAIR + g, pair)
    weigh(last, lse, core)
    for piece in range(MODES // WIDTH):
        load_rows(last, core, piece)

    def pair_sum(g, q):
        here = pl.ds(pl.multiple_of(q * ROWS, ROWS), ROWS)
        there = pl.ds(pl.multiple_of(core * (STEPS // 2) + q * ROWS, ROWS), ROWS)
        return loads[g, there, :] + pair_in[g, here, :]

    for g in range(GROUPS):
        arrived(pair_in.at[g], PAIR + g)
        for i, q in enumerate((y_far, y_up, y_down)):
            partial[g, i] = pair_sum(g, q)
            send(partial.at[g, i], near_in.at[g, i], RING, RING + g, ring[i])

    for g in range(GROUPS):
        ahead = jnp.ones((1, LANES), F32)
        state = jnp.zeros((1, LANES), F32)
        for r in range(ROW_BLOCKS):
            rows = pl.ds(r * ROWS, ROWS)
            block_sum = jnp.sum(head_prod[g, rows, :] * loads[g, rows, :], axis=0, keepdims=True)
            state = state + ahead * block_sum
            ahead = ahead * tail_prod[g, r * ROWS : r * ROWS + 1, :]
        carry_x[x, 0:1, pl.ds(g * LANES, LANES)] = ahead
        carry_x[x, 1:2, pl.ds(g * LANES, LANES)] = state
    for peer in x_peers:
        send(carry_x.at[x], carry_x.at[x], CARRY_X, CARRY_X, peer)

    arrived(carry_x.at[pl.ds(0, NX - 1)], CARRY_X)
    slab_scale = jnp.ones((1, MODES), F32)
    slab_state = jnp.zeros((1, MODES), F32)
    later_scale, later_state = slab_scale, slab_state
    for q in range(NX - 1, -1, -1):
        scale, offset = carry_x[q, 0:1, :], carry_x[q, 1:2, :]
        slab_state = offset + scale * slab_state
        slab_scale = scale * slab_scale
        later_state = jnp.where(q > x, offset + scale * later_state, later_state)
        later_scale = jnp.where(q > x, scale * later_scale, later_scale)
    carry_z[z, 0:1, :] = slab_scale
    carry_z[z, 1:2, :] = slab_state
    for peer in z_peers:
        send(carry_z.at[z], carry_z.at[z], CARRY_Z, CARRY_Z, peer)

    mine = core * NY + y

    def spread(g, block, send_slot, slot, peer):
        send(offsets.at[g, block], offsets.at[g, block], send_slot, slot, peer)

    mine_rows = pl.ds(pl.multiple_of(mine * ROWS, ROWS), ROWS)
    for g in range(GROUPS):
        arrived(near_in.at[g], RING + g)
        state = (pair_sum(g, y) + near_in[g, 1]) + (near_in[g, 2] + near_in[g, 0])
        state = state.reshape(tiles, 8, LANES)
        factor = decay[g, mine_rows, :].reshape(tiles, 8, LANES)
        for step in (1, 2, 4):
            inside = level < 8 - step
            state = state + factor * jnp.where(inside, pltpu.roll(state, 8 - step, 1), 0.0)
            factor = factor * jnp.where(inside, pltpu.roll(factor, 8 - step, 1), 1.0)
        running = jnp.zeros((1, LANES), F32)
        for m in range(tiles - 1, -1, -1):
            value = state[m] + factor[m] * running
            offsets[g, mine, pl.ds(m * 8, 8), :] = value
            running = value[0:1]
        for i in range(NY - 1):
            spread(g, mine, SPREAD, SPREAD + g, ring[i])
        spread(g, mine, ACROSS, ACROSS + g, pair)

    arrived(carry_z.at[pl.ds(0, NZ - 1)], CARRY_Z)
    far_state = jnp.zeros((1, MODES), F32)
    for q in range(NZ - 1, -1, -1):
        far_state = jnp.where(q > z, carry_z[q, 1:2, :] + carry_z[q, 0:1, :] * far_state, far_state)
    incoming[elem] = later_state + later_scale * far_state
    for peer in elem_peers:
        send(incoming.at[elem], incoming.at[elem], INCOMING, INCOMING, peer)

    for g in range(GROUPS):
        arrived(offsets.at[g, pl.ds(0, NY - 1)], SPREAD + g)
        for q in ring_y:
            spread(g, core * NY + q, ACROSS, ACROSS + g, pair)

    arrived(incoming.at[pl.ds(0, 2 * NY - 1)], INCOMING)
    behind = incoming[0]
    for e in range(1, 2 * NY):
        behind = behind + incoming[e]

    for g in range(GROUPS):
        arrived(offsets.at[g, pl.ds(0, NY)], ACROSS + g)
        there = pl.ds(g * LANES, LANES)
        state = behind[:, g * LANES : (g + 1) * LANES]
        for r in range(ROW_BLOCKS - 1, -1, -1):
            rows = pl.ds(r * ROWS, ROWS)
            result[rows, there] = offsets[g, r] + tail_prod[g, rows, :] * state
            state = offsets[g, r, 0:1, :] + tail_prod[g, r * ROWS : r * ROWS + 1, :] * state

    for c in range(CHUNKS):
        gone(shares.at[c, pl.ds(0, NX * NZ - 1)], LSE + c)
    gone(pair_in, PAIR)
    gone(partial, RING)
    gone(carry_x.at[pl.ds(0, NX - 1)], CARRY_X)
    gone(carry_z.at[pl.ds(0, NZ - 1)], CARRY_Z)
    gone(incoming.at[pl.ds(0, 2 * NY - 1)], INCOMING)
    gone(offsets.at[:, pl.ds(0, NY - 1)], SPREAD)
    gone(offsets.at[:, pl.ds(0, NY)], ACROSS)


def write_out(ks, result, ks_hbm, adjoint_hbm, sem):
    copies = [
        pltpu.make_async_copy(result, adjoint_hbm, sem.at[0]),
        pltpu.make_async_copy(ks, ks_hbm, sem.at[1]),
    ]
    for copy in copies:
        copy.start()
    for copy in copies:
        copy.wait()


def body(modal_coords, stress_modes, step_decay, ply_layup, lin_table, quad_table, base_index):
    hbm = pl.BlockSpec(memory_space=pl.ANY)
    vmem = pl.BlockSpec(memory_space=pltpu.VMEM)
    ks, adjoint = pl.pallas_call(
        kernel,
        out_shape=(
            pltpu.VMEM((BLOCKS, LANES), F32),
            pltpu.VMEM((STEPS, MODES), F32),
        ),
        in_specs=[hbm] * 7,
        out_specs=(vmem, vmem),
        scratch_shapes=[
            pltpu.SMEM((BLOCKS,), jnp.int32),
            pltpu.SMEM((2, LAYUPS), F32),
            pltpu.SMEM((3, LAYUPS), F32),
            pltpu.SMEM((LAYUPS,), F32),
            pltpu.VMEM((STEPS, MODES), BF16),
            pltpu.VMEM((3, MODES, COLS), BF16),
            pltpu.VMEM((GROUPS, STEPS, LANES), F32),
            pltpu.VMEM((2 * PARTS, 3, PART, TILE), F32),
            pltpu.VMEM((3, STEPS, COLS), F32),
            pltpu.VMEM((STEPS, COLS), F32),
            pltpu.VMEM((BLOCKS, SLABS, 8, LANES), F32),
            pltpu.VMEM((BLOCKS, 8, LANES), F32),
            pltpu.VMEM((BLOCKS, 8, LANES), F32),
            pltpu.VMEM((3, CHUNK_BLOCKS, STEPS, LANES), BF16),
            pltpu.VMEM((GROUPS, STEPS, LANES), F32),
            pltpu.VMEM((GROUPS, STEPS // 2, LANES), F32),
            pltpu.VMEM((GROUPS, NY - 1, ROWS, LANES), F32),
            pltpu.VMEM((GROUPS, NY - 1, ROWS, LANES), F32),
            pltpu.VMEM((GROUPS, STEPS, LANES), F32),
            pltpu.VMEM((GROUPS, STEPS, LANES), F32),
            pltpu.VMEM((GROUPS, ROW_BLOCKS, ROWS, LANES), F32),
            pltpu.VMEM((CHUNKS, NX * NZ, CHUNK_BLOCKS, LANES), F32),
            pltpu.VMEM((NX, 2, MODES), F32),
            pltpu.VMEM((NZ, 2, MODES), F32),
            pltpu.VMEM((2 * NY, 1, MODES), F32),
            pltpu.SemaphoreType.DMA((INPUTS,)),
            pltpu.SemaphoreType.DMA((RECEIVES,)),
            pltpu.SemaphoreType.DMA((RECEIVES,)),
        ],
        compiler_params=pltpu.CompilerParams(
            collective_id=0, has_side_effects=True, vmem_limit_bytes=48 * 1024 * 1024
        ),
        name="gust_adjoint",
    )(*(
        pltpu.with_memory_space_constraint(value, pltpu.HBM)
        for value in (
            modal_coords, stress_modes, step_decay, ply_layup,
            lin_table.T, quad_table.T, base_index,
        )
    ))
    ks, adjoint = pl.pallas_call(
        write_out,
        out_shape=(
            jax.ShapeDtypeStruct((BLOCKS, LANES), F32),
            jax.ShapeDtypeStruct((STEPS, MODES), F32),
        ),
        in_specs=[vmem] * 2,
        out_specs=(hbm, hbm),
        scratch_shapes=[pltpu.SemaphoreType.DMA((2,))],
        name="write_out",
    )(
        pltpu.with_memory_space_constraint(ks, pltpu.VMEM),
        pltpu.with_memory_space_constraint(adjoint, pltpu.VMEM),
    )
    return ks.reshape(COLS), adjoint


def solution(mesh):
    return jax.shard_map(
        body,
        mesh=mesh,
        in_specs=(P("tm", None), P(None, None, "elem"), P("tm", None), P("elem"), P(), P(), P()),
        out_specs=(P("elem"), P("tm", None)),
        check_vma=False,
    )
```
